32 devices in a mesh: rep: 8 (over z, y), grp: 4 (over x, core).
Axes of the slice: x: 2, y: 2, z: 4, core: 2. Of those that a mesh axis runs over, the one named last changes fastest.
Arguments:
- tokens: bfloat16 [8, 2048, 768], P('rep', 'grp'), may hold values from -6 to 6
- prev_logits: float32 [8, 2048, 12], P('rep', 'grp'), may hold values from -6 to 6
- routes: int32 [8, 2048, 2], P('rep', 'grp'), may hold values from 0 to 11, all different within a row; in each aligned block of 512 rows (0 to 511, 512 to 1023, ..., all dimensions but the last counted through in order) at most 128 rows name the same one
- branch_points: int32 [8, 2], P('rep'), may hold values from 1 to 1024, as said below
- cotangent: bfloat16 [8, 2048, 768], P('rep', 'grp'), may hold values from -6 to 6
- attn_gain: bfloat16 [768], replicated, may hold values from 0.5 to 1.5
- qkv_weight: bfloat16 [768, 2304], P('grp'), may hold values from -0.21875 to 0.21875
- out_weight: bfloat16 [768, 768], P('grp'), may hold values from -0.875 to 0.875
- ffn_gain: bfloat16 [768], replicated, may hold values from 0.5 to 1.5
- router_weight: bfloat16 [768, 12], replicated, may hold values from -0.109375 to 0.109375
- resid_weight: bfloat16 [12, 12], replicated, may hold values from -0.875 to 0.875
- const_weight: bfloat16 [2, 768, 2], replicated, may hold values from -0.21875 to 0.21875
- const_vector: bfloat16 [2, 768], replicated, may hold values from -6 to 6
- gate_weight: bfloat16 [768, 16384], P(None, 'grp'), may hold values from -0.21875 to 0.21875
- up_weight: bfloat16 [768, 16384], P(None, 'grp'), may hold values from -0.21875 to 0.21875
- down_weight: bfloat16 [16384, 768], P('grp'), may hold values from -0.375 to 0.375
Outputs:
- layer_output: float32 [8, 2048, 768], P('rep', 'grp')
- input_grad: float32 [8, 2048, 768], P('rep', 'grp')
- prev_grad: float32 [8, 2048, 12], P('rep', 'grp')
- gains_grad: float32 [2, 768], replicated
- qkv_grad: float32 [768, 2304], P('grp')
- projection_grad: float32 [768, 768], P('grp')
- router_grad: float32 [768, 12], replicated
- resid_grad: float32 [12, 12], replicated
- const_grad: float32 [2, 768, 2], replicated
- vector_grad: float32 [2, 768], replicated
- gate_grad: float32 [768, 16384], P(None, 'grp')
- up_grad: float32 [768, 16384], P(None, 'grp')
- down_grad: float32 [16384, 768], P('grp')
The draws below stay inside these ranges and needn't reach their ends.
Inputs may be any that keep to these rules, and one draw needn't show every extreme that they name: `routes`: each row names 2 different ids: 0 to 7 are feed-forward experts, 8 the zero expert, 9 the copy expert, 10 and 11 the constant experts. Among the rows of one device no id is named by more than 128 rows. `branch_points`: each group has one continuation that follows the whole prompt.
All inputs are finite; a program needn't handle non-finite values.
Results may differ from the reference program's by a relative error of at most 0.023.
Values may be sent and summed in bfloat16 or wider, within the bound.
No kernel may reach another device: no remote copies, remote signals or barrier semaphores. Data moves between devices by JAX's collectives and lax.ppermute only.
A program may use at most 256 MiB of HBM per device.

```python
import math
import jax
import jax.numpy as jnp
import numpy as np
from jax import lax

D = 768
HEADS = 12
HEAD_DIM = 64
FF = 2048
EXPERTS = 8
TOP = 2
P_DEV = 256
TOK_DEV = 512
CAP = 128
PROMPT = 1024
CONT_LEN = 512
NCONT = 2
GROUPS = 8
GROUP_TOK = 2048
N_GRP = 4


def draw_branch_points(key, part):
    length_key = jax.random.fold_in(key, 11)
    pick_key = jax.random.fold_in(key, 23)
    lengths = jax.random.randint(length_key, (GROUPS, NCONT), 1, PROMPT + 1)
    picked = jax.random.randint(pick_key, (GROUPS, 1), 0, NCONT)
    column = jnp.arange(NCONT)[None, :]
    return jnp.where(column == picked, PROMPT, lengths).astype(jnp.int32)


def block_scale(own_key, extent, cuts, low, top_value):
    level, own = 1.0, jax.random.fold_in(own_key, 6)
    for position, blocks in cuts:
        steps = jnp.exp(jax.random.uniform(jax.random.fold_in(own, position), (blocks,), jnp.float32, low / len(cuts), top_value / len(cuts)))
        level = level * jnp.repeat(steps, extent[position] // blocks).reshape([-1 if axis == position else 1 for axis in range(len(extent))])
    return level


def routed_block(rng, own, number, rows, amount, top, bound, skew):
    sequence = jax.random.permutation(rng, amount)
    packed, common = shares(amount, rows * top, bound, skew, True), shares(amount, rows * top, bound, skew, False)
    places = jnp.arange(amount)

    def named(tallies, turn):
        used = int((tallies > 0).sum())
        fixed = max(1, used // 4)
        moved = fixed + (places - fixed + turn * (used - fixed)) % max(1, amount - fixed)
        return jnp.zeros((amount,), jnp.int32).at[sequence[jnp.where(places < fixed, places, moved)]].set(jnp.asarray(tallies, jnp.int32))

    tallies = jnp.where(number % 4 == 0, named(packed, number // 4), named(common, number - number // 4 - 1))
    mixed = jax.random.permutation(jax.random.fold_in(own, 3), amount)
    giver, receiver = mixed[0:amount // 2 * 2:2], mixed[1:amount // 2 * 2:2]
    margin = jnp.minimum(tallies[giver] - 1, bound - tallies[receiver]) // 2
    margin = jnp.where((giver == sequence[0]) | (receiver == sequence[0]) | (tallies[receiver] == 0), 0, jnp.maximum(margin, 0))
    moved = jax.random.randint(jax.random.fold_in(own, 4), (amount // 2,), 0, 1 << 20) % (margin + 1)
    tallies = tallies.at[giver].add(-moved).at[receiver].add(moved)
    members = jnp.searchsorted(jnp.cumsum(tallies), jnp.arange(rows * top), side="right").astype(jnp.int32)
    grid = members.reshape(top, rows).T
    grid = grid[jax.random.permutation(jax.random.fold_in(own, 1), rows)]
    turn = jax.random.randint(jax.random.fold_in(own, 2), (rows, 1), 0, top)
    return jnp.take_along_axis(grid, (jnp.arange(top)[None, :] + turn) % top, axis=1)


def shares(count, total, most, slope, full):
    loads = [(1 << 20) // math.isqrt(standing ** slope) + 1 for standing in range(1, count + 1)]
    largest = most if full else min(most, max(-(-total // count), total * loads[0] // sum(loads)))
    least = 1 if total - largest >= count - 1 else 0
    counts, surplus = [largest] + [least] * (count - 1), total - largest - least * (count - 1)
    while surplus > 0:
        free = [i for i in range(1, count) if counts[i] < largest] or [i for i in range(1, count) if counts[i] < most]
        pool, left = sum([loads[i] for i in free]), surplus
        for i in free:
            addition = min(most - counts[i], max(1, left * loads[i] // pool), surplus)
            counts[i] = counts[i] + addition
            surplus = surplus - addition
    return np.array(counts)


def noise(rng, dims, scale, reach, shards=(), held_as=jnp.bfloat16):
    entries = jax.random.normal(rng, dims, jnp.float32) * scale
    if len(shards) > 0:
        entries = block_scale(rng, dims, shards, -0.22, 0.18) * entries
    return jnp.clip(entries, min=-reach, max=reach).astype(held_as)


def setup_inputs(seed: int = 0) -> dict:
    streams_of = jax.random.split(jax.random.key(seed), 17)
    tokens = noise(streams_of[0], (GROUPS, GROUP_TOK, D), 1.0, 6.0, ((0, 8), (1, 4)))
    prev_logits = noise(streams_of[1], (GROUPS, GROUP_TOK, EXPERTS + 4), 1.0, 6.0, ((0, 8), (1, 4)), jnp.float32)
    routes_keys = jax.random.split(jax.random.fold_in(streams_of[2], 1), GROUPS * GROUP_TOK // TOK_DEV)
    routes_turns = jax.random.permutation(jax.random.fold_in(streams_of[2], 3), GROUPS * GROUP_TOK // TOK_DEV)
    routes = jax.vmap(lambda own, number: routed_block(jax.random.fold_in(streams_of[2], 2), own, number, TOK_DEV, EXPERTS + 4, TOP, CAP, 1))(routes_keys, routes_turns).reshape((GROUPS, GROUP_TOK, TOP))
    branch_points = draw_branch_points(jax.random.fold_in(streams_of[16], 71), 0)
    cotangent = noise(streams_of[4], (GROUPS, GROUP_TOK, D), 1.0, 6.0, ((0, 8), (1, 4)))
    attn_gain = jnp.clip(1.0 + 0.1 * jax.random.normal(streams_of[5], (D,), jnp.float32), 0.5, 1.5).astype(jnp.bfloat16)
    qkv_weight = noise(streams_of[6], (D, 3 * D), D ** -0.5, 0.21875, ((0, 4),))
    out_weight = noise(streams_of[7], (D, D), (D // 16) ** -0.5, 0.875, ((0, 4),))
    ffn_gain = jnp.clip(1.0 + 0.1 * jax.random.normal(streams_of[8], (D,), jnp.float32), 0.5, 1.5).astype(jnp.bfloat16)
    router_weight = noise(streams_of[9], (D, EXPERTS + 4), (4 * D) ** -0.5, 0.109375)
    resid_weight = noise(streams_of[10], (EXPERTS + 4, EXPERTS + 4), (4 * (EXPERTS + 4)) ** -0.5, 0.875)
    const_weight = noise(streams_of[11], (2, D, 2), D ** -0.5, 0.21875)
    const_vector = noise(streams_of[12], (2, D), 1.0, 6.0)
    gate_weight = noise(streams_of[13], (D, EXPERTS * FF), D ** -0.5, 0.21875, ((1, 4),))
    up_weight = noise(streams_of[14], (D, EXPERTS * FF), D ** -0.5, 0.21875, ((1, 4),))
    down_weight = noise(streams_of[15], (EXPERTS * FF, D), (FF // 9) ** -0.5, 0.375, ((0, 4),))
    return dict(tokens=tokens, prev_logits=prev_logits, routes=routes, branch_points=branch_points, cotangent=cotangent, attn_gain=attn_gain, qkv_weight=qkv_weight, out_weight=out_weight, ffn_gain=ffn_gain, router_weight=router_weight, resid_weight=resid_weight, const_weight=const_weight, const_vector=const_vector, gate_weight=gate_weight, up_weight=up_weight, down_weight=down_weight)


@jax.custom_vjp
def low(v):
    return lax.optimization_barrier(v.astype(jnp.bfloat16)).astype(jnp.float32)

@jax.custom_vjp
def low_back(v):
    return v

def low_keep(v):
    return (low(v), None)

def low_pass(kept, grad):
    return (grad,)

def back_keep(v):
    return (v, None)

def back_low(kept, grad):
    return (low(grad),)
low.defvjp(low_keep, low_pass)
low_back.defvjp(back_keep, back_low)
NORM_EPS = 1e-06
MASKED = -1e+30
HIGHEST = lax.Precision.HIGHEST

def matmul(left, right):
    return jnp.dot(left, right, precision=HIGHEST, preferred_element_type=jnp.float32)

def rms_norm(values, gain):
    return values * lax.rsqrt(lax.optimization_barrier(jnp.mean(values * values, axis=-1, keepdims=True)) + NORM_EPS) * gain

def softmax_rows(logits):
    shifted = logits - lax.optimization_barrier(jnp.max(logits, axis=-1, keepdims=True))
    weights = jnp.exp(shifted)
    return weights / lax.optimization_barrier(jnp.sum(weights, axis=-1, keepdims=True))

def sigmoid_of(values):
    return 1.0 / (1.0 + jnp.exp(-values))

def attend(queries, key_rows, value_rows, allowed):
    query_heads = queries.reshape(queries.shape[0], HEADS, HEAD_DIM)
    key_heads = key_rows.reshape(key_rows.shape[0], HEADS, HEAD_DIM)
    value_heads = value_rows.reshape(value_rows.shape[0], HEADS, HEAD_DIM)
    scores = jnp.einsum('qhd,khd->hqk', query_heads, key_heads, precision=HIGHEST) * (1.0 / math.sqrt(HEAD_DIM))
    scores = low_back(scores)
    scores = jnp.where(allowed[None], scores, MASKED)
    weights = low(softmax_rows(scores))
    mixed_rows = jnp.einsum('hqk,khd->qhd', weights, value_heads, precision=HIGHEST)
    return mixed_rows.reshape(queries.shape[0], D)

def prompt_part(rows):
    return rows.reshape(N_GRP, 2, P_DEV, rows.shape[-1])[:, 0].reshape(PROMPT, rows.shape[-1])

def cont_part(rows):
    width = rows.shape[-1]
    held = rows.reshape(N_GRP, 2, P_DEV, width)[:, 1]
    held = held.reshape(NCONT, 2, 2, P_DEV // 2, width)
    return jnp.transpose(held, (0, 2, 1, 3, 4)).reshape(NCONT, CONT_LEN, width)

def join_parts(prompt_rows, cont_rows):
    width = prompt_rows.shape[-1]
    held = cont_rows.reshape(NCONT, 2, 2, P_DEV // 2, width)
    held = jnp.transpose(held, (0, 2, 1, 3, 4)).reshape(N_GRP, P_DEV, width)
    joined = jnp.stack([prompt_rows.reshape(N_GRP, P_DEV, width), held], axis=1)
    return joined.reshape(GROUP_TOK, width)

def group_attention(query_all, key_all, value_all, follow):
    prompt_keys = prompt_part(key_all)
    prompt_values = prompt_part(value_all)
    key_places = jnp.arange(PROMPT)
    query_blocks = prompt_part(query_all).reshape(N_GRP // 2, TOK_DEV, D)
    block_starts = jnp.arange(N_GRP // 2) * TOK_DEV

    def prompt_block(pieces):
        block_queries, offset = pieces
        allowed = key_places[None, :] <= (offset + jnp.arange(TOK_DEV))[:, None]
        return attend(block_queries, prompt_keys, prompt_values, allowed)
    prompt_rows = lax.map(jax.checkpoint(prompt_block), (query_blocks, block_starts)).reshape(PROMPT, D)

    def cont_block(pieces):
        block_queries, block_keys, block_values, follow_len = pieces
        keys_joined = jnp.concatenate([prompt_keys, block_keys], axis=0)
        values_joined = jnp.concatenate([prompt_values, block_values], axis=0)
        prompt_allowed = jnp.broadcast_to((key_places < follow_len)[None, :], (CONT_LEN, PROMPT))
        self_places = jnp.arange(CONT_LEN)
        self_allowed = self_places[None, :] <= self_places[:, None]
        allowed = jnp.concatenate([prompt_allowed, self_allowed], axis=1)
        return attend(block_queries, keys_joined, values_joined, allowed)
    cont_rows = lax.map(jax.checkpoint(cont_block), (cont_part(query_all), cont_part(key_all), cont_part(value_all), follow))
    return join_parts(prompt_rows, cont_rows)

def expert_mix(hidden_low, route_rows, gate_w, up_w, down_w):
    device_routes = route_rows.reshape(N_GRP, TOK_DEV * TOP)
    matches = (device_routes[:, :, None] == jnp.arange(EXPERTS, dtype=jnp.int32)[None, None, :]).astype(jnp.int32)
    slots = lax.optimization_barrier(jnp.sum((jnp.cumsum(matches, axis=1) - 1) * matches, axis=2))
    device_ids = jnp.arange(N_GRP, dtype=jnp.int32)[:, None]
    is_expert = device_routes < EXPERTS
    places = jnp.where(is_expert, (device_routes * N_GRP + device_ids) * CAP + slots, EXPERTS * N_GRP * CAP).reshape(-1)
    token_ids = jnp.arange(GROUP_TOK * TOP, dtype=jnp.int32) // TOP
    rows_of = jnp.full((EXPERTS * N_GRP * CAP + 1,), GROUP_TOK, jnp.int32).at[places].set(token_ids)[:-1]
    padded = jnp.concatenate([hidden_low, jnp.zeros((1, D), jnp.float32)], axis=0)
    buffers = padded[rows_of].reshape(EXPERTS, N_GRP * CAP, D)
    gate_blocks = gate_w.reshape(D, EXPERTS, FF)
    up_blocks = up_w.reshape(D, EXPERTS, FF)
    gate_act = low_back(jnp.einsum('erd,def->erf', buffers, gate_blocks, precision=HIGHEST))
    up_act = low_back(jnp.einsum('erd,def->erf', buffers, up_blocks, precision=HIGHEST))
    hidden = low(gate_act * sigmoid_of(gate_act) * up_act)
    expert_out = low_back(jnp.einsum('erf,efd->erd', hidden, down_w.reshape(EXPERTS, FF, D), precision=HIGHEST))
    padded_out = jnp.concatenate([expert_out.reshape(-1, D), jnp.zeros((1, D), jnp.float32)], axis=0)
    return padded_out[places].reshape(GROUP_TOK, TOP, D)

def layer_forward(inputs, previous, route_rows, follow, param_set):
    first_gain, qkv_w, out_w, second_gain, router_w, resid_w, const_w, const_v, gate_w, up_w, down_w = param_set
    normed = rms_norm(inputs, first_gain)
    normed_low = low(normed)
    projected = low_back(low(matmul(normed_low, qkv_w)))
    mixed = group_attention(projected[:, :D], projected[:, D:2 * D], projected[:, 2 * D:], follow)
    mixed_low = low_back(low(mixed))
    residual = inputs + low_back(matmul(mixed_low, out_w))
    hidden_in = rms_norm(residual, second_gain)
    hidden_low = low(hidden_in)
    logits = matmul(hidden_low, router_w) + matmul(previous, resid_w)
    chances = softmax_rows(logits)
    chosen = jnp.take_along_axis(chances, route_rows, axis=1)
    gate_vals = chosen / lax.optimization_barrier(jnp.sum(chosen, axis=1, keepdims=True))
    const_outs = []
    for member in range(2):
        mixing = softmax_rows(matmul(hidden_low, const_w[member]))
        const_outs.append(mixing[:, :1] * hidden_in + mixing[:, 1:] * const_v[member][None, :])
    ffn_out = expert_mix(hidden_low, route_rows, gate_w, up_w, down_w)
    layer_out = residual
    for picked in range(TOP):
        route_id = route_rows[:, picked][:, None]
        branch_out = ffn_out[:, picked] + jnp.where(route_id == EXPERTS + 1, hidden_in, 0.0)
        for member in range(2):
            branch_out = branch_out + jnp.where(route_id == EXPERTS + 2 + member, const_outs[member], 0.0)
        layer_out = layer_out + gate_vals[:, picked:picked + 1] * branch_out
    return layer_out

def reference(tokens, prev_logits, routes, branch_points, cotangent, attn_gain, qkv_weight, out_weight, ffn_gain, router_weight, resid_weight, const_weight, const_vector, gate_weight, up_weight, down_weight):
    params = tuple((array.astype(jnp.float32) for array in (attn_gain, qkv_weight, out_weight, ffn_gain, router_weight, resid_weight, const_weight, const_vector, gate_weight, up_weight, down_weight)))

    def group_step(totals, pieces):
        group_tokens, group_prev, group_routes, group_follow, group_cot = pieces

        def forward(inputs, previous, param_set):
            return layer_forward(inputs, previous, group_routes, group_follow, param_set)
        output, backward = jax.vjp(forward, group_tokens.astype(jnp.float32), group_prev, params)
        input_grad, prev_grad, param_grads = backward(group_cot.astype(jnp.float32))
        totals = jax.tree.map(jnp.add, totals, param_grads)
        return (totals, (output, input_grad, prev_grad))
    initial = jax.tree.map(jnp.zeros_like, params)
    totals, (outputs, input_grads, prev_grads) = lax.scan(group_step, initial, (tokens, prev_logits, routes, branch_points, cotangent))
    first_gain, qkv_sum, out_sum, second_gain, router_sum, resid_sum, const_sum, vector_sum, gate_sum, up_sum, down_sum = totals
    gains = jnp.stack([first_gain, second_gain], axis=0)
    return (outputs, input_grads, prev_grads, gains, qkv_sum, out_sum, router_sum, resid_sum, const_sum, vector_sum, gate_sum, up_sum, down_sum)
```

```python
from functools import partial
import math

import jax
import jax.numpy as jnp
import numpy as np
from jax import lax
from jax.experimental import pallas as pl
from jax.experimental.pallas import tpu as pltpu
from jax.sharding import PartitionSpec as P

D = 768
HEADS = 12
HEAD_DIM = 64
EXPERTS = 8
TOP = 2
P_DEV = 256
TOK_DEV = 512
CAP = 128
IDS = EXPERTS + 4
EXT = 16
BLOCK = TOK_DEV + EXT
LANES = 128
PAIRS = D // LANES

NORM_EPS = 1e-06
MASKED = -1e30
HIGHEST = lax.Precision.HIGHEST
F32 = jnp.float32
BF16 = jnp.bfloat16
VMEM_LIMIT = 56 * 2**20
SMALL_ROWS = 40


def mm(left, right):
    return jnp.dot(left, right, preferred_element_type=F32)


def mm_nt(left, right):
    return lax.dot_general(left, right, (((1,), (1,)), ((), ())), preferred_element_type=F32)


def mm_tn(left, right):
    return lax.dot_general(left, right, (((0,), (0,)), ((), ())), preferred_element_type=F32)


def split(values):
    high = values.astype(BF16)
    return high, (values - high.astype(F32)).astype(BF16)


def shape_of(dims, dtype):
    return jax.ShapeDtypeStruct(dims, dtype)


def estimate(flops, bytes_accessed):
    return pl.CostEstimate(
        flops=int(flops), bytes_accessed=int(bytes_accessed), transcendentals=0
    )


def params():
    return pltpu.CompilerParams(vmem_limit_bytes=VMEM_LIMIT)


def whole_call(kernel, name, scalars, arrays, outs, flops, scratch=()):
    vmem = pl.BlockSpec(memory_space=pltpu.VMEM)
    moved = sum(a.size * a.dtype.itemsize for a in arrays)
    moved += sum(math.prod(o.shape) * np.dtype(o.dtype).itemsize for o in outs)
    return pl.pallas_call(
        kernel,
        out_shape=tuple(outs),
        in_specs=[pl.BlockSpec(memory_space=pltpu.SMEM)] + [vmem] * len(arrays),
        out_specs=tuple([vmem] * len(outs)),
        scratch_shapes=list(scratch),
        compiler_params=params(),
        cost_estimate=estimate(flops, moved),
        name=name,
    )(scalars, *arrays)


def xor_permute(value, offset):
    pairs = [(source, source ^ offset) for source in range(lax.axis_size("grp"))]
    return lax.ppermute(value, "grp", pairs)


def ring_permute(value, step):
    count = lax.axis_size("rep")
    order = list(range(0, count, 2)) + list(range(count - 1, 0, -2))
    pairs = [(order[at], order[(at + step) % count]) for at in range(count)]
    return lax.ppermute(value, "rep", pairs)


def gather_group(value, lowest):
    pieces = {0: value}
    bit = lax.axis_size("grp") // 2
    while bit >= lowest:
        for offset in list(pieces):
            pieces[offset | bit] = xor_permute(pieces[offset], bit)
        bit //= 2
    return pieces


def projection_kernel(group, scal, gain, tok, partner, *rest):
    prompts, shards = rest[: group - 1], rest[group - 1 : 2 * group - 1]
    q_out, kp_out, vp_out, kc_out, vc_out, w_out, n_out = rest[2 * group - 1 :]
    rows = D // group
    for offset in range(group):
        start = pl.multiple_of(scal[offset] * rows, rows)
        w_out[pl.ds(start, rows), :] = shards[offset][...]

    def normed(values):
        wide = values.astype(F32)
        scale = lax.rsqrt(jnp.mean(wide * wide, axis=-1, keepdims=True) + NORM_EPS)
        return (wide * scale * gain[...]).astype(BF16)

    own = normed(tok[...])
    n_out[...] = own
    q_out[...] = mm(own, w_out[:, :D]).astype(BF16)
    kv = mm(own, w_out[:, D:]).astype(BF16)
    start = pl.multiple_of(scal[0] * P_DEV, P_DEV)
    kp_out[pl.ds(start, P_DEV), :] = kv[:P_DEV, :D]
    vp_out[pl.ds(start, P_DEV), :] = kv[:P_DEV, D:]
    kc_out[:P_DEV, :] = kv[P_DEV:, :D]
    vc_out[:P_DEV, :] = kv[P_DEV:, D:]
    kv = mm(normed(partner[...]), w_out[:, D:]).astype(BF16)
    kc_out[P_DEV:, :] = kv[:, :D]
    vc_out[P_DEV:, :] = kv[:, D:]
    for offset in range(1, group):
        kv = mm(normed(prompts[offset - 1][...]), w_out[:, D:]).astype(BF16)
        start = pl.multiple_of(scal[offset] * P_DEV, P_DEV)
        kp_out[pl.ds(start, P_DEV), :] = kv[:, :D]
        vp_out[pl.ds(start, P_DEV), :] = kv[:, D:]


def place_of(local, side):
    half = P_DEV // 2
    return (side + 2 * (local // half)) * half + local % half


def attention_kernel(group, scal, q_ref, kp_ref, vp_ref, kc_ref, vc_ref, o_ref, lse_ref):
    prompt = kp_ref.shape[0]
    index, follow, side = scal[0], scal[group], scal[group + 1]
    lane = lax.broadcasted_iota(jnp.int32, (1, LANES), 1)
    row = lax.broadcasted_iota(jnp.int32, (P_DEV, 1), 0)
    key_at = lax.broadcasted_iota(jnp.int32, (1, prompt), 1)
    cont_at = lax.broadcasted_iota(jnp.int32, (1, 2 * P_DEV), 1)
    cont_place = place_of(cont_at % P_DEV, jnp.where(cont_at < P_DEV, side, 1 - side))
    row_place = place_of(row, side)
    for part in range(2):
        rows = pl.ds(part * P_DEV, P_DEV)
        scaled = q_ref[rows, :] * BF16(1.0 / math.sqrt(HEAD_DIM))
        limit = index * P_DEV + row + 1 if part == 0 else jnp.broadcast_to(follow, (P_DEV, 1))
        mixed, logs = [], []
        for head in range(2):
            masked = jnp.where(lane // HEAD_DIM == head, scaled, BF16(0))
            scores = jnp.where(key_at < limit, mm_nt(masked, kp_ref[...]), MASKED)
            top = jnp.max(scores, axis=1, keepdims=True)
            if part == 1:
                later = jnp.where(cont_place <= row_place, mm_nt(masked, kc_ref[...]), MASKED)
                top = jnp.maximum(top, jnp.max(later, axis=1, keepdims=True))
            weights = jnp.exp(scores - top)
            total = jnp.sum(weights, axis=1, keepdims=True)
            out = mm(weights.astype(BF16), vp_ref[...])
            if part == 1:
                weights = jnp.exp(later - top)
                total = total + jnp.sum(weights, axis=1, keepdims=True)
                out = out + mm(weights.astype(BF16), vc_ref[...])
            mixed.append(out / total)
            logs.append(top + jnp.log(total))
        o_ref[rows, :] = jnp.where(lane < HEAD_DIM, mixed[0], mixed[1])
        lse_ref[rows, :] = jnp.where(lane < HEAD_DIM, logs[0], logs[1])


def attention(scal, q, kp, vp, kc, vc, group):
    prompt = kp.shape[0]
    column = lambda rows: pl.BlockSpec((rows, LANES), lambda p: (0, p))
    flops = 4 * 2 * HEADS * P_DEV * (2 * prompt + 2 * P_DEV) * LANES
    return pl.pallas_call(
        partial(attention_kernel, group),
        out_shape=(shape_of((TOK_DEV, D), F32), shape_of((TOK_DEV, D), F32)),
        grid=(PAIRS,),
        in_specs=[pl.BlockSpec(memory_space=pltpu.SMEM)]
        + [column(n) for n in (TOK_DEV, prompt, prompt, 2 * P_DEV, 2 * P_DEV)],
        out_specs=(column(TOK_DEV), column(TOK_DEV)),
        compiler_params=params(),
        cost_estimate=estimate(flops, 10 * TOK_DEV * D * 2),
        name="attention_forward",
    )(scal, q, kp, vp, kc, vc)


def attention_back_kernel(group, scal, q_ref, kp_ref, vp_ref, kc_ref, vc_ref, do_ref, o_ref, lse_ref, *rest):
    prompt = kp_ref.shape[0]
    dq_ref = rest[0]
    pieces = rest[1 : 1 + group]
    own_ref, other_ref, dkp_acc, dvp_acc, dkc_acc, dvc_acc = rest[1 + group :]
    index, follow, side = scal[0], scal[group], scal[group + 1]
    lane = lax.broadcasted_iota(jnp.int32, (1, LANES), 1)
    sub = lax.broadcasted_iota(jnp.int32, (LANES, 1), 0)
    col = lax.broadcasted_iota(jnp.int32, (1, P_DEV), 1)
    key_at = lax.broadcasted_iota(jnp.int32, (prompt, 1), 0)
    cont_at = lax.broadcasted_iota(jnp.int32, (2 * P_DEV, 1), 0)
    cont_place = place_of(cont_at % P_DEV, jnp.where(cont_at < P_DEV, side, 1 - side))
    col_place = place_of(col, side)
    logs = jnp.transpose(lse_ref[...])
    products = jnp.transpose(do_ref[...].astype(F32) * o_ref[...])
    keys_t = jnp.transpose(kp_ref[...])
    later_t = jnp.transpose(kc_ref[...])
    for part in range(2):
        rows = pl.ds(part * P_DEV, P_DEV)
        span = slice(part * P_DEV, (part + 1) * P_DEV)
        scaled = q_ref[rows, :] * BF16(1.0 / math.sqrt(HEAD_DIM))
        grads = do_ref[rows, :]
        limit = index * P_DEV + col + 1 if part == 0 else jnp.broadcast_to(follow, (1, P_DEV))
        turned = []
        for head in range(2):
            mine = lane // HEAD_DIM == head
            query = jnp.where(mine, scaled, BF16(0))
            grad = jnp.where(mine, grads, BF16(0))
            log_row = logs[head * HEAD_DIM : head * HEAD_DIM + 1, span]
            delta = jnp.sum(
                products[head * HEAD_DIM : (head + 1) * HEAD_DIM, span], axis=0, keepdims=True
            )

            def back(keys, values, allowed):
                probs = jnp.exp(jnp.where(allowed, mm_nt(keys, query) - log_row, MASKED))
                score_grad = (probs * (mm_nt(values, grad) - delta)).astype(BF16)
                return score_grad, mm(score_grad, query), mm(probs.astype(BF16), grad)

            score_grad, dk, dv = back(kp_ref[...], vp_ref[...], key_at < limit)
            dq_t = mm(keys_t, score_grad)
            if part == 0 and head == 0:
                dkp_acc[...] = dk
                dvp_acc[...] = dv
            else:
                dkp_acc[...] += dk
                dvp_acc[...] += dv
            if part == 1:
                score_grad, dk, dv = back(kc_ref[...], vc_ref[...], cont_place <= col_place)
                dq_t = dq_t + mm(later_t, score_grad)
                if head == 0:
                    dkc_acc[...] = dk
                    dvc_acc[...] = dv
                else:
                    dkc_acc[...] += dk
                    dvc_acc[...] += dv
            turned.append(dq_t)
        both = jnp.where(sub < HEAD_DIM, turned[0], turned[1]) * (1.0 / math.sqrt(HEAD_DIM))
        dq_ref[rows, :] = jnp.transpose(both).astype(BF16)
    for offset in range(group):
        start = pl.multiple_of(scal[offset] * P_DEV, P_DEV)
        pieces[offset][0] = dkp_acc[pl.ds(start, P_DEV), :].astype(BF16)
        pieces[offset][1] = dvp_acc[pl.ds(start, P_DEV), :].astype(BF16)
    own_ref[0] = dkc_acc[:P_DEV, :]
    own_ref[1] = dvc_acc[:P_DEV, :]
    other_ref[0] = dkc_acc[P_DEV:, :].astype(BF16)
    other_ref[1] = dvc_acc[P_DEV:, :].astype(BF16)


def attention_back(scal, q, kp, vp, kc, vc, do, o32, lse, group):
    prompt = kp.shape[0]
    column = lambda rows: pl.BlockSpec((rows, LANES), lambda p: (0, p))
    double = pl.BlockSpec((2, P_DEV, LANES), lambda p: (0, 0, p))
    flops = 10 * 2 * HEADS * P_DEV * (2 * prompt + 2 * P_DEV) * LANES
    return pl.pallas_call(
        partial(attention_back_kernel, group),
        out_shape=(
            shape_of((TOK_DEV, D), BF16),
            *[shape_of((2, P_DEV, D), BF16)] * group,
            shape_of((2, P_DEV, D), F32),
            shape_of((2, P_DEV, D), BF16),
        ),
        grid=(PAIRS,),
        in_specs=[pl.BlockSpec(memory_space=pltpu.SMEM)]
        + [
            column(n)
            for n in (TOK_DEV, prompt, prompt, 2 * P_DEV, 2 * P_DEV, TOK_DEV, TOK_DEV, TOK_DEV)
        ],
        out_specs=(column(TOK_DEV), *[double] * group, double, double),
        scratch_shapes=[
            pltpu.VMEM((prompt, LANES), F32),
            pltpu.VMEM((prompt, LANES), F32),
            pltpu.VMEM((2 * P_DEV, LANES), F32),
            pltpu.VMEM((2 * P_DEV, LANES), F32),
        ],
        compiler_params=params(),
        cost_estimate=estimate(flops, 20 * TOK_DEV * D * 2),
        name="attention_backward",
    )(scal, q, kp, vp, kc, vc, do, o32, lse)


def columns(values):
    lane = lax.broadcasted_iota(jnp.int32, (1, LANES), 1)
    packed = None
    for at, value in values.items():
        term = jnp.where(lane == at, value, 0.0)
        packed = term if packed is None else packed + term
    return packed


def routing_kernel(group, scal, tok, o32, *rest):
    shards = rest[:group]
    gain, mixers, vectors, previous, routes = rest[group : group + 5]
    w_out, res_out, base_out, blk_out, info_out, low_out = rest[group + 5 :]
    rows = D // group
    for offset in range(group):
        start = pl.multiple_of(scal[offset] * rows, rows)
        w_out[pl.ds(start, rows), :] = shards[offset][...]
    low = o32[...].astype(BF16)
    low_out[...] = low
    res = tok[...].astype(F32) + mm(low, w_out[...])
    res_out[...] = res
    scale = lax.rsqrt(jnp.mean(res * res, axis=-1, keepdims=True) + NORM_EPS)
    hidden = res * scale * gain[...]
    hidden_low = hidden.astype(BF16)
    blk_out[:TOK_DEV, :] = hidden_low
    lane = lax.broadcasted_iota(jnp.int32, (1, LANES), 1)
    dots = mm(hidden_low, mixers[...])
    logits = jnp.where(lane < IDS, dots + previous[...], MASKED)
    weights = jnp.exp(logits - jnp.max(logits, axis=1, keepdims=True))
    chances = weights / jnp.sum(weights, axis=1, keepdims=True)
    first, second = routes[:, 0:1], routes[:, 1:2]
    chosen0 = jnp.sum(jnp.where(lane == first, chances, 0.0), axis=1, keepdims=True)
    chosen1 = jnp.sum(jnp.where(lane == second, chances, 0.0), axis=1, keepdims=True)
    both = chosen0 + chosen1
    gate0, gate1 = chosen0 / both, chosen1 / both

    def gate_of(ident):
        return jnp.where(first == ident, gate0, 0.0) + jnp.where(second == ident, gate1, 0.0)

    info = {12: gate0, 13: gate1, 21: both}
    hidden_part = gate_of(EXPERTS + 1)
    base = res
    for member in range(2):
        left = dots[:, IDS + 2 * member : IDS + 2 * member + 1]
        right = dots[:, IDS + 2 * member + 1 : IDS + 2 * member + 2]
        top = jnp.maximum(left, right)
        left, right = jnp.exp(left - top), jnp.exp(right - top)
        alpha0, alpha1 = left / (left + right), right / (left + right)
        gate = gate_of(EXPERTS + 2 + member)
        hidden_part = hidden_part + gate * alpha0
        base = base + (gate * alpha1) * vectors[member : member + 1, :]
        info[15 + member] = gate * alpha1
        info[17 + 2 * member] = alpha0
        info[18 + 2 * member] = alpha1
        info[22 + member] = gate
    info[14] = hidden_part
    base_out[...] = base + hidden_part * hidden
    info_out[...] = jnp.where(lane < IDS, chances, columns(info))
    gates = jnp.where(lane == first, gate0, 0.0) + jnp.where(lane == second, gate1, 0.0)
    turned = jnp.transpose(gates)[:EXPERTS, :]
    high = turned.astype(BF16).astype(F32)
    ext = jnp.concatenate([high, turned - high], axis=0).astype(BF16)
    blk_out[TOK_DEV:, :TOK_DEV] = ext
    blk_out[TOK_DEV:, TOK_DEV:] = jnp.zeros((EXT, D - TOK_DEV), BF16)


def rows_kernel(group, per, share, aliased, scal, *rest):
    hidden = rest[:group]
    grads = rest[group : 2 * group]
    outs = rest[2 * group + aliased :]
    x_out, s_out, xt_out, st_out, slots, gates = outs
    slot = lax.broadcasted_iota(jnp.int32, (CAP, 1), 0).astype(F32)
    for at in range(group):
        slots[...] = grads[at][TOK_DEV:, :TOK_DEV].astype(F32)
        pair = hidden[at][TOK_DEV:, :TOK_DEV].astype(F32)
        gates[...] = pair[:EXPERTS, :] + pair[EXPERTS:, :]
        for member in range(per):
            expert = (scal[0] * per + member) // share
            picked = slots[pl.ds(expert, 1), :] == slot
            gate = jnp.sum(
                jnp.where(picked, gates[pl.ds(expert, 1), :], 0.0), axis=1, keepdims=True
            )
            chooser = jnp.where(picked, 1.0, 0.0).astype(BF16)
            span = pl.ds(at * CAP, CAP)
            x_out[0, member, span, :] = mm(chooser, hidden[at][:TOK_DEV, :]).astype(BF16)
            s_out[0, member, span, :] = (mm(chooser, grads[at][:TOK_DEV, :]) * gate).astype(BF16)
    for member in range(per):
        xt_out[0, member] = jnp.transpose(x_out[0, member])
        st_out[0, member] = jnp.transpose(s_out[0, member])


def expert_rows(scal, hidden, grads, at, count, stacks, group, per, share):
    rows = group * CAP
    natural, turned = (count, per, rows, D), (count, per, D, rows)
    block = lambda dims: pl.BlockSpec((1, *dims[1:]), lambda i: (at, 0, 0, 0))
    vmem = pl.BlockSpec((BLOCK, D), lambda i: (0, 0))
    held = [pl.BlockSpec(memory_space=pl.ANY)] * len(stacks)
    first = 1 + 2 * group
    return pl.pallas_call(
        partial(rows_kernel, group, per, share, len(stacks)),
        out_shape=tuple(shape_of(d, BF16) for d in (natural, natural, turned, turned)),
        grid=(1,),
        in_specs=[pl.BlockSpec(memory_space=pltpu.SMEM)] + [vmem] * (2 * group) + held,
        out_specs=tuple(block(d) for d in (natural, natural, turned, turned)),
        scratch_shapes=[pltpu.VMEM((EXT, TOK_DEV), F32), pltpu.VMEM((EXPERTS, TOK_DEV), F32)],
        input_output_aliases={first + n: n for n in range(len(stacks))},
        compiler_params=params(),
        cost_estimate=estimate(
            4 * group * per * CAP * TOK_DEV * D, 2 * (2 * group * BLOCK + 4 * per * rows) * D
        ),
        name="expert_rows",
    )(scal, *hidden, *grads, *stacks)


def sigmoid(values):
    return 0.5 * jnp.tanh(0.5 * values) + 0.5


def expert_terms(x, s, gate_w, up_w, down_w):
    act_a, act_b = mm(x, gate_w), mm(x, up_w)
    sig = sigmoid(act_a)
    silu = act_a * sig
    hidden = (silu * act_b).astype(BF16)
    hidden_grad = mm_nt(s, down_w)
    grad_a = (hidden_grad * act_b * (sig + silu * (1.0 - sig))).astype(BF16)
    grad_b = (hidden_grad * silu).astype(BF16)
    return hidden, grad_a, grad_b


def expert_kernel(group, offsets, x_ref, s_ref, wg, wu, wd, *rest):
    outs, out_acc, in_acc = rest[:group], rest[group], rest[group + 1]
    step = pl.program_id(0)
    rows = x_ref.shape[2]
    chunk = min(rows, 512)
    for start in range(0, rows, chunk):
        span = pl.ds(start, chunk)
        hidden, grad_a, grad_b = expert_terms(
            x_ref[0, 0, span, :], s_ref[0, 0, span, :], wg[...], wu[...], wd[...]
        )
        out = mm(hidden, wd[...])
        back = mm_nt(grad_a, wg[...]) + mm_nt(grad_b, wu[...])

        @pl.when(step == 0)
        def _():
            out_acc[span, :] = out
            in_acc[span, :] = back

        @pl.when(step > 0)
        def _():
            out_acc[span, :] += out
            in_acc[span, :] += back

    @pl.when(step == pl.num_programs(0) - 1)
    def _():
        for at in range(group):
            outs[offsets[at]][0] = out_acc[at * CAP : (at + 1) * CAP, :].astype(BF16)
            outs[offsets[at]][1] = in_acc[at * CAP : (at + 1) * CAP, :].astype(BF16)


def local_expert(x, s, gate_w, up_w, down_w, member, offsets, group, per):
    width = gate_w.shape[1] // per
    tile = min(512, width)
    steps = width // tile
    rows = group * CAP
    side = pl.BlockSpec((1, 1, rows, D), lambda t: (0, member, 0, 0))
    wide = pl.BlockSpec((D, tile), lambda t: (0, member * steps + t))
    tall = pl.BlockSpec((tile, D), lambda t: (member * steps + t, 0))
    piece = pl.BlockSpec((2, CAP, D), lambda t: (0, 0, 0))
    return pl.pallas_call(
        partial(expert_kernel, group, offsets),
        out_shape=tuple([shape_of((2, CAP, D), BF16)] * group),
        grid=(steps,),
        in_specs=[side, side, wide, wide, tall],
        out_specs=tuple([piece] * group),
        scratch_shapes=[pltpu.VMEM((rows, D), F32), pltpu.VMEM((rows, D), F32)],
        compiler_params=params(),
        cost_estimate=estimate(12 * rows * D * width, 6 * D * width + 8 * rows * D),
        name="local_expert",
    )(x, s, gate_w, up_w, down_w)


def slice_kernel(mode, at_ref, x, s, xt, st, wg, wu, wd, *rest):
    outs, (gate_acc, up_acc, down_acc) = rest[:-3], rest[-3:]
    step = pl.program_id(1)
    batches, rows = x.shape[0], x.shape[2]
    terms = [
        expert_terms(x[n, 0], s[n, 0], wg[...], wu[...], wd[...]) for n in range(batches)
    ]
    gate = sum(mm(xt[n, 0], terms[n][1]) for n in range(batches))
    up = sum(mm(xt[n, 0], terms[n][2]) for n in range(batches))
    down = sum(mm(st[n, 0], terms[n][0]) for n in range(batches))

    @pl.when(step == 0)
    def _():
        gate_acc[...] = gate
        up_acc[...] = up
        down_acc[...] = down

    @pl.when(step > 0)
    def _():
        gate_acc[...] += gate
        up_acc[...] += up
        down_acc[...] += down

    @pl.when(step == pl.num_programs(1) - 1)
    def _():
        if mode == "pack":
            outs[0][0] = gate_acc[...].astype(BF16)
            outs[0][1] = up_acc[...].astype(BF16)
            outs[0][2] = down_acc[...].astype(BF16)
        else:
            outs[0][...] = gate_acc[...]
            outs[1][...] = up_acc[...]
            outs[2][...] = jnp.transpose(down_acc[...])


def weight_slices(at, stacks, weights, member, tile, tiles, mode, batches, per):
    x, s, xt, st = stacks
    count, rows = x.shape[0], x.shape[2]
    steps = count // batches
    natural = pl.BlockSpec((batches, 1, rows, D), lambda t, d, ref: (d, member, 0, 0))
    turned = pl.BlockSpec((batches, 1, D, rows), lambda t, d, ref: (d, member, 0, 0))
    wide = pl.BlockSpec((D, tile), lambda t, d, ref: (0, ref[0] + t))
    tall = pl.BlockSpec((tile, D), lambda t, d, ref: (ref[0] + t, 0))
    units = weights[0].shape[1]
    if mode == "pack":
        outs = (shape_of((3, D, tile), BF16),)
        specs = (pl.BlockSpec((3, D, tile), lambda t, d, ref: (0, 0, 0)),)
    else:
        outs = (shape_of((D, units), F32), shape_of((D, units), F32), shape_of((units, D), F32))
        specs = (wide, wide, tall)
    return pl.pallas_call(
        partial(slice_kernel, mode),
        out_shape=outs,
        grid_spec=pltpu.PrefetchScalarGridSpec(
            num_scalar_prefetch=1,
            grid=(tiles, steps),
            in_specs=[natural, natural, turned, turned, wide, wide, tall],
            out_specs=specs,
            scratch_shapes=[pltpu.VMEM((D, tile), F32)] * 3,
        ),
        compiler_params=params(),
        cost_estimate=estimate(
            12 * count * rows * D * tile * tiles, tiles * (8 * count * rows * D + 6 * D * tile)
        ),
        name="weight_slices",
    )(at, *stacks, *weights)


def place_kernel(held, at_ref, piece, *rest):
    gate_out, up_out, down_out = rest[held:]
    gate_out[...] = piece[0].astype(F32)
    up_out[...] = piece[1].astype(F32)
    down_out[...] = jnp.transpose(piece[2].astype(F32))


def place_slice(at, piece, held, units):
    tile = piece.shape[2]
    wide = pl.BlockSpec((D, tile), lambda t, ref: (0, ref[0]))
    tall = pl.BlockSpec((tile, D), lambda t, ref: (ref[0], 0))
    return pl.pallas_call(
        partial(place_kernel, len(held)),
        out_shape=(shape_of((D, units), F32), shape_of((D, units), F32), shape_of((units, D), F32)),
        grid_spec=pltpu.PrefetchScalarGridSpec(
            num_scalar_prefetch=1,
            grid=(1,),
            in_specs=[pl.BlockSpec((3, D, tile), lambda t, ref: (0, 0, 0))]
            + [pl.BlockSpec(memory_space=pl.ANY)] * len(held),
            out_specs=(wide, wide, tall),
        ),
        input_output_aliases={2 + n: n for n in range(len(held))},
        compiler_params=params(),
        cost_estimate=estimate(0, 18 * D * tile),
        name="place_slice",
    )(at, piece, *held)


def combine_kernel(group, per, share, scal, *refs):
    pieces = refs[: group * per]
    (base, cot, blk, info_ref, slots, routes, res_ref, gain, vectors, mixers_t, resid_t, prev, w_out) = refs[
        group * per : group * per + 13
    ]
    layer_out, grad_out, mix_out, mixed_out, prev_out, small_out = refs[group * per + 13 :]
    info = info_ref[...]
    first, second = routes[:, 0:1], routes[:, 1:2]
    lane = lax.broadcasted_iota(jnp.int32, (1, LANES), 1)
    slot_lane = lane.astype(F32)
    taken = slots[...]
    out0 = out1 = back = None
    for offset in range(group):
        for member in range(per):
            expert = (scal[offset] * per + member) // share
            column = jnp.sum(jnp.where(lane == expert, taken, 0.0), axis=1, keepdims=True)
            chooser = column == slot_lane
            piece = pieces[offset * per + member]
            pick0 = jnp.where(chooser & (first == expert), 1.0, 0.0).astype(BF16)
            pick1 = jnp.where(chooser & (second == expert), 1.0, 0.0).astype(BF16)
            add0, add1 = mm(pick0, piece[0]), mm(pick1, piece[0])
            add2 = mm(pick0 + pick1, piece[1])
            out0 = add0 if out0 is None else out0 + add0
            out1 = add1 if out1 is None else out1 + add1
            back = add2 if back is None else back + add2
    get = lambda at: info[:, at : at + 1]
    gate0, gate1, hidden_part, both = get(12), get(13), get(14), get(21)
    layer_out[...] = base[...] + gate0 * out0 + gate1 * out1
    grad = cot[...].astype(F32)
    res = res_ref[...]
    scale = lax.rsqrt(jnp.mean(res * res, axis=-1, keepdims=True) + NORM_EPS)
    unit = res * scale
    total = lambda values: jnp.sum(values, axis=1, keepdims=True)
    dot_hidden = total(grad * (unit * gain[...]))
    dot_vector = [total(grad * vectors[k : k + 1, :]) for k in range(2)]

    def gate_grad(route, out):
        value = total(grad * out) + jnp.where(route == EXPERTS + 1, dot_hidden, 0.0)
        for k in range(2):
            const = get(17 + 2 * k) * dot_hidden + get(18 + 2 * k) * dot_vector[k]
            value = value + jnp.where(route == EXPERTS + 2 + k, const, 0.0)
        return value

    dgate0, dgate1 = gate_grad(first, out0), gate_grad(second, out1)
    mean = gate0 * dgate0 + gate1 * dgate1
    dchance = (
        jnp.where(lane == first, dgate0 - mean, 0.0) + jnp.where(lane == second, dgate1 - mean, 0.0)
    ) / both
    chances = jnp.where(lane < IDS, info, 0.0)
    logits_grad = chances * (dchance - total(chances * dchance))
    extra = {16: get(15), 17: get(16)}
    for k in range(2):
        alpha0, alpha1, gate = get(17 + 2 * k), get(18 + 2 * k), get(22 + k)
        d0, d1 = gate * dot_hidden, gate * dot_vector[k]
        inner = alpha0 * d0 + alpha1 * d1
        extra[IDS + 2 * k] = alpha0 * (d0 - inner)
        extra[IDS + 2 * k + 1] = alpha1 * (d1 - inner)
    packed = logits_grad + columns(extra)
    high, low = split(packed)
    prev_out[...] = mm(high, resid_t[...]) + mm(low, resid_t[...])
    hidden_total = (
        back + hidden_part * grad + mm(high, mixers_t[...]) + mm(low, mixers_t[...])
    )
    turned = jnp.transpose(packed)[:32, :]
    t_high, t_low = split(turned)
    hidden_low = blk[:TOK_DEV, :]
    by_hidden = mm(t_high, hidden_low) + mm(t_low, hidden_low)
    by_grad = mm(t_high, cot[...]) + mm(t_low, cot[...])
    prev_high, prev_low = split(prev[...])
    by_prev = mm(t_high, prev_high) + mm(t_high, prev_low) + mm(t_low, prev_high)
    gain_grad = jnp.sum(hidden_total * unit, axis=0, keepdims=True)
    sub = lax.broadcasted_iota(jnp.int32, (8, 1), 0)
    small_out[:16, :] = by_hidden[:16, :]
    small_out[16:24, :] = jnp.where(sub == 2, gain_grad, by_grad[16:24, :])
    small_out[24:40, :] = jnp.zeros((16, D), F32)
    small_out[24:40, :LANES] = by_prev[:16, :]
    u = gain[...] * hidden_total
    inner = jnp.mean(res * u, axis=1, keepdims=True)
    residual_grad = grad + scale * u - res * (scale * scale * scale * inner)
    grad_out[...] = residual_grad
    mix = residual_grad.astype(BF16)
    mix_out[...] = mix
    mixed_out[...] = mm_nt(mix, w_out[...]).astype(BF16)


def finish_kernel(prompt_terms, scal, dq, own, received, *rest):
    terms = rest[:prompt_terms]
    weights, tok, gain, res_grad = rest[prompt_terms : prompt_terms + 4]
    low_out, grad_out, small_out = rest[prompt_terms + 4 :]
    low_out[:, :D] = dq[...]
    for half in range(2):
        columns_at = slice((half + 1) * D, (half + 2) * D)
        prompt = terms[0][half].astype(F32)
        for term in terms[1:]:
            prompt = prompt + term[half].astype(F32)
        low_out[:P_DEV, columns_at] = prompt.astype(BF16)
        low_out[P_DEV:, columns_at] = (own[half] + received[half].astype(F32)).astype(BF16)
    normed_grad = mm_nt(low_out[...], weights[...])
    x = tok[...].astype(F32)
    scale = lax.rsqrt(jnp.mean(x * x, axis=-1, keepdims=True) + NORM_EPS)
    u = gain[...] * normed_grad
    inner = jnp.mean(x * u, axis=1, keepdims=True)
    grad_out[...] = res_grad[...] + scale * u - x * (scale * scale * scale * inner)
    row = jnp.sum(normed_grad * (x * scale), axis=0, keepdims=True)
    sub = lax.broadcasted_iota(jnp.int32, (8, 1), 0)
    small_out[...] = jnp.where(sub == 0, row, 0.0)


def sum_everywhere(value):
    for axis in ("rep", "grp"):
        count = lax.axis_size(axis)
        bit = 1
        while bit < count:
            pairs = [(source, source ^ bit) for source in range(count)]
            value = value + lax.ppermute(value, axis, pairs)
            bit *= 2
    return value


def sum_replicas(value):
    count = lax.axis_size("rep")
    index = lax.axis_index("rep")
    bits = [1 << n for n in range(count.bit_length() - 1)]
    for bit in bits:
        half = value.shape[1] // 2
        left, right = value[:, :half], value[:, half:]
        upper = (index & bit) != 0
        keep = jnp.where(upper, right, left)
        give = jnp.where(upper, left, right).astype(BF16)
        pairs = [(source, source ^ bit) for source in range(count)]
        value = keep + lax.ppermute(give, "rep", pairs).astype(F32)
    value = value.astype(BF16)
    for bit in reversed(bits):
        pairs = [(source, source ^ bit) for source in range(count)]
        other = lax.ppermute(value, "rep", pairs)
        upper = (index & bit) != 0
        value = jnp.concatenate(
            [jnp.where(upper, other, value), jnp.where(upper, value, other)], axis=1
        )
    return value.astype(F32)


def body(
    tokens,
    prev_logits,
    routes,
    branch_points,
    cotangent,
    attn_gain,
    qkv_weight,
    out_weight,
    ffn_gain,
    router_weight,
    resid_weight,
    const_weight,
    const_vector,
    gate_weight,
    up_weight,
    down_weight,
):
    group, count = lax.axis_size("grp"), lax.axis_size("rep")
    index, replica = lax.axis_index("grp"), lax.axis_index("rep")
    per, share = max(1, EXPERTS // group), max(1, group // EXPERTS)
    prompt = P_DEV * group
    spread = group * count <= 32
    tok, cot, route_rows, prev = tokens[0], cotangent[0], routes[0], prev_logits[0]
    follow = lax.dynamic_index_in_dim(branch_points[0], index // 2, keepdims=True)
    scal = jnp.concatenate(
        [
            index ^ jnp.arange(group, dtype=jnp.int32),
            follow.astype(jnp.int32),
            (index % 2)[None].astype(jnp.int32),
        ]
    )

    shards = gather_group(qkv_weight, 1)
    prompts = gather_group(tok[:P_DEV], 1)
    partner = xor_permute(tok[P_DEV:], 1)
    out_shards = gather_group(out_weight, 1)

    ids = jnp.arange(LANES, dtype=jnp.int32)[None, :]
    named = (route_rows[:, :1] == ids) | (route_rows[:, 1:] == ids)
    at = jnp.arange(TOK_DEV)
    before = (at[None, :] < at[:, None]).astype(BF16)
    slots = jnp.where(named, mm(before, named.astype(BF16)), -1.0)
    ext = jnp.pad(
        jnp.transpose(slots[:, :EXT]).astype(BF16), ((0, 0), (0, D - TOK_DEV)), constant_values=-1
    )
    grad_block = jnp.concatenate([cot, ext], axis=0)
    route_lanes = jnp.pad(route_rows, ((0, 0), (0, LANES - TOP)))
    prev_lanes = jnp.pad(prev, ((0, 0), (0, LANES - IDS)))
    previous = jnp.pad(
        jnp.dot(prev, resid_weight.astype(F32), precision=HIGHEST, preferred_element_type=F32),
        ((0, 0), (0, LANES - IDS)),
    )
    mixers = jnp.pad(
        jnp.concatenate([router_weight, const_weight[0], const_weight[1]], axis=1),
        ((0, 0), (0, LANES - IDS - 4)),
    )
    mixers_t = jnp.transpose(mixers)
    resid_t = jnp.pad(jnp.transpose(resid_weight), ((0, LANES - IDS), (0, LANES - IDS)))
    vectors = jnp.pad(const_vector.astype(F32), ((0, 6), (0, 0)))
    gain_one = attn_gain.astype(F32)[None]
    gain_two = ffn_gain.astype(F32)[None]

    offsets = [o for o in range(0, group, 2)] + [o for o in range(1, group, 2)]

    def group_blocks(block):
        held = gather_group(block, 2)
        own = [held[o] for o in range(0, group, 2)]
        return own, own + [xor_permute(piece, 1) for piece in own]

    def all_blocks(own):
        half = max(1, len(own) // 2)
        forth, back = own[:half], own[half:]
        result = []
        for _ in range(count - 1):
            forth = [ring_permute(piece, 1) for piece in forth]
            back = [ring_permute(piece, -1) for piece in back]
            now = forth + back
            result.append(now + [xor_permute(piece, 1) for piece in now])
        return result

    grad_own, grad_group = group_blocks(grad_block)
    if spread:
        grad_far = all_blocks(grad_own)

    q, kp, vp, kc, vc, w_qkv, normed = whole_call(
        partial(projection_kernel, group),
        "projections",
        scal,
        [gain_one, tok, partner]
        + [prompts[o] for o in range(1, group)]
        + [shards[o] for o in range(group)],
        [
            shape_of((TOK_DEV, D), BF16),
            shape_of((prompt, D), BF16),
            shape_of((prompt, D), BF16),
            shape_of((2 * P_DEV, D), BF16),
            shape_of((2 * P_DEV, D), BF16),
            shape_of((D, 3 * D), BF16),
            shape_of((TOK_DEV, D), BF16),
        ],
        2 * TOK_DEV * D * D + 4 * (prompt + 2 * P_DEV) * D * D,
    )
    o32, lse = attention(scal, q, kp, vp, kc, vc, group)
    w_out, res, base, block, info, mixed_low = whole_call(
        partial(routing_kernel, group),
        "routing",
        scal,
        [tok, o32]
        + [out_shards[o] for o in range(group)]
        + [gain_two, mixers, vectors, previous, route_lanes],
        [
            shape_of((D, D), BF16),
            shape_of((TOK_DEV, D), F32),
            shape_of((TOK_DEV, D), F32),
            shape_of((BLOCK, D), BF16),
            shape_of((TOK_DEV, LANES), F32),
            shape_of((TOK_DEV, D), BF16),
        ],
        2 * TOK_DEV * D * D,
    )

    own, near = group_blocks(block)
    local = expert_rows(scal, near, grad_group, 0, 1, (), group, per, share)
    if spread:
        far = all_blocks(own)

    weights = (gate_weight, up_weight, down_weight)
    returned = {}
    for member in range(per):
        outs = local_expert(local[0], local[1], *weights, member, offsets, group, per)
        for offset in range(group):
            returned[offset, member] = xor_permute(outs[offset], offset) if offset else outs[0]

    layer_out, res_grad, mix_grad, mixed_grad, prev_grad, small = whole_call(
        partial(combine_kernel, group, per, share),
        "combine",
        scal,
        [returned[o, m] for o in range(group) for m in range(per)]
        + [
            base,
            cot,
            block,
            info,
            slots,
            route_lanes,
            res,
            gain_two,
            vectors,
            mixers_t,
            resid_t,
            prev_lanes,
            w_out,
        ],
        [
            shape_of((TOK_DEV, D), F32),
            shape_of((TOK_DEV, D), F32),
            shape_of((TOK_DEV, D), BF16),
            shape_of((TOK_DEV, D), BF16),
            shape_of((TOK_DEV, LANES), F32),
            shape_of((SMALL_ROWS, D), F32),
        ],
        6 * TOK_DEV * group * per * CAP * D + 2 * TOK_DEV * D * D,
    )

    back = attention_back(scal, q, kp, vp, kc, vc, mixed_grad, o32, lse, group)
    dq, pieces, later_own, later_other = back[0], list(back[1 : 1 + group]), back[-2], back[-1]
    later_in = xor_permute(later_other, 1)
    held = {o: [pieces[o]] for o in range(group)}
    bit = 1
    while bit < group:
        for offset in sorted(held):
            if offset & bit:
                terms = held.pop(offset)
                value = terms[0]
                if len(terms) > 1:
                    value = sum(t.astype(F32) for t in terms).astype(BF16)
                held[offset ^ bit].append(xor_permute(value, bit))
        bit *= 2
    terms = held[0]
    qkv_low, input_grad, small_two = whole_call(
        partial(finish_kernel, len(terms)),
        "finish",
        scal,
        [dq, later_own, later_in] + terms + [w_qkv, tok, gain_one, res_grad],
        [
            shape_of((TOK_DEV, 3 * D), BF16),
            shape_of((TOK_DEV, D), F32),
            shape_of((8, D), F32),
        ],
        6 * TOK_DEV * D * D,
    )
    full = jnp.concatenate([mm_tn(normed, qkv_low), mm_tn(mixed_low, mix_grad)], axis=1)
    rows = D // group
    held = {
        o: lax.dynamic_slice_in_dim(full, (index ^ o) * rows, rows, axis=0) for o in range(group)
    }
    bit = 1
    while bit < group:
        for offset in sorted(held):
            if offset & bit:
                value = xor_permute(held.pop(offset).astype(BF16), bit)
                held[offset ^ bit] = held[offset ^ bit] + value.astype(F32)
        bit *= 2
    dense = sum_replicas(held[0])
    small = sum_everywhere(jnp.concatenate([small, small_two], axis=0))

    units = gate_weight.shape[1]
    width = units // per
    if spread:
        stacks = ()
        for step in range(count):
            hidden = near if step == 0 else far[step - 1]
            grads = grad_group if step == 0 else grad_far[step - 1]
            stacks = expert_rows(scal, hidden, grads, step, count, stacks, group, per, share)
        tile = width // count
        first = replica.astype(jnp.int32)[None]
        finished = [
            weight_slices(
                first + member * count, stacks, weights, member, tile, 1, "pack", 2, per
            )[0]
            for member in range(per)
        ]
        spot = jnp.where(replica % 2 == 0, replica // 2, count - 1 - replica // 2)
        held = ()
        for step in range(count):
            for member in range(per):
                toward = 1 if member % 2 == 0 else -1
                if step:
                    finished[member] = ring_permute(finished[member], toward)
                source = (spot - toward * step) % count
                source = jnp.where(
                    source < count // 2, 2 * source, 2 * (count - 1 - source) + 1
                ).astype(jnp.int32)[None]
                held = place_slice(source + member * count, finished[member], held, units)
        gate_sum, up_sum, down_sum = held
    else:
        tile = min(512, width)
        sums = weight_slices(
            jnp.zeros((1,), jnp.int32), local, weights, 0, tile, width // tile, "write", 1, per
        )
        gate_sum, up_sum, down_sum = [
            lax.psum(part.astype(BF16), "rep").astype(F32) for part in sums
        ]

    gains = jnp.stack([small[SMALL_ROWS], small[18]], axis=0)
    router_grad = jnp.transpose(small[:IDS])
    const_grad = jnp.transpose(small[IDS : IDS + 4].reshape(2, 2, D), (0, 2, 1))
    resid_grad = jnp.transpose(small[24 : 24 + IDS, :IDS])
    return (
        layer_out[None],
        input_grad[None],
        prev_grad[:, :IDS][None],
        gains,
        dense[:, : 3 * D],
        dense[:, 3 * D :],
        router_grad,
        resid_grad,
        const_grad,
        small[16:18],
        gate_sum,
        up_sum,
        down_sum,
    )


def solution(mesh):
    in_specs = (
        P("rep", "grp", None),
        P("rep", "grp", None),
        P("rep", "grp", None),
        P("rep", None),
        P("rep", "grp", None),
        P(),
        P("grp", None),
        P("grp", None),
        P(),
        P(),
        P(),
        P(),
        P(),
        P(None, "grp"),
        P(None, "grp"),
        P("grp", None),
    )
    out_specs = (
        P("rep", "grp", None),
        P("rep", "grp", None),
        P("rep", "grp", None),
        P(),
        P("grp", None),
        P("grp", None),
        P(),
        P(),
        P(),
        P(),
        P(None, "grp"),
        P(None, "grp"),
        P("grp", None),
    )
    return jax.shard_map(body, mesh=mesh, in_specs=in_specs, out_specs=out_specs, check_vma=False)
```

```python
from functools import partial
import math

import jax
import jax.numpy as jnp
import numpy as np
from jax import lax
from jax.experimental import pallas as pl
from jax.experimental.pallas import tpu as pltpu
from jax.sharding import PartitionSpec as P

D = 768
HEADS = 12
HEAD_DIM = 64
EXPERTS = 8
TOP = 2
P_DEV = 256
TOK_DEV = 512
CAP = 128
IDS = EXPERTS + 4
EXT = 16
BLOCK = TOK_DEV + EXT
LANES = 128
PAIRS = D // LANES

NORM_EPS = 1e-06
MASKED = -1e30
HIGHEST = lax.Precision.HIGHEST
F32 = jnp.float32
BF16 = jnp.bfloat16
VMEM_LIMIT = 56 * 2**20
SMALL_ROWS = 40
COST = {"column_rows": 4.0}
W_KEYS = 1
SC_DENSE = 1
W_DENSE = 1
SC_SMALL = 0
W_PACK = 0
W_NEAR = 1
W_FRONT = 1
W_RING = 0
W_LOCAL = 1
W_SLICE = 0
W_BACK = 1


def mm(left, right):
    return jnp.dot(left, right, preferred_element_type=F32)


def mm_nt(left, right):
    return lax.dot_general(left, right, (((1,), (1,)), ((), ())), preferred_element_type=F32)


def mm_tn(left, right):
    return lax.dot_general(left, right, (((0,), (0,)), ((), ())), preferred_element_type=F32)


def split(values):
    high = values.astype(BF16)
    return high, (values - high.astype(F32)).astype(BF16)


def shape_of(dims, dtype):
    return jax.ShapeDtypeStruct(dims, dtype)


def estimate(name, flops, bytes_accessed):
    scale = COST.get(name, 1.0)
    return pl.CostEstimate(
        flops=int(scale * flops), bytes_accessed=int(scale * bytes_accessed), transcendentals=0
    )


def params():
    return pltpu.CompilerParams(vmem_limit_bytes=VMEM_LIMIT)


def without(kernel, first, count):
    if not count:
        return kernel

    def run(*refs):
        return kernel(*refs[:first], *refs[first + count :])

    return run


HELD = pl.BlockSpec(memory_space=pl.ANY)


def whole_call(kernel, name, scalars, arrays, outs, flops, scratch=(), waits=()):
    vmem = pl.BlockSpec(memory_space=pltpu.VMEM)
    moved = sum(a.size * a.dtype.itemsize for a in arrays)
    moved += sum(math.prod(o.shape) * np.dtype(o.dtype).itemsize for o in outs)
    return pl.pallas_call(
        without(kernel, 1 + len(arrays), len(waits)),
        out_shape=tuple(outs),
        in_specs=[pl.BlockSpec(memory_space=pltpu.SMEM)]
        + [vmem] * len(arrays)
        + [HELD] * len(waits),
        out_specs=tuple([vmem] * len(outs)),
        scratch_shapes=list(scratch),
        compiler_params=params(),
        cost_estimate=estimate(name, flops, moved),
        name=name,
    )(scalars, *arrays, *waits)


def xor_permute(value, offset):
    pairs = [(source, source ^ offset) for source in range(lax.axis_size("grp"))]
    return lax.ppermute(value, "grp", pairs)


def ring_permute(value, step):
    count = lax.axis_size("rep")
    order = list(range(0, count, 2)) + list(range(count - 1, 0, -2))
    pairs = [(order[at], order[(at + step) % count]) for at in range(count)]
    return lax.ppermute(value, "rep", pairs)


def gather_group(value, lowest):
    pieces = {0: value}
    bit = lax.axis_size("grp") // 2
    while bit >= lowest:
        for offset in list(pieces):
            pieces[offset | bit] = xor_permute(pieces[offset], bit)
        bit //= 2
    return pieces


def lanes_of(values):
    rows, width = values.shape
    return jnp.concatenate([values, jnp.zeros((rows, LANES - width), values.dtype)], axis=1)


def prepare_kernel(routes, prev, cot, router, resid, const_w, const_v, prompt, *rest):
    prompt_out, block, slots_out, routes_out, prev_out, previous_out, mixers_out, turned_out, resid_out, vectors_out = rest
    prompt_out[...] = prompt[:P_DEV, :]
    lane = lax.broadcasted_iota(jnp.int32, (1, LANES), 1)
    ids = routes[...]
    named = (ids[:, 0:1] == lane) | (ids[:, 1:2] == lane)
    row = lax.broadcasted_iota(jnp.int32, (TOK_DEV, 1), 0)
    col = lax.broadcasted_iota(jnp.int32, (1, TOK_DEV), 1)
    before = jnp.where(col < row, 1.0, 0.0).astype(BF16)
    slots = jnp.where(named, mm(before, jnp.where(named, 1.0, 0.0).astype(BF16)), -1.0)
    slots_out[...] = slots
    block[:TOK_DEV, :] = cot[...]
    block[TOK_DEV:, :TOK_DEV] = jnp.transpose(slots)[:EXT, :].astype(BF16)
    block[TOK_DEV:, TOK_DEV:] = jnp.full((EXT, D - TOK_DEV), -1, BF16)
    routes_out[...] = jnp.where(lane == 0, ids[:, 0:1], jnp.where(lane == 1, ids[:, 1:2], 0))
    wide = lanes_of(prev[...])
    prev_out[...] = wide
    square = jnp.concatenate(
        [lanes_of(resid[...].astype(F32)), jnp.zeros((LANES - IDS, LANES), F32)], axis=0
    )
    turned_resid = jnp.transpose(square).astype(BF16)
    resid_out[...] = turned_resid
    high, rest_of = split(wide)
    low = (wide - high.astype(F32) - rest_of.astype(F32)).astype(BF16)
    resid_low = square.astype(BF16)
    previous_out[...] = mm(high, resid_low) + mm(rest_of, resid_low) + mm(low, resid_low)
    mixers = jnp.concatenate(
        [
            router[...].astype(F32),
            const_w[0].astype(F32),
            const_w[1].astype(F32),
            jnp.zeros((D, LANES - IDS - 4), F32),
        ],
        axis=1,
    )
    mixers_out[...] = mixers.astype(BF16)
    turned_out[...] = jnp.transpose(mixers).astype(BF16)
    vectors_out[...] = jnp.concatenate([const_v[...].astype(F32), jnp.zeros((6, D), F32)], axis=0)


def prepare(routes, prev, cot, router, resid, const_w, const_v, tok, waits):
    vmem = pl.BlockSpec(memory_space=pltpu.VMEM)
    arrays = (routes, prev, cot, router, resid, const_w, const_v, tok)
    outs = (
        shape_of((P_DEV, D), BF16),
        shape_of((BLOCK, D), BF16),
        shape_of((TOK_DEV, LANES), F32),
        shape_of((TOK_DEV, LANES), jnp.int32),
        shape_of((TOK_DEV, LANES), F32),
        shape_of((TOK_DEV, LANES), F32),
        shape_of((D, LANES), BF16),
        shape_of((LANES, D), BF16),
        shape_of((LANES, LANES), BF16),
        shape_of((8, D), F32),
    )
    return pl.pallas_call(
        without(prepare_kernel, len(arrays), len(waits)),
        out_shape=outs,
        in_specs=[vmem] * len(arrays) + [HELD] * len(waits),
        out_specs=tuple([vmem] * len(outs)),
        compiler_params=params(),
        cost_estimate=estimate("prepare", 2 * TOK_DEV * TOK_DEV * LANES, 8 * TOK_DEV * D),
        name="prepare",
    )(*arrays, *waits)


def projection_kernel(group, scal, gain, tok, *rest):
    prompts, shards = rest[: group - 1], rest[group - 1 : 2 * group - 1]
    passed = (len(rest) - 2 * group + 1 - 7) // 2
    q_out, kp_out, vp_out, kc_out, vc_out, w_out, n_out = rest[2 * group - 1 + passed : 2 * group + 6 + passed]
    for at in range(passed):
        rest[2 * group + 6 + passed + at][...] = rest[2 * group - 1 + at][...]
    rows = D // group
    for offset in range(group):
        start = pl.multiple_of(scal[offset] * rows, rows)
        w_out[pl.ds(start, rows), :] = shards[offset][...]

    def normed(values):
        wide = values.astype(F32)
        scale = lax.rsqrt(jnp.mean(wide * wide, axis=-1, keepdims=True) + NORM_EPS)
        return (wide * scale * gain[...]).astype(BF16)

    own = normed(tok[...])
    n_out[...] = own
    q_out[...] = mm(own, w_out[:, :D]).astype(BF16)
    kv = mm(own, w_out[:, D:]).astype(BF16)
    start = pl.multiple_of(scal[0] * P_DEV, P_DEV)
    kp_out[pl.ds(start, P_DEV), :] = kv[:P_DEV, :D]
    vp_out[pl.ds(start, P_DEV), :] = kv[:P_DEV, D:]
    kc_out[:P_DEV, :] = kv[P_DEV:, :D]
    vc_out[:P_DEV, :] = kv[P_DEV:, D:]
    kv = mm(normed(prompts[0][P_DEV:, :]), w_out[:, D:]).astype(BF16)
    kc_out[P_DEV:, :] = kv[:, :D]
    vc_out[P_DEV:, :] = kv[:, D:]
    for offset in range(1, group):
        kv = mm(normed(prompts[offset - 1][:P_DEV, :]), w_out[:, D:]).astype(BF16)
        start = pl.multiple_of(scal[offset] * P_DEV, P_DEV)
        kp_out[pl.ds(start, P_DEV), :] = kv[:, :D]
        vp_out[pl.ds(start, P_DEV), :] = kv[:, D:]


def place_of(local, side):
    half = P_DEV // 2
    return (side + 2 * (local // half)) * half + local % half


def attention_kernel(group, scal, q_ref, kp_ref, vp_ref, kc_ref, vc_ref, o_ref, lse_ref):
    prompt = kp_ref.shape[0]
    index, follow, side = scal[0], scal[group], scal[group + 1]
    lane = lax.broadcasted_iota(jnp.int32, (1, LANES), 1)
    row = lax.broadcasted_iota(jnp.int32, (P_DEV, 1), 0)
    key_at = lax.broadcasted_iota(jnp.int32, (1, prompt), 1)
    cont_at = lax.broadcasted_iota(jnp.int32, (1, 2 * P_DEV), 1)
    cont_place = place_of(cont_at % P_DEV, jnp.where(cont_at < P_DEV, side, 1 - side))
    row_place = place_of(row, side)
    for part in range(2):
        rows = pl.ds(part * P_DEV, P_DEV)
        scaled = q_ref[rows, :] * BF16(1.0 / math.sqrt(HEAD_DIM))
        limit = index * P_DEV + row + 1 if part == 0 else jnp.broadcast_to(follow, (P_DEV, 1))
        mixed, logs = [], []
        for head in range(2):
            masked = jnp.where(lane // HEAD_DIM == head, scaled, BF16(0))
            scores = jnp.where(key_at < limit, mm_nt(masked, kp_ref[...]), MASKED)
            top = jnp.max(scores, axis=1, keepdims=True)
            if part == 1:
                later = jnp.where(cont_place <= row_place, mm_nt(masked, kc_ref[...]), MASKED)
                top = jnp.maximum(top, jnp.max(later, axis=1, keepdims=True))
            weights = jnp.exp(scores - top)
            total = jnp.sum(weights, axis=1, keepdims=True)
            out = mm(weights.astype(BF16), vp_ref[...])
            if part == 1:
                weights = jnp.exp(later - top)
                total = total + jnp.sum(weights, axis=1, keepdims=True)
                out = out + mm(weights.astype(BF16), vc_ref[...])
            mixed.append(out / total)
            logs.append(top + jnp.log(total))
        o_ref[rows, :] = jnp.where(lane < HEAD_DIM, mixed[0], mixed[1])
        lse_ref[rows, :] = jnp.where(lane < HEAD_DIM, logs[0], logs[1])


def attention(scal, q, kp, vp, kc, vc, group, waits):
    prompt = kp.shape[0]
    column = lambda rows: pl.BlockSpec((rows, LANES), lambda p: (0, p))
    flops = 4 * 2 * HEADS * P_DEV * (2 * prompt + 2 * P_DEV) * LANES
    return pl.pallas_call(
        without(partial(attention_kernel, group), 6, len(waits)),
        out_shape=(shape_of((TOK_DEV, D), F32), shape_of((TOK_DEV, D), F32)),
        grid=(PAIRS,),
        in_specs=[pl.BlockSpec(memory_space=pltpu.SMEM)]
        + [column(n) for n in (TOK_DEV, prompt, prompt, 2 * P_DEV, 2 * P_DEV)]
        + [HELD] * len(waits),
        out_specs=(column(TOK_DEV), column(TOK_DEV)),
        compiler_params=params(),
        cost_estimate=estimate("attention_forward", flops, 10 * TOK_DEV * D * 2),
        name="attention_forward",
    )(scal, q, kp, vp, kc, vc, *waits)


def attention_back_kernel(group, scal, q_ref, kp_ref, vp_ref, kc_ref, vc_ref, do_ref, o_ref, lse_ref, *rest):
    prompt = kp_ref.shape[0]
    dq_ref = rest[0]
    pieces = rest[1 : 1 + group]
    own_ref, other_ref, dkp_acc, dvp_acc, dkc_acc, dvc_acc = rest[1 + group :]
    index, follow, side = scal[0], scal[group], scal[group + 1]
    lane = lax.broadcasted_iota(jnp.int32, (1, LANES), 1)
    sub = lax.broadcasted_iota(jnp.int32, (LANES, 1), 0)
    col = lax.broadcasted_iota(jnp.int32, (1, P_DEV), 1)
    key_at = lax.broadcasted_iota(jnp.int32, (prompt, 1), 0)
    cont_at = lax.broadcasted_iota(jnp.int32, (2 * P_DEV, 1), 0)
    cont_place = place_of(cont_at % P_DEV, jnp.where(cont_at < P_DEV, side, 1 - side))
    col_place = place_of(col, side)
    logs = jnp.transpose(lse_ref[...])
    products = jnp.transpose(do_ref[...].astype(F32) * o_ref[...])
    keys_t = jnp.transpose(kp_ref[...])
    later_t = jnp.transpose(kc_ref[...])
    for part in range(2):
        rows = pl.ds(part * P_DEV, P_DEV)
        span = slice(part * P_DEV, (part + 1) * P_DEV)
        scaled = q_ref[rows, :] * BF16(1.0 / math.sqrt(HEAD_DIM))
        grads = do_ref[rows, :]
        limit = index * P_DEV + col + 1 if part == 0 else jnp.broadcast_to(follow, (1, P_DEV))
        turned = []
        for head in range(2):
            mine = lane // HEAD_DIM == head
            query = jnp.where(mine, scaled, BF16(0))
            grad = jnp.where(mine, grads, BF16(0))
            log_row = logs[head * HEAD_DIM : head * HEAD_DIM + 1, span]
            delta = jnp.sum(
                products[head * HEAD_DIM : (head + 1) * HEAD_DIM, span], axis=0, keepdims=True
            )

            def back(keys, values, allowed):
                probs = jnp.exp(jnp.where(allowed, mm_nt(keys, query) - log_row, MASKED))
                score_grad = (probs * (mm_nt(values, grad) - delta)).astype(BF16)
                return score_grad, mm(score_grad, query), mm(probs.astype(BF16), grad)

            score_grad, dk, dv = back(kp_ref[...], vp_ref[...], key_at < limit)
            dq_t = mm(keys_t, score_grad)
            if part == 0 and head == 0:
                dkp_acc[...] = dk
                dvp_acc[...] = dv
            else:
                dkp_acc[...] += dk
                dvp_acc[...] += dv
            if part == 1:
                score_grad, dk, dv = back(kc_ref[...], vc_ref[...], cont_place <= col_place)
                dq_t = dq_t + mm(later_t, score_grad)
                if head == 0:
                    dkc_acc[...] = dk
                    dvc_acc[...] = dv
                else:
                    dkc_acc[...] += dk
                    dvc_acc[...] += dv
            turned.append(dq_t)
        both = jnp.where(sub < HEAD_DIM, turned[0], turned[1]) * (1.0 / math.sqrt(HEAD_DIM))
        dq_ref[rows, :] = jnp.transpose(both).astype(BF16)
    for offset in range(group):
        start = pl.multiple_of(scal[offset] * P_DEV, P_DEV)
        pieces[offset][0] = dkp_acc[pl.ds(start, P_DEV), :].astype(BF16)
        pieces[offset][1] = dvp_acc[pl.ds(start, P_DEV), :].astype(BF16)
    own_ref[0] = dkc_acc[:P_DEV, :]
    own_ref[1] = dvc_acc[:P_DEV, :]
    other_ref[0] = dkc_acc[P_DEV:, :].astype(BF16)
    other_ref[1] = dvc_acc[P_DEV:, :].astype(BF16)


def attention_back(scal, q, kp, vp, kc, vc, do, o32, lse, group, waits):
    prompt = kp.shape[0]
    column = lambda rows: pl.BlockSpec((rows, LANES), lambda p: (0, p))
    double = pl.BlockSpec((2, P_DEV, LANES), lambda p: (0, 0, p))
    flops = 10 * 2 * HEADS * P_DEV * (2 * prompt + 2 * P_DEV) * LANES
    return pl.pallas_call(
        without(partial(attention_back_kernel, group), 9, len(waits)),
        out_shape=(
            shape_of((TOK_DEV, D), BF16),
            *[shape_of((2, P_DEV, D), BF16)] * group,
            shape_of((2, P_DEV, D), F32),
            shape_of((2, P_DEV, D), BF16),
        ),
        grid=(PAIRS,),
        in_specs=[pl.BlockSpec(memory_space=pltpu.SMEM)]
        + [
            column(n)
            for n in (TOK_DEV, prompt, prompt, 2 * P_DEV, 2 * P_DEV, TOK_DEV, TOK_DEV, TOK_DEV)
        ]
        + [HELD] * len(waits),
        out_specs=(column(TOK_DEV), *[double] * group, double, double),
        scratch_shapes=[
            pltpu.VMEM((prompt, LANES), F32),
            pltpu.VMEM((prompt, LANES), F32),
            pltpu.VMEM((2 * P_DEV, LANES), F32),
            pltpu.VMEM((2 * P_DEV, LANES), F32),
        ],
        compiler_params=params(),
        cost_estimate=estimate("attention_backward", flops, 20 * TOK_DEV * D * 2),
        name="attention_backward",
    )(scal, q, kp, vp, kc, vc, do, o32, lse, *waits)


def columns(values):
    lane = lax.broadcasted_iota(jnp.int32, (1, LANES), 1)
    packed = None
    for at, value in values.items():
        term = jnp.where(lane == at, value, 0.0)
        packed = term if packed is None else packed + term
    return packed


def routing_kernel(group, scal, tok, o32, *rest):
    shards = rest[:group]
    gain, mixers, vectors, previous, routes = rest[group : group + 5]
    w_out, res_out, base_out, blk_out, info_out, low_out = rest[group + 5 :]
    rows = D // group
    for offset in range(group):
        start = pl.multiple_of(scal[offset] * rows, rows)
        w_out[pl.ds(start, rows), :] = shards[offset][...]
    low = o32[...].astype(BF16)
    low_out[...] = low
    res = tok[...].astype(F32) + mm(low, w_out[...])
    res_out[...] = res
    scale = lax.rsqrt(jnp.mean(res * res, axis=-1, keepdims=True) + NORM_EPS)
    hidden = res * scale * gain[...]
    hidden_low = hidden.astype(BF16)
    blk_out[:TOK_DEV, :] = hidden_low
    lane = lax.broadcasted_iota(jnp.int32, (1, LANES), 1)
    dots = mm(hidden_low, mixers[...])
    logits = jnp.where(lane < IDS, dots + previous[...], MASKED)
    weights = jnp.exp(logits - jnp.max(logits, axis=1, keepdims=True))
    chances = weights / jnp.sum(weights, axis=1, keepdims=True)
    first, second = routes[:, 0:1], routes[:, 1:2]
    chosen0 = jnp.sum(jnp.where(lane == first, chances, 0.0), axis=1, keepdims=True)
    chosen1 = jnp.sum(jnp.where(lane == second, chances, 0.0), axis=1, keepdims=True)
    both = chosen0 + chosen1
    gate0, gate1 = chosen0 / both, chosen1 / both

    def gate_of(ident):
        return jnp.where(first == ident, gate0, 0.0) + jnp.where(second == ident, gate1, 0.0)

    info = {12: gate0, 13: gate1, 21: both}
    hidden_part = gate_of(EXPERTS + 1)
    base = res
    for member in range(2):
        left = dots[:, IDS + 2 * member : IDS + 2 * member + 1]
        right = dots[:, IDS + 2 * member + 1 : IDS + 2 * member + 2]
        top = jnp.maximum(left, right)
        left, right = jnp.exp(left - top), jnp.exp(right - top)
        alpha0, alpha1 = left / (left + right), right / (left + right)
        gate = gate_of(EXPERTS + 2 + member)
        hidden_part = hidden_part + gate * alpha0
        base = base + (gate * alpha1) * vectors[member : member + 1, :]
        info[15 + member] = gate * alpha1
        info[17 + 2 * member] = alpha0
        info[18 + 2 * member] = alpha1
        info[22 + member] = gate
    info[14] = hidden_part
    base_out[...] = base + hidden_part * hidden
    info_out[...] = jnp.where(lane < IDS, chances, columns(info))
    gates = jnp.where(lane == first, gate0, 0.0) + jnp.where(lane == second, gate1, 0.0)
    turned = jnp.transpose(gates)[:EXPERTS, :]
    high = turned.astype(BF16).astype(F32)
    ext = jnp.concatenate([high, turned - high], axis=0).astype(BF16)
    blk_out[TOK_DEV:, :TOK_DEV] = ext
    blk_out[TOK_DEV:, TOK_DEV:] = jnp.zeros((EXT, D - TOK_DEV), BF16)


def fill_rows(hidden, grads, experts, slots, gates, chooser, scales):
    slot = lax.broadcasted_iota(jnp.int32, (CAP, 1), 0).astype(F32)
    slots[...] = grads[TOK_DEV:, :TOK_DEV].astype(F32)
    pair = hidden[TOK_DEV:, :TOK_DEV].astype(F32)
    gates[...] = pair[:EXPERTS, :] + pair[EXPERTS:, :]
    for at, expert in enumerate(experts):
        picked = slots[pl.ds(expert, 1), :] == slot
        span = pl.ds(at * CAP, CAP)
        chooser[span, :] = jnp.where(picked, 1.0, 0.0).astype(BF16)
        scales[span, :] = jnp.sum(
            jnp.where(picked, gates[pl.ds(expert, 1), :], 0.0), axis=1, keepdims=True
        )
    x = mm(chooser[...], hidden[:TOK_DEV, :]).astype(BF16)
    s = (mm(chooser[...], grads[:TOK_DEV, :]) * scales[...]).astype(BF16)
    return x, s


def row_scratch(experts):
    return (
        pltpu.VMEM((EXT, TOK_DEV), F32),
        pltpu.VMEM((EXPERTS, TOK_DEV), F32),
        pltpu.VMEM((experts * CAP, TOK_DEV), BF16),
        pltpu.VMEM((experts * CAP, 1), F32),
    )


def near_rows_kernel(group, per, share, scal, *rest):
    hidden, grads = rest[:group], rest[group : 2 * group]
    x_out, s_out = rest[2 * group : 2 * group + 2]
    experts = [(scal[0] * per + member) // share for member in range(per)]
    for at in range(group):
        x, s = fill_rows(hidden[at], grads[at], experts, *rest[2 * group + 2 :])
        for member in range(per):
            part = slice(member * CAP, (member + 1) * CAP)
            x_out[member, at * CAP : (at + 1) * CAP, :] = x[part]
            s_out[member, at * CAP : (at + 1) * CAP, :] = s[part]


def near_rows(scal, hidden, grads, group, per, share, waits):
    dims = (per, group * CAP, D)
    return whole_call(
        partial(near_rows_kernel, group, per, share),
        "near_rows",
        scal,
        [*hidden, *grads],
        [shape_of(dims, BF16), shape_of(dims, BF16)],
        4 * group * per * CAP * TOK_DEV * D,
        row_scratch(per),
        waits,
    )


def column_rows_kernel(many, *refs):
    x_out, s_out = refs[-6:-4]
    for at in range(many):

        @pl.when(pl.program_id(0) == at)
        def _():
            x, s = fill_rows(refs[at], refs[many + at], range(EXPERTS), *refs[-4:])
            x_out[...] = x.reshape(1, EXPERTS, CAP, D)
            s_out[...] = s.reshape(1, EXPERTS, CAP, D)


def column_rows(hidden, grads, first, count, stacks, waits):
    many = len(hidden)
    dims = (count, EXPERTS, CAP, D)
    block = pl.BlockSpec((1, *dims[1:]), lambda i: (first + i, 0, 0, 0))
    token = pl.BlockSpec((BLOCK, D), lambda i: (0, 0))
    return pl.pallas_call(
        partial(column_rows_kernel, many),
        out_shape=(shape_of(dims, BF16), shape_of(dims, BF16)),
        grid=(many,),
        in_specs=[token] * (2 * many) + [HELD] * (len(stacks) + len(waits)),
        out_specs=(block, block),
        scratch_shapes=list(row_scratch(EXPERTS)),
        input_output_aliases={2 * many + n: n for n in range(len(stacks))},
        compiler_params=params(),
        cost_estimate=estimate("column_rows",
            4 * many * EXPERTS * CAP * TOK_DEV * D, 4 * many * (BLOCK + EXPERTS * CAP) * D
        ),
        name="column_rows",
    )(*hidden, *grads, *stacks, *waits)


def sigmoid(values):
    return 0.5 * jnp.tanh(0.5 * values) + 0.5


def add_low(left, right):
    return (left.astype(F32) + right.astype(F32)).astype(BF16)


def expert_terms(act_a, act_b, hidden_grad):
    sig = sigmoid(act_a)
    silu = act_a * sig
    hidden = (silu * act_b).astype(BF16)
    grad_a = (hidden_grad * act_b * (sig + silu * (1.0 - sig))).astype(BF16)
    grad_b = (hidden_grad * silu).astype(BF16)
    return hidden, grad_a, grad_b


def expert_kernel(group, offsets, x_ref, s_ref, wg, wu, wd, *rest):
    outs, out_acc, in_acc = rest[:group], rest[group], rest[group + 1]
    step = pl.program_id(0)
    rows = x_ref.shape[1]
    chunk = min(rows, 512)
    for start in range(0, rows, chunk):
        span = pl.ds(start, chunk)
        x = x_ref[0, span, :]
        hidden, grad_a, grad_b = expert_terms(
            mm(x, wg[...]), mm(x, wu[...]), mm_nt(s_ref[0, span, :], wd[...])
        )
        out = mm(hidden, wd[...])
        back = mm_nt(grad_a, wg[...]) + mm_nt(grad_b, wu[...])

        @pl.when(step == 0)
        def _():
            out_acc[span, :] = out
            in_acc[span, :] = back

        @pl.when(step > 0)
        def _():
            out_acc[span, :] += out
            in_acc[span, :] += back

    @pl.when(step == pl.num_programs(0) - 1)
    def _():
        for at in range(group):
            outs[offsets[at]][0] = out_acc[at * CAP : (at + 1) * CAP, :].astype(BF16)
            outs[offsets[at]][1] = in_acc[at * CAP : (at + 1) * CAP, :].astype(BF16)


def local_expert(x, s, gate_w, up_w, down_w, member, offsets, group, per, waits):
    width = gate_w.shape[1] // per
    tile = min(512, width)
    steps = width // tile
    rows = group * CAP
    side = pl.BlockSpec((1, rows, D), lambda t: (member, 0, 0))
    wide = pl.BlockSpec((D, tile), lambda t: (0, member * steps + t))
    tall = pl.BlockSpec((tile, D), lambda t: (member * steps + t, 0))
    piece = pl.BlockSpec((2, CAP, D), lambda t: (0, 0, 0))
    return pl.pallas_call(
        without(partial(expert_kernel, group, offsets), 5, len(waits)),
        out_shape=tuple([shape_of((2, CAP, D), BF16)] * group),
        grid=(steps,),
        in_specs=[side, side, wide, wide, tall] + [HELD] * len(waits),
        out_specs=tuple([piece] * group),
        scratch_shapes=[pltpu.VMEM((rows, D), F32), pltpu.VMEM((rows, D), F32)],
        compiler_params=params(),
        cost_estimate=estimate("local_expert", 12 * rows * D * width, 6 * D * width + 8 * rows * D),
        name="local_expert",
    )(x, s, gate_w, up_w, down_w, *waits)


def pack_kernel(at_ref, wg, wu, wd, out):
    out[0, 0] = jnp.transpose(wg[...])
    out[0, 1] = jnp.transpose(wu[...])
    out[0, 2] = wd[...]


def pack_weights(at, weights, member, per, count, waits):
    tile = weights[0].shape[1] // per // count
    wide = pl.BlockSpec((D, tile), lambda m, ref: (0, ref[0] + member * count))
    tall = pl.BlockSpec((tile, D), lambda m, ref: (ref[0] + member * count, 0))
    return pl.pallas_call(
        without(pack_kernel, 4, len(waits)),
        out_shape=shape_of((1, 3, tile, D), BF16),
        grid_spec=pltpu.PrefetchScalarGridSpec(
            num_scalar_prefetch=1,
            grid=(1,),
            in_specs=[wide, wide, tall] + [HELD] * len(waits),
            out_specs=pl.BlockSpec((1, 3, tile, D), lambda m, ref: (0, 0, 0, 0)),
        ),
        compiler_params=params(),
        cost_estimate=estimate("pack_weights", 0, 12 * tile * D),
        name="pack_weights",
    )(at, *weights, *waits)


def slice_kernel(many, experts, x_ref, s_ref, *rest):
    weights, outs = rest[:many], rest[many:]
    for at in range(many):

        @pl.when(pl.program_id(0) == at)
        def _():
            rows = x_ref.shape[0] * x_ref.shape[2]
            x, s = x_ref[...].reshape(rows, D), s_ref[...].reshape(rows, D)
            gate_w, up_w, down_w = (weights[at][0, n] for n in range(3))
            act_a, act_b = mm_nt(gate_w, x), mm_nt(up_w, x)
            hidden, grad_a, grad_b = expert_terms(act_a, act_b, mm_nt(down_w, s))
            outs[at][0] = mm(grad_a, x).astype(BF16)
            outs[at][1] = mm(grad_b, x).astype(BF16)
            outs[at][2] = mm(hidden, s).astype(BF16)


def weight_slices(experts, stacks, packed, waits):
    count, tile, many = stacks[0].shape[0], packed[0].shape[2], len(packed)
    side = pl.BlockSpec((count, 1, CAP, D), lambda t, ref: (0, ref[t], 0, 0))
    held = pl.BlockSpec((1, 3, tile, D), lambda t, ref: (0, 0, 0, 0))
    out = pl.BlockSpec((3, tile, D), lambda t, ref: (0, 0, 0))
    rows = count * CAP
    return pl.pallas_call(
        without(partial(slice_kernel, many), 3 + many, len(waits)),
        out_shape=tuple([shape_of((3, tile, D), BF16)] * many),
        grid_spec=pltpu.PrefetchScalarGridSpec(
            num_scalar_prefetch=1,
            grid=(many,),
            in_specs=[side, side] + [held] * many + [HELD] * len(waits),
            out_specs=tuple([out] * many),
        ),
        compiler_params=params(),
        cost_estimate=estimate("weight_slices", 12 * many * rows * D * tile, many * (4 * rows + 12 * tile) * D),
        name="weight_slices",
    )(experts, *stacks, *packed, *waits)


def place_kernel(held, at_ref, piece, *rest):
    gate_out, up_out, down_out = rest[held:]
    gate_out[...] = jnp.transpose(piece[0].astype(F32))
    up_out[...] = jnp.transpose(piece[1].astype(F32))
    down_out[...] = piece[2].astype(F32)


def place_slice(at, piece, held, units):
    tile = piece.shape[1]
    wide = pl.BlockSpec((D, tile), lambda t, ref: (0, ref[0]))
    tall = pl.BlockSpec((tile, D), lambda t, ref: (ref[0], 0))
    return pl.pallas_call(
        partial(place_kernel, len(held)),
        out_shape=(shape_of((D, units), F32), shape_of((D, units), F32), shape_of((units, D), F32)),
        grid_spec=pltpu.PrefetchScalarGridSpec(
            num_scalar_prefetch=1,
            grid=(1,),
            in_specs=[pl.BlockSpec((3, tile, D), lambda t, ref: (0, 0, 0))]
            + [HELD] * len(held),
            out_specs=(wide, wide, tall),
        ),
        input_output_aliases={2 + n: n for n in range(len(held))},
        compiler_params=params(),
        cost_estimate=estimate("place_slice", 0, 18 * D * tile),
        name="place_slice",
    )(at, piece, *held)


def combine_kernel(group, per, share, scal, *refs):
    pieces = refs[: group * per]
    (base, cot, blk, info_ref, slots, routes, res_ref, gain, vectors, mixers_t, resid_t, prev, w_out) = refs[
        group * per : group * per + 13
    ]
    layer_out, grad_out, mix_out, mixed_out, prev_out, small_out = refs[group * per + 13 :]
    info = info_ref[...]
    first, second = routes[:, 0:1], routes[:, 1:2]
    lane = lax.broadcasted_iota(jnp.int32, (1, LANES), 1)
    slot_lane = lane.astype(F32)
    taken = slots[...]
    out0 = out1 = back = None
    for offset in range(group):
        for member in range(per):
            expert = (scal[offset] * per + member) // share
            column = jnp.sum(jnp.where(lane == expert, taken, 0.0), axis=1, keepdims=True)
            chooser = column == slot_lane
            piece = pieces[offset * per + member]
            pick0 = jnp.where(chooser & (first == expert), 1.0, 0.0).astype(BF16)
            pick1 = jnp.where(chooser & (second == expert), 1.0, 0.0).astype(BF16)
            add0, add1 = mm(pick0, piece[0]), mm(pick1, piece[0])
            add2 = mm(pick0 + pick1, piece[1])
            out0 = add0 if out0 is None else out0 + add0
            out1 = add1 if out1 is None else out1 + add1
            back = add2 if back is None else back + add2
    get = lambda at: info[:, at : at + 1]
    gate0, gate1, hidden_part, both = get(12), get(13), get(14), get(21)
    layer_out[...] = base[...] + gate0 * out0 + gate1 * out1
    grad = cot[...].astype(F32)
    res = res_ref[...]
    scale = lax.rsqrt(jnp.mean(res * res, axis=-1, keepdims=True) + NORM_EPS)
    unit = res * scale
    total = lambda values: jnp.sum(values, axis=1, keepdims=True)
    dot_hidden = total(grad * (unit * gain[...]))
    dot_vector = [total(grad * vectors[k : k + 1, :]) for k in range(2)]

    def gate_grad(route, out):
        value = total(grad * out) + jnp.where(route == EXPERTS + 1, dot_hidden, 0.0)
        for k in range(2):
            const = get(17 + 2 * k) * dot_hidden + get(18 + 2 * k) * dot_vector[k]
            value = value + jnp.where(route == EXPERTS + 2 + k, const, 0.0)
        return value

    dgate0, dgate1 = gate_grad(first, out0), gate_grad(second, out1)
    mean = gate0 * dgate0 + gate1 * dgate1
    dchance = (
        jnp.where(lane == first, dgate0 - mean, 0.0) + jnp.where(lane == second, dgate1 - mean, 0.0)
    ) / both
    chances = jnp.where(lane < IDS, info, 0.0)
    logits_grad = chances * (dchance - total(chances * dchance))
    extra = {16: get(15), 17: get(16)}
    for k in range(2):
        alpha0, alpha1, gate = get(17 + 2 * k), get(18 + 2 * k), get(22 + k)
        d0, d1 = gate * dot_hidden, gate * dot_vector[k]
        inner = alpha0 * d0 + alpha1 * d1
        extra[IDS + 2 * k] = alpha0 * (d0 - inner)
        extra[IDS + 2 * k + 1] = alpha1 * (d1 - inner)
    packed = logits_grad + columns(extra)
    high, low = split(packed)
    prev_out[...] = mm(high, resid_t[...]) + mm(low, resid_t[...])
    hidden_total = (
        back + hidden_part * grad + mm(high, mixers_t[...]) + mm(low, mixers_t[...])
    )
    turned = jnp.transpose(packed)[:32, :]
    t_high, t_low = split(turned)
    hidden_low = blk[:TOK_DEV, :]
    by_hidden = mm(t_high, hidden_low) + mm(t_low, hidden_low)
    by_grad = mm(t_high, cot[...]) + mm(t_low, cot[...])
    prev_high, prev_low = split(prev[...])
    by_prev = mm(t_high, prev_high) + mm(t_high, prev_low) + mm(t_low, prev_high)
    gain_grad = jnp.sum(hidden_total * unit, axis=0, keepdims=True)
    sub = lax.broadcasted_iota(jnp.int32, (8, 1), 0)
    small_out[:16, :] = by_hidden[:16, :]
    small_out[16:24, :] = jnp.where(sub == 2, gain_grad, by_grad[16:24, :])
    small_out[24:40, :] = jnp.zeros((16, D), F32)
    small_out[24:40, :LANES] = by_prev[:16, :]
    u = gain[...] * hidden_total
    inner = jnp.mean(res * u, axis=1, keepdims=True)
    residual_grad = grad + scale * u - res * (scale * scale * scale * inner)
    grad_out[...] = residual_grad
    mix = residual_grad.astype(BF16)
    mix_out[...] = mix
    mixed_out[...] = mm_nt(mix, w_out[...]).astype(BF16)


def finish_kernel(prompt_terms, scal, dq, own, received, *rest):
    terms = rest[:prompt_terms]
    weights, tok, gain, res_grad = rest[prompt_terms : prompt_terms + 4]
    low_out, grad_out, small_out = rest[prompt_terms + 4 :]
    low_out[:, :D] = dq[...]
    for half in range(2):
        columns_at = slice((half + 1) * D, (half + 2) * D)
        prompt = terms[0][half].astype(F32)
        for term in terms[1:]:
            prompt = prompt + term[half].astype(F32)
        low_out[:P_DEV, columns_at] = prompt.astype(BF16)
        low_out[P_DEV:, columns_at] = (own[half] + received[half].astype(F32)).astype(BF16)
    normed_grad = mm_nt(low_out[...], weights[...])
    x = tok[...].astype(F32)
    scale = lax.rsqrt(jnp.mean(x * x, axis=-1, keepdims=True) + NORM_EPS)
    u = gain[...] * normed_grad
    inner = jnp.mean(x * u, axis=1, keepdims=True)
    grad_out[...] = res_grad[...] + scale * u - x * (scale * scale * scale * inner)
    row = jnp.sum(normed_grad * (x * scale), axis=0, keepdims=True)
    sub = lax.broadcasted_iota(jnp.int32, (8, 1), 0)
    small_out[...] = jnp.where(sub == 0, row, 0.0)


def sum_everywhere(value):
    for axis in ("rep", "grp"):
        count = lax.axis_size(axis)
        bit = 1
        while bit < count:
            pairs = [(source, source ^ bit) for source in range(count)]
            value = value + lax.ppermute(value, axis, pairs)
            bit *= 2
    return value


def sum_replicas(value):
    count = lax.axis_size("rep")
    index = lax.axis_index("rep")
    bits = [1 << n for n in range(count.bit_length() - 1)]
    for bit in bits:
        half = value.shape[1] // 2
        left, right = value[:, :half], value[:, half:]
        upper = (index & bit) != 0
        keep = jnp.where(upper, right, left)
        give = jnp.where(upper, left, right).astype(BF16)
        pairs = [(source, source ^ bit) for source in range(count)]
        value = keep + lax.ppermute(give, "rep", pairs).astype(F32)
    value = value.astype(BF16)
    for bit in reversed(bits):
        pairs = [(source, source ^ bit) for source in range(count)]
        other = lax.ppermute(value, "rep", pairs)
        upper = (index & bit) != 0
        value = jnp.concatenate(
            [jnp.where(upper, other, value), jnp.where(upper, value, other)], axis=1
        )
    return value.astype(F32)


def body(
    tokens,
    prev_logits,
    routes,
    branch_points,
    cotangent,
    attn_gain,
    qkv_weight,
    out_weight,
    ffn_gain,
    router_weight,
    resid_weight,
    const_weight,
    const_vector,
    gate_weight,
    up_weight,
    down_weight,
):
    group, count = lax.axis_size("grp"), lax.axis_size("rep")
    index, replica = lax.axis_index("grp"), lax.axis_index("rep")
    per, share = max(1, EXPERTS // group), max(1, group // EXPERTS)
    prompt = P_DEV * group
    spread = group * count <= 32
    tok, cot, route_rows, prev = tokens[0], cotangent[0], routes[0], prev_logits[0]
    follow = lax.dynamic_index_in_dim(branch_points[0], index // 2, keepdims=True)
    scal = jnp.concatenate(
        [
            index ^ jnp.arange(group, dtype=jnp.int32),
            follow.astype(jnp.int32),
            (index % 2)[None].astype(jnp.int32),
        ]
    )

    shards = gather_group(qkv_weight, 1)
    weights = (gate_weight, up_weight, down_weight)
    mine = replica.astype(jnp.int32)[None]
    early = []
    if spread:
        early = [pack_weights(mine, weights, 0, per, count, ())]
    (
        prompt_rows,
        grad_block,
        slots,
        route_lanes,
        prev_lanes,
        previous,
        mixers,
        mixers_t,
        resid_t,
        vectors,
    ) = prepare(
        route_rows,
        prev,
        cot,
        router_weight,
        resid_weight,
        const_weight,
        const_vector,
        tok,
        early,
    )
    prompts = gather_group(prompt_rows, 2)
    for offset in range(0, group, 2):
        prompts[offset + 1] = xor_permute(prompts[offset] if offset else tok, 1)
    gain_one = attn_gain.astype(F32)[None]
    gain_two = ffn_gain.astype(F32)[None]

    offsets = [o for o in range(0, group, 2)] + [o for o in range(1, group, 2)]

    def group_blocks(block):
        held = gather_group(block, 2)
        own = [held[o] for o in range(0, group, 2)]
        return own + [xor_permute(piece, 1) for piece in own]

    def all_blocks(block):
        result, forth, back = [[block]], block, block
        for step in range(1, count // 2 + 1):
            forth = ring_permute(forth, 1)
            result.append([forth])
            if step < count - step:
                back = ring_permute(back, -1)
                result[-1].append(back)
        return result

    grad_far = all_blocks(grad_block) if spread else [[grad_block]]
    hops = len(grad_far) - 1

    def hop_of(blocks, at):
        return blocks[at] if 0 < at <= hops else []

    q, kp, vp, kc, vc, w_qkv, normed, later_block, later_shard, *early = whole_call(
        partial(projection_kernel, group),
        "projections",
        scal,
        [gain_one, tok]
        + [prompts[o] for o in range(1, group)]
        + [shards[o] for o in range(group)]
        + [grad_block, out_weight, *early],
        [
            shape_of((TOK_DEV, D), BF16),
            shape_of((prompt, D), BF16),
            shape_of((prompt, D), BF16),
            shape_of((2 * P_DEV, D), BF16),
            shape_of((2 * P_DEV, D), BF16),
            shape_of((D, 3 * D), BF16),
            shape_of((TOK_DEV, D), BF16),
            shape_of((BLOCK, D), BF16),
            shape_of((D // group, D), BF16),
            *[shape_of(v.shape, BF16) for v in early],
        ],
        2 * TOK_DEV * D * D + 4 * (prompt + 2 * P_DEV) * D * D,
    )
    out_shards = gather_group(later_shard, 1)
    grad_near = group_blocks(later_block)
    packed = [gather_group(v, 1) for v in early]
    o32, lse = attention(scal, q, kp, vp, kc, vc, group, hop_of(grad_far, 1) if W_FRONT else [])
    w_out, res, base, block, info, mixed_low = whole_call(
        partial(routing_kernel, group),
        "routing",
        scal,
        [tok, o32]
        + [out_shards[o] for o in range(group)]
        + [gain_two, mixers, vectors, previous, route_lanes],
        [
            shape_of((D, D), BF16),
            shape_of((TOK_DEV, D), F32),
            shape_of((TOK_DEV, D), F32),
            shape_of((BLOCK, D), BF16),
            shape_of((TOK_DEV, LANES), F32),
            shape_of((TOK_DEV, D), BF16),
        ],
        2 * TOK_DEV * D * D,
        waits=[*(hop_of(grad_far, 2) if W_FRONT else []), *(grad_near[1:-1] if W_NEAR else [])],
    )

    near = group_blocks(block)
    rings, returned, locals_out = [], {}, []

    def give_back(member):
        for offset in range(group):
            value = locals_out[member][offset]
            returned[offset, member] = xor_permute(value, offset) if offset else value
        return [returned[offset, member] for offset in range(1, group)]

    if not spread:
        local = near_rows(scal, near, grad_near, group, per, share, ())
        locals_out = [
            local_expert(*local, *weights, member, offsets, group, per, ())
            for member in range(per)
        ]
    else:
        forth = back = block
        stacks, done, kept = (), 0, []
        for hop in range(1, hops + 1):
            forth = ring_permute(forth, 1)
            back = ring_permute(back, -1) if hop < count - hop else None
            take, waits = [(block, grad_block)], hop_of(grad_far, 3)
            if hop == 2:
                take, waits = kept, hop_of(grad_far, 4)
            elif hop > 2:
                take, waits = kept if hop == hops else (), locals_out[-1][:1] if locals_out else ()
            kept = [] if hop == 1 or take is kept else kept
            if take:
                stacks = column_rows(
                    [h for h, g in take], [g for h, g in take], done, count, stacks, waits
                )
                done += len(take)
            if hop == 2:
                for member in range(1, per):
                    later = pack_weights(mine, weights, member, per, count, [near[1], *([h for h, g in take] if W_PACK else [])])
                    packed.append(gather_group(later, 1))
            if hop == 3:
                waits = [packed[-1][0], *packed[0].values(), stacks[0]]
                local = near_rows(scal, near, grad_near, group, per, share, waits[:-1])
                locals_out.append(
                    local_expert(*local, *weights, 0, offsets, group, per, ())
                )
            kept = kept + list(zip([v for v in (forth, back) if v is not None], grad_far[hop]))
        stacks = column_rows(
            [h for h, g in kept], [g for h, g in kept], done, count, stacks, ()
        )
        parts = [{} for _ in range(per)]
        last = [v for p in packed for v in p.values()]
        for low in range(group - 2, -1, -2):
            chosen = [(m, o) for m in range(per) for o in (low + 1, low)]
            experts = jnp.stack([(index ^ o) * per + m for m, o in chosen]).astype(jnp.int32)
            outs = weight_slices(experts, stacks, [packed[m][o] for m, o in chosen], last)
            for m in range(per):
                parts[m][low] = add_low(outs[2 * m + 1], xor_permute(outs[2 * m], 1))
            last = [outs[0]]
            if low:
                last += [parts[0][low]]
                last += give_back(0) if W_SLICE else []
        for member, part in enumerate(parts):
            bit = 2
            while bit < group:
                for offset in sorted(part, reverse=True):
                    if offset & bit:
                        value = part.pop(offset)
                        if rings:
                            value, rings[-1][0] = lax.optimization_barrier((value, rings[-1][0]))
                        value = xor_permute(value, bit)
                        if rings:
                            waits = [last[0], rings[0][0]] if W_LOCAL else []
                            outs = local_expert(
                                *local, *weights, member, offsets, group, per, waits
                            )
                            if W_LOCAL:
                                value, *outs = lax.optimization_barrier((value, *outs))
                            locals_out.append(outs)
                            give_back(member)
                        part[offset ^ bit] = add_low(part[offset ^ bit], value)
                bit *= 2
            rings.append([part[0]])
    for member in range(per):
        if (0, member) not in returned:
            give_back(member)
    placed = ()
    units = gate_weight.shape[1]
    spot = jnp.where(replica % 2 == 0, replica // 2, count - 1 - replica // 2)

    def advance(step):
        nonlocal placed
        for member, ring in enumerate(rings):
            toward = 1 - 2 * (member % 2)
            if step < count:
                ring.append(ring_permute(ring[-1], toward))
            source = (spot - toward * (step - 1)) % count
            source = jnp.where(source < count // 2, 2 * source, 2 * (count - 1 - source) + 1)
            at = source.astype(jnp.int32)[None] + member * count
            placed = place_slice(at, ring[step - 1], placed, units)
            if step < count and W_BACK:
                ring[step], *placed = lax.optimization_barrier((ring[step], *placed))

    def advance_to(*steps):
        for step in steps:
            if spread:
                advance(step)

    def arrived(*steps):
        return [ring[step] for ring, step in zip(rings, steps) if step >= 0]

    advance_to(1, 2, 3)
    layer_out, res_grad, mix_grad, mixed_grad, prev_grad, small = whole_call(
        partial(combine_kernel, group, per, share),
        "combine",
        scal,
        [returned[o, m] for o in range(group) for m in range(per)]
        + [
            base,
            cot,
            block,
            info,
            slots,
            route_lanes,
            res,
            gain_two,
            vectors,
            mixers_t,
            resid_t,
            prev_lanes,
            w_out,
        ],
        [
            shape_of((TOK_DEV, D), F32),
            shape_of((TOK_DEV, D), F32),
            shape_of((TOK_DEV, D), BF16),
            shape_of((TOK_DEV, D), BF16),
            shape_of((TOK_DEV, LANES), F32),
            shape_of((SMALL_ROWS, D), F32),
        ],
        6 * TOK_DEV * group * per * CAP * D + 2 * TOK_DEV * D * D,
        waits=arrived(1, 0) if W_RING else (),
    )

    back = attention_back(
        scal, q, kp, vp, kc, vc, mixed_grad, o32, lse, group, arrived(2, 1) if W_RING else []
    )
    dq, pieces, later_own, later_other = back[0], list(back[1 : 1 + group]), back[-2], back[-1]
    if W_KEYS and spread:
        tied = lax.optimization_barrier((later_other, *pieces[1:], rings[0][3], rings[1][2]))
        later_other, rings[0][3], rings[1][2] = tied[0], tied[-2], tied[-1]
        pieces = [pieces[0], *tied[1:-2]]
    advance_to(4, 5)
    later_in = xor_permute(later_other, 1)
    held = {o: [pieces[o]] for o in range(group)}
    bit = 1
    while bit < group:
        for offset in sorted(held):
            if offset & bit:
                terms = held.pop(offset)
                value = terms[0]
                if len(terms) > 1:
                    value = sum(t.astype(F32) for t in terms).astype(BF16)
                held[offset ^ bit].append(xor_permute(value, bit))
        bit *= 2
    terms = held[0]
    qkv_low, input_grad, small_two = whole_call(
        partial(finish_kernel, len(terms)),
        "finish",
        scal,
        [dq, later_own, later_in] + terms + [w_qkv, tok, gain_one, res_grad],
        [
            shape_of((TOK_DEV, 3 * D), BF16),
            shape_of((TOK_DEV, D), F32),
            shape_of((8, D), F32),
        ],
        6 * TOK_DEV * D * D,
        waits=(arrived(4, 3) if W_KEYS else arrived(3, 2)) if W_RING else (),
    )
    full = jnp.concatenate([mm_tn(normed, qkv_low), mm_tn(mixed_low, mix_grad)], axis=1)
    rows = D // group
    held = {
        o: lax.dynamic_slice_in_dim(full, (index ^ o) * rows, rows, axis=0) for o in range(group)
    }
    bit, at = 1, 5
    while bit < group:
        for offset in sorted(held):
            if offset & bit:
                value = xor_permute(held.pop(offset).astype(BF16), bit)
                if W_DENSE and spread and offset == bit:
                    value, rings[0][at], rings[1][at - 1] = lax.optimization_barrier(
                        (value, rings[0][at], rings[1][at - 1])
                    )
                    at += 1
                    advance_to(at)
                held[offset ^ bit] = held[offset ^ bit] + value.astype(F32)
        bit *= 2
    if SC_DENSE:
        dense = lax.psum(held[0].astype(BF16), "rep").astype(F32)
    else:
        dense = sum_replicas(held[0])
    small = jnp.concatenate([small, small_two], axis=0)
    small = lax.psum(small, ("rep", "grp")) if SC_SMALL else sum_everywhere(small)

    if spread:
        for step in range(len(rings[0]), count + 1):
            advance(step)
        gate_sum, up_sum, down_sum = placed
    else:
        x, s = local[0][0], local[1][0]
        hidden, grad_a, grad_b = expert_terms(
            mm(x, gate_weight), mm(x, up_weight), mm_nt(s, down_weight)
        )
        sums = (mm_tn(x, grad_a), mm_tn(x, grad_b), mm_tn(hidden, s))
        gate_sum, up_sum, down_sum = [
            lax.psum(part.astype(BF16), "rep").astype(F32) for part in sums
        ]

    gains = jnp.stack([small[SMALL_ROWS], small[18]], axis=0)
    router_grad = jnp.transpose(small[:IDS])
    const_grad = jnp.transpose(small[IDS : IDS + 4].reshape(2, 2, D), (0, 2, 1))
    resid_grad = jnp.transpose(small[24 : 24 + IDS, :IDS])
    return (
        layer_out[None],
        input_grad[None],
        prev_grad[:, :IDS][None],
        gains,
        dense[:, : 3 * D],
        dense[:, 3 * D :],
        router_grad,
        resid_grad,
        const_grad,
        small[16:18],
        gate_sum,
        up_sum,
        down_sum,
    )


def solution(mesh):
    in_specs = (
        P("rep", "grp", None),
        P("rep", "grp", None),
        P("rep", "grp", None),
        P("rep", None),
        P("rep", "grp", None),
        P(),
        P("grp", None),
        P("grp", None),
        P(),
        P(),
        P(),
        P(),
        P(),
        P(None, "grp"),
        P(None, "grp"),
        P("grp", None),
    )
    out_specs = (
        P("rep", "grp", None),
        P("rep", "grp", None),
        P("rep", "grp", None),
        P(),
        P("grp", None),
        P("grp", None),
        P(),
        P(),
        P(),
        P(),
        P(None, "grp"),
        P(None, "grp"),
        P("grp", None),
    )
    return jax.shard_map(body, mesh=mesh, in_specs=in_specs, out_specs=out_specs, check_vma=False)
```

```python
from functools import partial
import math

import jax
import jax.numpy as jnp
import numpy as np
from jax import lax
from jax.experimental import pallas as pl
from jax.experimental.pallas import tpu as pltpu
from jax.sharding import PartitionSpec as P

D = 768
HEADS = 12
HEAD_DIM = 64
EXPERTS = 8
TOP = 2
P_DEV = 256
TOK_DEV = 512
CAP = 128
IDS = EXPERTS + 4
EXT = 16
BLOCK = TOK_DEV + EXT
LANES = 128
PAIRS = D // LANES

NORM_EPS = 1e-06
MASKED = -1e30
HIGHEST = lax.Precision.HIGHEST
F32 = jnp.float32
BF16 = jnp.bfloat16
VMEM_LIMIT = 56 * 2**20
SMALL_ROWS = 40
COST = {"column_rows": 4.0}
W_KEYS = 1
SC_DENSE = 1
W_DENSE = 1
SC_SMALL = 0
W_PACK = 0
W_NEAR = 1
W_FRONT = 1
W_RING = 0
W_LOCAL = 1
W_SLICE = 1
W_BACK = 1


def mm(left, right):
    return jnp.dot(left, right, preferred_element_type=F32)


def mm_nt(left, right):
    return lax.dot_general(left, right, (((1,), (1,)), ((), ())), preferred_element_type=F32)


def mm_tn(left, right):
    return lax.dot_general(left, right, (((0,), (0,)), ((), ())), preferred_element_type=F32)


def split(values):
    high = values.astype(BF16)
    return high, (values - high.astype(F32)).astype(BF16)


def shape_of(dims, dtype):
    return jax.ShapeDtypeStruct(dims, dtype)


def estimate(name, flops, bytes_accessed):
    scale = COST.get(name, 1.0)
    return pl.CostEstimate(
        flops=int(scale * flops), bytes_accessed=int(scale * bytes_accessed), transcendentals=0
    )


def params():
    return pltpu.CompilerParams(vmem_limit_bytes=VMEM_LIMIT)


def without(kernel, first, count):
    if not count:
        return kernel

    def run(*refs):
        return kernel(*refs[:first], *refs[first + count :])

    return run


HELD = pl.BlockSpec(memory_space=pl.ANY)


def whole_call(kernel, name, scalars, arrays, outs, flops, scratch=(), waits=()):
    vmem = pl.BlockSpec(memory_space=pltpu.VMEM)
    moved = sum(a.size * a.dtype.itemsize for a in arrays)
    moved += sum(math.prod(o.shape) * np.dtype(o.dtype).itemsize for o in outs)
    return pl.pallas_call(
        without(kernel, 1 + len(arrays), len(waits)),
        out_shape=tuple(outs),
        in_specs=[pl.BlockSpec(memory_space=pltpu.SMEM)]
        + [vmem] * len(arrays)
        + [HELD] * len(waits),
        out_specs=tuple([vmem] * len(outs)),
        scratch_shapes=list(scratch),
        compiler_params=params(),
        cost_estimate=estimate(name, flops, moved),
        name=name,
    )(scalars, *arrays, *waits)


def xor_permute(value, offset):
    pairs = [(source, source ^ offset) for source in range(lax.axis_size("grp"))]
    return lax.ppermute(value, "grp", pairs)


def ring_permute(value, step):
    count = lax.axis_size("rep")
    order = list(range(0, count, 2)) + list(range(count - 1, 0, -2))
    pairs = [(order[at], order[(at + step) % count]) for at in range(count)]
    return lax.ppermute(value, "rep", pairs)


def gather_group(value, lowest):
    pieces = {0: value}
    bit = lax.axis_size("grp") // 2
    while bit >= lowest:
        for offset in list(pieces):
            pieces[offset | bit] = xor_permute(pieces[offset], bit)
        bit //= 2
    return pieces


def lanes_of(values):
    rows, width = values.shape
    return jnp.concatenate([values, jnp.zeros((rows, LANES - width), values.dtype)], axis=1)


def prepare_kernel(routes, prev, cot, router, resid, const_w, const_v, prompt, *rest):
    prompt_out, block, slots_out, routes_out, prev_out, previous_out, mixers_out, turned_out, resid_out, vectors_out = rest
    prompt_out[...] = prompt[:P_DEV, :]
    lane = lax.broadcasted_iota(jnp.int32, (1, LANES), 1)
    ids = routes[...]
    named = (ids[:, 0:1] == lane) | (ids[:, 1:2] == lane)
    row = lax.broadcasted_iota(jnp.int32, (TOK_DEV, 1), 0)
    col = lax.broadcasted_iota(jnp.int32, (1, TOK_DEV), 1)
    before = jnp.where(col < row, 1.0, 0.0).astype(BF16)
    slots = jnp.where(named, mm(before, jnp.where(named, 1.0, 0.0).astype(BF16)), -1.0)
    slots_out[...] = slots
    block[:TOK_DEV, :] = cot[...]
    block[TOK_DEV:, :TOK_DEV] = jnp.transpose(slots)[:EXT, :].astype(BF16)
    block[TOK_DEV:, TOK_DEV:] = jnp.full((EXT, D - TOK_DEV), -1, BF16)
    routes_out[...] = jnp.where(lane == 0, ids[:, 0:1], jnp.where(lane == 1, ids[:, 1:2], 0))
    wide = lanes_of(prev[...])
    prev_out[...] = wide
    square = jnp.concatenate(
        [lanes_of(resid[...].astype(F32)), jnp.zeros((LANES - IDS, LANES), F32)], axis=0
    )
    turned_resid = jnp.transpose(square).astype(BF16)
    resid_out[...] = turned_resid
    high, rest_of = split(wide)
    low = (wide - high.astype(F32) - rest_of.astype(F32)).astype(BF16)
    resid_low = square.astype(BF16)
    previous_out[...] = mm(high, resid_low) + mm(rest_of, resid_low) + mm(low, resid_low)
    mixers = jnp.concatenate(
        [
            router[...].astype(F32),
            const_w[0].astype(F32),
            const_w[1].astype(F32),
            jnp.zeros((D, LANES - IDS - 4), F32),
        ],
        axis=1,
    )
    mixers_out[...] = mixers.astype(BF16)
    turned_out[...] = jnp.transpose(mixers).astype(BF16)
    vectors_out[...] = jnp.concatenate([const_v[...].astype(F32), jnp.zeros((6, D), F32)], axis=0)


def prepare(routes, prev, cot, router, resid, const_w, const_v, tok, waits):
    vmem = pl.BlockSpec(memory_space=pltpu.VMEM)
    arrays = (routes, prev, cot, router, resid, const_w, const_v, tok)
    outs = (
        shape_of((P_DEV, D), BF16),
        shape_of((BLOCK, D), BF16),
        shape_of((TOK_DEV, LANES), F32),
        shape_of((TOK_DEV, LANES), jnp.int32),
        shape_of((TOK_DEV, LANES), F32),
        shape_of((TOK_DEV, LANES), F32),
        shape_of((D, LANES), BF16),
        shape_of((LANES, D), BF16),
        shape_of((LANES, LANES), BF16),
        shape_of((8, D), F32),
    )
    return pl.pallas_call(
        without(prepare_kernel, len(arrays), len(waits)),
        out_shape=outs,
        in_specs=[vmem] * len(arrays) + [HELD] * len(waits),
        out_specs=tuple([vmem] * len(outs)),
        compiler_params=params(),
        cost_estimate=estimate("prepare", 2 * TOK_DEV * TOK_DEV * LANES, 8 * TOK_DEV * D),
        name="prepare",
    )(*arrays, *waits)


def projection_kernel(group, scal, gain, tok, *rest):
    prompts, shards = rest[: group - 1], rest[group - 1 : 2 * group - 1]
    passed = (len(rest) - 2 * group + 1 - 7) // 2
    q_out, kp_out, vp_out, kc_out, vc_out, w_out, n_out = rest[2 * group - 1 + passed : 2 * group + 6 + passed]
    for at in range(passed):
        rest[2 * group + 6 + passed + at][...] = rest[2 * group - 1 + at][...]
    rows = D // group
    for offset in range(group):
        start = pl.multiple_of(scal[offset] * rows, rows)
        w_out[pl.ds(start, rows), :] = shards[offset][...]

    def normed(values):
        wide = values.astype(F32)
        scale = lax.rsqrt(jnp.mean(wide * wide, axis=-1, keepdims=True) + NORM_EPS)
        return (wide * scale * gain[...]).astype(BF16)

    own = normed(tok[...])
    n_out[...] = own
    q_out[...] = mm(own, w_out[:, :D]).astype(BF16)
    kv = mm(own, w_out[:, D:]).astype(BF16)
    start = pl.multiple_of(scal[0] * P_DEV, P_DEV)
    kp_out[pl.ds(start, P_DEV), :] = kv[:P_DEV, :D]
    vp_out[pl.ds(start, P_DEV), :] = kv[:P_DEV, D:]
    kc_out[:P_DEV, :] = kv[P_DEV:, :D]
    vc_out[:P_DEV, :] = kv[P_DEV:, D:]
    kv = mm(normed(prompts[0][P_DEV:, :]), w_out[:, D:]).astype(BF16)
    kc_out[P_DEV:, :] = kv[:, :D]
    vc_out[P_DEV:, :] = kv[:, D:]
    for offset in range(1, group):
        kv = mm(normed(prompts[offset - 1][:P_DEV, :]), w_out[:, D:]).astype(BF16)
        start = pl.multiple_of(scal[offset] * P_DEV, P_DEV)
        kp_out[pl.ds(start, P_DEV), :] = kv[:, :D]
        vp_out[pl.ds(start, P_DEV), :] = kv[:, D:]


def place_of(local, side):
    half = P_DEV // 2
    return (side + 2 * (local // half)) * half + local % half


def attention_kernel(group, scal, q_ref, kp_ref, vp_ref, kc_ref, vc_ref, o_ref, lse_ref):
    prompt = kp_ref.shape[0]
    index, follow, side = scal[0], scal[group], scal[group + 1]
    lane = lax.broadcasted_iota(jnp.int32, (1, LANES), 1)
    row = lax.broadcasted_iota(jnp.int32, (P_DEV, 1), 0)
    key_at = lax.broadcasted_iota(jnp.int32, (1, prompt), 1)
    cont_at = lax.broadcasted_iota(jnp.int32, (1, 2 * P_DEV), 1)
    cont_place = place_of(cont_at % P_DEV, jnp.where(cont_at < P_DEV, side, 1 - side))
    row_place = place_of(row, side)
    for part in range(2):
        rows = pl.ds(part * P_DEV, P_DEV)
        scaled = q_ref[rows, :] * BF16(1.0 / math.sqrt(HEAD_DIM))
        limit = index * P_DEV + row + 1 if part == 0 else jnp.broadcast_to(follow, (P_DEV, 1))
        mixed, logs = [], []
        for head in range(2):
            masked = jnp.where(lane // HEAD_DIM == head, scaled, BF16(0))
            scores = jnp.where(key_at < limit, mm_nt(masked, kp_ref[...]), MASKED)
            top = jnp.max(scores, axis=1, keepdims=True)
            if part == 1:
                later = jnp.where(cont_place <= row_place, mm_nt(masked, kc_ref[...]), MASKED)
                top = jnp.maximum(top, jnp.max(later, axis=1, keepdims=True))
            weights = jnp.exp(scores - top)
            total = jnp.sum(weights, axis=1, keepdims=True)
            out = mm(weights.astype(BF16), vp_ref[...])
            if part == 1:
                weights = jnp.exp(later - top)
                total = total + jnp.sum(weights, axis=1, keepdims=True)
                out = out + mm(weights.astype(BF16), vc_ref[...])
            mixed.append(out / total)
            logs.append(top + jnp.log(total))
        o_ref[rows, :] = jnp.where(lane < HEAD_DIM, mixed[0], mixed[1])
        lse_ref[rows, :] = jnp.where(lane < HEAD_DIM, logs[0], logs[1])


def attention(scal, q, kp, vp, kc, vc, group, waits):
    prompt = kp.shape[0]
    column = lambda rows: pl.BlockSpec((rows, LANES), lambda p: (0, p))
    flops = 4 * 2 * HEADS * P_DEV * (2 * prompt + 2 * P_DEV) * LANES
    return pl.pallas_call(
        without(partial(attention_kernel, group), 6, len(waits)),
        out_shape=(shape_of((TOK_DEV, D), F32), shape_of((TOK_DEV, D), F32)),
        grid=(PAIRS,),
        in_specs=[pl.BlockSpec(memory_space=pltpu.SMEM)]
        + [column(n) for n in (TOK_DEV, prompt, prompt, 2 * P_DEV, 2 * P_DEV)]
        + [HELD] * len(waits),
        out_specs=(column(TOK_DEV), column(TOK_DEV)),
        compiler_params=params(),
        cost_estimate=estimate("attention_forward", flops, 10 * TOK_DEV * D * 2),
        name="attention_forward",
    )(scal, q, kp, vp, kc, vc, *waits)


def attention_back_kernel(group, scal, q_ref, kp_ref, vp_ref, kc_ref, vc_ref, do_ref, o_ref, lse_ref, *rest):
    prompt = kp_ref.shape[0]
    dq_ref = rest[0]
    pieces = rest[1 : 1 + group]
    own_ref, other_ref, dkp_acc, dvp_acc, dkc_acc, dvc_acc = rest[1 + group :]
    index, follow, side = scal[0], scal[group], scal[group + 1]
    lane = lax.broadcasted_iota(jnp.int32, (1, LANES), 1)
    sub = lax.broadcasted_iota(jnp.int32, (LANES, 1), 0)
    col = lax.broadcasted_iota(jnp.int32, (1, P_DEV), 1)
    key_at = lax.broadcasted_iota(jnp.int32, (prompt, 1), 0)
    cont_at = lax.broadcasted_iota(jnp.int32, (2 * P_DEV, 1), 0)
    cont_place = place_of(cont_at % P_DEV, jnp.where(cont_at < P_DEV, side, 1 - side))
    col_place = place_of(col, side)
    logs = jnp.transpose(lse_ref[...])
    products = jnp.transpose(do_ref[...].astype(F32) * o_ref[...])
    keys_t = jnp.transpose(kp_ref[...])
    later_t = jnp.transpose(kc_ref[...])
    for part in range(2):
        rows = pl.ds(part * P_DEV, P_DEV)
        span = slice(part * P_DEV, (part + 1) * P_DEV)
        scaled = q_ref[rows, :] * BF16(1.0 / math.sqrt(HEAD_DIM))
        grads = do_ref[rows, :]
        limit = index * P_DEV + col + 1 if part == 0 else jnp.broadcast_to(follow, (1, P_DEV))
        turned = []
        for head in range(2):
            mine = lane // HEAD_DIM == head
            query = jnp.where(mine, scaled, BF16(0))
            grad = jnp.where(mine, grads, BF16(0))
            log_row = logs[head * HEAD_DIM : head * HEAD_DIM + 1, span]
            delta = jnp.sum(
                products[head * HEAD_DIM : (head + 1) * HEAD_DIM, span], axis=0, keepdims=True
            )

            def back(keys, values, allowed):
                probs = jnp.exp(jnp.where(allowed, mm_nt(keys, query) - log_row, MASKED))
                score_grad = (probs * (mm_nt(values, grad) - delta)).astype(BF16)
                return score_grad, mm(score_grad, query), mm(probs.astype(BF16), grad)

            score_grad, dk, dv = back(kp_ref[...], vp_ref[...], key_at < limit)
            dq_t = mm(keys_t, score_grad)
            if part == 0 and head == 0:
                dkp_acc[...] = dk
                dvp_acc[...] = dv
            else:
                dkp_acc[...] += dk
                dvp_acc[...] += dv
            if part == 1:
                score_grad, dk, dv = back(kc_ref[...], vc_ref[...], cont_place <= col_place)
                dq_t = dq_t + mm(later_t, score_grad)
                if head == 0:
                    dkc_acc[...] = dk
                    dvc_acc[...] = dv
                else:
                    dkc_acc[...] += dk
                    dvc_acc[...] += dv
            turned.append(dq_t)
        both = jnp.where(sub < HEAD_DIM, turned[0], turned[1]) * (1.0 / math.sqrt(HEAD_DIM))
        dq_ref[rows, :] = jnp.transpose(both).astype(BF16)
    for offset in range(group):
        start = pl.multiple_of(scal[offset] * P_DEV, P_DEV)
        pieces[offset][0] = dkp_acc[pl.ds(start, P_DEV), :].astype(BF16)
        pieces[offset][1] = dvp_acc[pl.ds(start, P_DEV), :].astype(BF16)
    own_ref[0] = dkc_acc[:P_DEV, :]
    own_ref[1] = dvc_acc[:P_DEV, :]
    other_ref[0] = dkc_acc[P_DEV:, :].astype(BF16)
    other_ref[1] = dvc_acc[P_DEV:, :].astype(BF16)


def attention_back(scal, q, kp, vp, kc, vc, do, o32, lse, group, waits):
    prompt = kp.shape[0]
    column = lambda rows: pl.BlockSpec((rows, LANES), lambda p: (0, p))
    double = pl.BlockSpec((2, P_DEV, LANES), lambda p: (0, 0, p))
    flops = 10 * 2 * HEADS * P_DEV * (2 * prompt + 2 * P_DEV) * LANES
    return pl.pallas_call(
        without(partial(attention_back_kernel, group), 9, len(waits)),
        out_shape=(
            shape_of((TOK_DEV, D), BF16),
            *[shape_of((2, P_DEV, D), BF16)] * group,
            shape_of((2, P_DEV, D), F32),
            shape_of((2, P_DEV, D), BF16),
        ),
        grid=(PAIRS,),
        in_specs=[pl.BlockSpec(memory_space=pltpu.SMEM)]
        + [
            column(n)
            for n in (TOK_DEV, prompt, prompt, 2 * P_DEV, 2 * P_DEV, TOK_DEV, TOK_DEV, TOK_DEV)
        ]
        + [HELD] * len(waits),
        out_specs=(column(TOK_DEV), *[double] * group, double, double),
        scratch_shapes=[
            pltpu.VMEM((prompt, LANES), F32),
            pltpu.VMEM((prompt, LANES), F32),
            pltpu.VMEM((2 * P_DEV, LANES), F32),
            pltpu.VMEM((2 * P_DEV, LANES), F32),
        ],
        compiler_params=params(),
        cost_estimate=estimate("attention_backward", flops, 20 * TOK_DEV * D * 2),
        name="attention_backward",
    )(scal, q, kp, vp, kc, vc, do, o32, lse, *waits)


def columns(values):
    lane = lax.broadcasted_iota(jnp.int32, (1, LANES), 1)
    packed = None
    for at, value in values.items():
        term = jnp.where(lane == at, value, 0.0)
        packed = term if packed is None else packed + term
    return packed


def routing_kernel(group, scal, tok, o32, *rest):
    shards = rest[:group]
    gain, mixers, vectors, previous, routes = rest[group : group + 5]
    w_out, res_out, base_out, blk_out, info_out, low_out = rest[group + 5 :]
    rows = D // group
    for offset in range(group):
        start = pl.multiple_of(scal[offset] * rows, rows)
        w_out[pl.ds(start, rows), :] = shards[offset][...]
    low = o32[...].astype(BF16)
    low_out[...] = low
    res = tok[...].astype(F32) + mm(low, w_out[...])
    res_out[...] = res
    scale = lax.rsqrt(jnp.mean(res * res, axis=-1, keepdims=True) + NORM_EPS)
    hidden = res * scale * gain[...]
    hidden_low = hidden.astype(BF16)
    blk_out[:TOK_DEV, :] = hidden_low
    lane = lax.broadcasted_iota(jnp.int32, (1, LANES), 1)
    dots = mm(hidden_low, mixers[...])
    logits = jnp.where(lane < IDS, dots + previous[...], MASKED)
    weights = jnp.exp(logits - jnp.max(logits, axis=1, keepdims=True))
    chances = weights / jnp.sum(weights, axis=1, keepdims=True)
    first, second = routes[:, 0:1], routes[:, 1:2]
    chosen0 = jnp.sum(jnp.where(lane == first, chances, 0.0), axis=1, keepdims=True)
    chosen1 = jnp.sum(jnp.where(lane == second, chances, 0.0), axis=1, keepdims=True)
    both = chosen0 + chosen1
    gate0, gate1 = chosen0 / both, chosen1 / both

    def gate_of(ident):
        return jnp.where(first == ident, gate0, 0.0) + jnp.where(second == ident, gate1, 0.0)

    info = {12: gate0, 13: gate1, 21: both}
    hidden_part = gate_of(EXPERTS + 1)
    base = res
    for member in range(2):
        left = dots[:, IDS + 2 * member : IDS + 2 * member + 1]
        right = dots[:, IDS + 2 * member + 1 : IDS + 2 * member + 2]
        top = jnp.maximum(left, right)
        left, right = jnp.exp(left - top), jnp.exp(right - top)
        alpha0, alpha1 = left / (left + right), right / (left + right)
        gate = gate_of(EXPERTS + 2 + member)
        hidden_part = hidden_part + gate * alpha0
        base = base + (gate * alpha1) * vectors[member : member + 1, :]
        info[15 + member] = gate * alpha1
        info[17 + 2 * member] = alpha0
        info[18 + 2 * member] = alpha1
        info[22 + member] = gate
    info[14] = hidden_part
    base_out[...] = base + hidden_part * hidden
    info_out[...] = jnp.where(lane < IDS, chances, columns(info))
    gates = jnp.where(lane == first, gate0, 0.0) + jnp.where(lane == second, gate1, 0.0)
    turned = jnp.transpose(gates)[:EXPERTS, :]
    high = turned.astype(BF16).astype(F32)
    ext = jnp.concatenate([high, turned - high], axis=0).astype(BF16)
    blk_out[TOK_DEV:, :TOK_DEV] = ext
    blk_out[TOK_DEV:, TOK_DEV:] = jnp.zeros((EXT, D - TOK_DEV), BF16)


def fill_rows(hidden, grads, experts, slots, gates, chooser, scales):
    slot = lax.broadcasted_iota(jnp.int32, (CAP, 1), 0).astype(F32)
    slots[...] = grads[TOK_DEV:, :TOK_DEV].astype(F32)
    pair = hidden[TOK_DEV:, :TOK_DEV].astype(F32)
    gates[...] = pair[:EXPERTS, :] + pair[EXPERTS:, :]
    for at, expert in enumerate(experts):
        picked = slots[pl.ds(expert, 1), :] == slot
        span = pl.ds(at * CAP, CAP)
        chooser[span, :] = jnp.where(picked, 1.0, 0.0).astype(BF16)
        scales[span, :] = jnp.sum(
            jnp.where(picked, gates[pl.ds(expert, 1), :], 0.0), axis=1, keepdims=True
        )
    x = mm(chooser[...], hidden[:TOK_DEV, :]).astype(BF16)
    s = (mm(chooser[...], grads[:TOK_DEV, :]) * scales[...]).astype(BF16)
    return x, s


def row_scratch(experts):
    return (
        pltpu.VMEM((EXT, TOK_DEV), F32),
        pltpu.VMEM((EXPERTS, TOK_DEV), F32),
        pltpu.VMEM((experts * CAP, TOK_DEV), BF16),
        pltpu.VMEM((experts * CAP, 1), F32),
    )


def near_rows_kernel(group, per, share, scal, *rest):
    hidden, grads = rest[:group], rest[group : 2 * group]
    x_out, s_out = rest[2 * group : 2 * group + 2]
    experts = [(scal[0] * per + member) // share for member in range(per)]
    for at in range(group):
        x, s = fill_rows(hidden[at], grads[at], experts, *rest[2 * group + 2 :])
        for member in range(per):
            part = slice(member * CAP, (member + 1) * CAP)
            x_out[member, at * CAP : (at + 1) * CAP, :] = x[part]
            s_out[member, at * CAP : (at + 1) * CAP, :] = s[part]


def near_rows(scal, hidden, grads, group, per, share, waits):
    dims = (per, group * CAP, D)
    return whole_call(
        partial(near_rows_kernel, group, per, share),
        "near_rows",
        scal,
        [*hidden, *grads],
        [shape_of(dims, BF16), shape_of(dims, BF16)],
        4 * group * per * CAP * TOK_DEV * D,
        row_scratch(per),
        waits,
    )


def column_rows_kernel(many, *refs):
    x_out, s_out = refs[-6:-4]
    for at in range(many):

        @pl.when(pl.program_id(0) == at)
        def _():
            x, s = fill_rows(refs[at], refs[many + at], range(EXPERTS), *refs[-4:])
            x_out[...] = x.reshape(1, EXPERTS, CAP, D)
            s_out[...] = s.reshape(1, EXPERTS, CAP, D)


def column_rows(hidden, grads, first, count, stacks, waits):
    many = len(hidden)
    dims = (count, EXPERTS, CAP, D)
    block = pl.BlockSpec((1, *dims[1:]), lambda i: (first + i, 0, 0, 0))
    token = pl.BlockSpec((BLOCK, D), lambda i: (0, 0))
    return pl.pallas_call(
        partial(column_rows_kernel, many),
        out_shape=(shape_of(dims, BF16), shape_of(dims, BF16)),
        grid=(many,),
        in_specs=[token] * (2 * many) + [HELD] * (len(stacks) + len(waits)),
        out_specs=(block, block),
        scratch_shapes=list(row_scratch(EXPERTS)),
        input_output_aliases={2 * many + n: n for n in range(len(stacks))},
        compiler_params=params(),
        cost_estimate=estimate("column_rows",
            4 * many * EXPERTS * CAP * TOK_DEV * D, 4 * many * (BLOCK + EXPERTS * CAP) * D
        ),
        name="column_rows",
    )(*hidden, *grads, *stacks, *waits)


def sigmoid(values):
    return 0.5 * jnp.tanh(0.5 * values) + 0.5


def add_low(left, right):
    return (left.astype(F32) + right.astype(F32)).astype(BF16)


def expert_terms(act_a, act_b, hidden_grad):
    sig = sigmoid(act_a)
    silu = act_a * sig
    hidden = (silu * act_b).astype(BF16)
    grad_a = (hidden_grad * act_b * (sig + silu * (1.0 - sig))).astype(BF16)
    grad_b = (hidden_grad * silu).astype(BF16)
    return hidden, grad_a, grad_b


def expert_kernel(group, offsets, x_ref, s_ref, wg, wu, wd, *rest):
    outs, out_acc, in_acc = rest[:group], rest[group], rest[group + 1]
    step = pl.program_id(0)
    rows = x_ref.shape[1]
    chunk = min(rows, 512)
    for start in range(0, rows, chunk):
        span = pl.ds(start, chunk)
        x = x_ref[0, span, :]
        hidden, grad_a, grad_b = expert_terms(
            mm(x, wg[...]), mm(x, wu[...]), mm_nt(s_ref[0, span, :], wd[...])
        )
        out = mm(hidden, wd[...])
        back = mm_nt(grad_a, wg[...]) + mm_nt(grad_b, wu[...])

        @pl.when(step == 0)
        def _():
            out_acc[span, :] = out
            in_acc[span, :] = back

        @pl.when(step > 0)
        def _():
            out_acc[span, :] += out
            in_acc[span, :] += back

    @pl.when(step == pl.num_programs(0) - 1)
    def _():
        for at in range(group):
            outs[offsets[at]][0] = out_acc[at * CAP : (at + 1) * CAP, :].astype(BF16)
            outs[offsets[at]][1] = in_acc[at * CAP : (at + 1) * CAP, :].astype(BF16)


def local_expert(x, s, gate_w, up_w, down_w, member, offsets, group, per, waits):
    width = gate_w.shape[1] // per
    tile = min(512, width)
    steps = width // tile
    rows = group * CAP
    side = pl.BlockSpec((1, rows, D), lambda t: (member, 0, 0))
    wide = pl.BlockSpec((D, tile), lambda t: (0, member * steps + t))
    tall = pl.BlockSpec((tile, D), lambda t: (member * steps + t, 0))
    piece = pl.BlockSpec((2, CAP, D), lambda t: (0, 0, 0))
    return pl.pallas_call(
        without(partial(expert_kernel, group, offsets), 5, len(waits)),
        out_shape=tuple([shape_of((2, CAP, D), BF16)] * group),
        grid=(steps,),
        in_specs=[side, side, wide, wide, tall] + [HELD] * len(waits),
        out_specs=tuple([piece] * group),
        scratch_shapes=[pltpu.VMEM((rows, D), F32), pltpu.VMEM((rows, D), F32)],
        compiler_params=params(),
        cost_estimate=estimate("local_expert", 12 * rows * D * width, 6 * D * width + 8 * rows * D),
        name="local_expert",
    )(x, s, gate_w, up_w, down_w, *waits)


def pack_kernel(at_ref, wg, wu, wd, out):
    out[0, 0] = jnp.transpose(wg[...])
    out[0, 1] = jnp.transpose(wu[...])
    out[0, 2] = wd[...]


def pack_weights(at, weights, member, per, count, waits):
    tile = weights[0].shape[1] // per // count
    wide = pl.BlockSpec((D, tile), lambda m, ref: (0, ref[0] + member * count))
    tall = pl.BlockSpec((tile, D), lambda m, ref: (ref[0] + member * count, 0))
    return pl.pallas_call(
        without(pack_kernel, 4, len(waits)),
        out_shape=shape_of((1, 3, tile, D), BF16),
        grid_spec=pltpu.PrefetchScalarGridSpec(
            num_scalar_prefetch=1,
            grid=(1,),
            in_specs=[wide, wide, tall] + [HELD] * len(waits),
            out_specs=pl.BlockSpec((1, 3, tile, D), lambda m, ref: (0, 0, 0, 0)),
        ),
        compiler_params=params(),
        cost_estimate=estimate("pack_weights", 0, 12 * tile * D),
        name="pack_weights",
    )(at, *weights, *waits)


def slice_kernel(many, experts, x_ref, s_ref, *rest):
    weights, outs = rest[:many], rest[many:]
    for at in range(many):

        @pl.when(pl.program_id(0) == at)
        def _():
            rows = x_ref.shape[0] * x_ref.shape[2]
            x, s = x_ref[...].reshape(rows, D), s_ref[...].reshape(rows, D)
            gate_w, up_w, down_w = (weights[at][0, n] for n in range(3))
            act_a, act_b = mm_nt(gate_w, x), mm_nt(up_w, x)
            hidden, grad_a, grad_b = expert_terms(act_a, act_b, mm_nt(down_w, s))
            outs[at][0] = mm(grad_a, x).astype(BF16)
            outs[at][1] = mm(grad_b, x).astype(BF16)
            outs[at][2] = mm(hidden, s).astype(BF16)


def weight_slices(experts, stacks, packed, waits):
    count, tile, many = stacks[0].shape[0], packed[0].shape[2], len(packed)
    side = pl.BlockSpec((count, 1, CAP, D), lambda t, ref: (0, ref[t], 0, 0))
    held = pl.BlockSpec((1, 3, tile, D), lambda t, ref: (0, 0, 0, 0))
    out = pl.BlockSpec((3, tile, D), lambda t, ref: (0, 0, 0))
    rows = count * CAP
    return pl.pallas_call(
        without(partial(slice_kernel, many), 3 + many, len(waits)),
        out_shape=tuple([shape_of((3, tile, D), BF16)] * many),
        grid_spec=pltpu.PrefetchScalarGridSpec(
            num_scalar_prefetch=1,
            grid=(many,),
            in_specs=[side, side] + [held] * many + [HELD] * len(waits),
            out_specs=tuple([out] * many),
        ),
        compiler_params=params(),
        cost_estimate=estimate("weight_slices", 12 * many * rows * D * tile, many * (4 * rows + 12 * tile) * D),
        name="weight_slices",
    )(experts, *stacks, *packed, *waits)


def place_kernel(held, at_ref, piece, *rest):
    gate_out, up_out, down_out = rest[held:]
    gate_out[...] = jnp.transpose(piece[0].astype(F32))
    up_out[...] = jnp.transpose(piece[1].astype(F32))
    down_out[...] = piece[2].astype(F32)


def place_slice(at, piece, held, units):
    tile = piece.shape[1]
    wide = pl.BlockSpec((D, tile), lambda t, ref: (0, ref[0]))
    tall = pl.BlockSpec((tile, D), lambda t, ref: (ref[0], 0))
    return pl.pallas_call(
        partial(place_kernel, len(held)),
        out_shape=(shape_of((D, units), F32), shape_of((D, units), F32), shape_of((units, D), F32)),
        grid_spec=pltpu.PrefetchScalarGridSpec(
            num_scalar_prefetch=1,
            grid=(1,),
            in_specs=[pl.BlockSpec((3, tile, D), lambda t, ref: (0, 0, 0))]
            + [HELD] * len(held),
            out_specs=(wide, wide, tall),
        ),
        input_output_aliases={2 + n: n for n in range(len(held))},
        compiler_params=params(),
        cost_estimate=estimate("place_slice", 0, 18 * D * tile),
        name="place_slice",
    )(at, piece, *held)


def combine_kernel(group, per, share, scal, *refs):
    pieces = refs[: group * per]
    (base, cot, blk, info_ref, slots, routes, res_ref, gain, vectors, mixers_t, resid_t, prev, w_out) = refs[
        group * per : group * per + 13
    ]
    layer_out, grad_out, mix_out, mixed_out, prev_out, small_out = refs[group * per + 13 :]
    info = info_ref[...]
    first, second = routes[:, 0:1], routes[:, 1:2]
    lane = lax.broadcasted_iota(jnp.int32, (1, LANES), 1)
    slot_lane = lane.astype(F32)
    taken = slots[...]
    out0 = out1 = back = None
    for offset in range(group):
        for member in range(per):
            expert = (scal[offset] * per + member) // share
            column = jnp.sum(jnp.where(lane == expert, taken, 0.0), axis=1, keepdims=True)
            chooser = column == slot_lane
            piece = pieces[offset * per + member]
            pick0 = jnp.where(chooser & (first == expert), 1.0, 0.0).astype(BF16)
            pick1 = jnp.where(chooser & (second == expert), 1.0, 0.0).astype(BF16)
            add0, add1 = mm(pick0, piece[0]), mm(pick1, piece[0])
            add2 = mm(pick0 + pick1, piece[1])
            out0 = add0 if out0 is None else out0 + add0
            out1 = add1 if out1 is None else out1 + add1
            back = add2 if back is None else back + add2
    get = lambda at: info[:, at : at + 1]
    gate0, gate1, hidden_part, both = get(12), get(13), get(14), get(21)
    layer_out[...] = base[...] + gate0 * out0 + gate1 * out1
    grad = cot[...].astype(F32)
    res = res_ref[...]
    scale = lax.rsqrt(jnp.mean(res * res, axis=-1, keepdims=True) + NORM_EPS)
    unit = res * scale
    total = lambda values: jnp.sum(values, axis=1, keepdims=True)
    dot_hidden = total(grad * (unit * gain[...]))
    dot_vector = [total(grad * vectors[k : k + 1, :]) for k in range(2)]

    def gate_grad(route, out):
        value = total(grad * out) + jnp.where(route == EXPERTS + 1, dot_hidden, 0.0)
        for k in range(2):
            const = get(17 + 2 * k) * dot_hidden + get(18 + 2 * k) * dot_vector[k]
            value = value + jnp.where(route == EXPERTS + 2 + k, const, 0.0)
        return value

    dgate0, dgate1 = gate_grad(first, out0), gate_grad(second, out1)
    mean = gate0 * dgate0 + gate1 * dgate1
    dchance = (
        jnp.where(lane == first, dgate0 - mean, 0.0) + jnp.where(lane == second, dgate1 - mean, 0.0)
    ) / both
    chances = jnp.where(lane < IDS, info, 0.0)
    logits_grad = chances * (dchance - total(chances * dchance))
    extra = {16: get(15), 17: get(16)}
    for k in range(2):
        alpha0, alpha1, gate = get(17 + 2 * k), get(18 + 2 * k), get(22 + k)
        d0, d1 = gate * dot_hidden, gate * dot_vector[k]
        inner = alpha0 * d0 + alpha1 * d1
        extra[IDS + 2 * k] = alpha0 * (d0 - inner)
        extra[IDS + 2 * k + 1] = alpha1 * (d1 - inner)
    packed = logits_grad + columns(extra)
    high, low = split(packed)
    prev_out[...] = mm(high, resid_t[...]) + mm(low, resid_t[...])
    hidden_total = (
        back + hidden_part * grad + mm(high, mixers_t[...]) + mm(low, mixers_t[...])
    )
    turned = jnp.transpose(packed)[:32, :]
    t_high, t_low = split(turned)
    hidden_low = blk[:TOK_DEV, :]
    by_hidden = mm(t_high, hidden_low) + mm(t_low, hidden_low)
    by_grad = mm(t_high, cot[...]) + mm(t_low, cot[...])
    prev_high, prev_low = split(prev[...])
    by_prev = mm(t_high, prev_high) + mm(t_high, prev_low) + mm(t_low, prev_high)
    gain_grad = jnp.sum(hidden_total * unit, axis=0, keepdims=True)
    sub = lax.broadcasted_iota(jnp.int32, (8, 1), 0)
    small_out[:16, :] = by_hidden[:16, :]
    small_out[16:24, :] = jnp.where(sub == 2, gain_grad, by_grad[16:24, :])
    small_out[24:40, :] = jnp.zeros((16, D), F32)
    small_out[24:40, :LANES] = by_prev[:16, :]
    u = gain[...] * hidden_total
    inner = jnp.mean(res * u, axis=1, keepdims=True)
    residual_grad = grad + scale * u - res * (scale * scale * scale * inner)
    grad_out[...] = residual_grad
    mix = residual_grad.astype(BF16)
    mix_out[...] = mix
    mixed_out[...] = mm_nt(mix, w_out[...]).astype(BF16)


def finish_kernel(prompt_terms, scal, dq, own, received, *rest):
    terms = rest[:prompt_terms]
    weights, tok, gain, res_grad = rest[prompt_terms : prompt_terms + 4]
    low_out, grad_out, small_out = rest[prompt_terms + 4 :]
    low_out[:, :D] = dq[...]
    for half in range(2):
        columns_at = slice((half + 1) * D, (half + 2) * D)
        prompt = terms[0][half].astype(F32)
        for term in terms[1:]:
            prompt = prompt + term[half].astype(F32)
        low_out[:P_DEV, columns_at] = prompt.astype(BF16)
        low_out[P_DEV:, columns_at] = (own[half] + received[half].astype(F32)).astype(BF16)
    normed_grad = mm_nt(low_out[...], weights[...])
    x = tok[...].astype(F32)
    scale = lax.rsqrt(jnp.mean(x * x, axis=-1, keepdims=True) + NORM_EPS)
    u = gain[...] * normed_grad
    inner = jnp.mean(x * u, axis=1, keepdims=True)
    grad_out[...] = res_grad[...] + scale * u - x * (scale * scale * scale * inner)
    row = jnp.sum(normed_grad * (x * scale), axis=0, keepdims=True)
    sub = lax.broadcasted_iota(jnp.int32, (8, 1), 0)
    small_out[...] = jnp.where(sub == 0, row, 0.0)


def sum_everywhere(value):
    for axis in ("rep", "grp"):
        count = lax.axis_size(axis)
        bit = 1
        while bit < count:
            pairs = [(source, source ^ bit) for source in range(count)]
            value = value + lax.ppermute(value, axis, pairs)
            bit *= 2
    return value


def sum_replicas(value):
    count = lax.axis_size("rep")
    index = lax.axis_index("rep")
    bits = [1 << n for n in range(count.bit_length() - 1)]
    for bit in bits:
        half = value.shape[1] // 2
        left, right = value[:, :half], value[:, half:]
        upper = (index & bit) != 0
        keep = jnp.where(upper, right, left)
        give = jnp.where(upper, left, right).astype(BF16)
        pairs = [(source, source ^ bit) for source in range(count)]
        value = keep + lax.ppermute(give, "rep", pairs).astype(F32)
    value = value.astype(BF16)
    for bit in reversed(bits):
        pairs = [(source, source ^ bit) for source in range(count)]
        other = lax.ppermute(value, "rep", pairs)
        upper = (index & bit) != 0
        value = jnp.concatenate(
            [jnp.where(upper, other, value), jnp.where(upper, value, other)], axis=1
        )
    return value.astype(F32)


def body(
    tokens,
    prev_logits,
    routes,
    branch_points,
    cotangent,
    attn_gain,
    qkv_weight,
    out_weight,
    ffn_gain,
    router_weight,
    resid_weight,
    const_weight,
    const_vector,
    gate_weight,
    up_weight,
    down_weight,
):
    group, count = lax.axis_size("grp"), lax.axis_size("rep")
    index, replica = lax.axis_index("grp"), lax.axis_index("rep")
    per, share = max(1, EXPERTS // group), max(1, group // EXPERTS)
    prompt = P_DEV * group
    spread = group * count <= 32
    tok, cot, route_rows, prev = tokens[0], cotangent[0], routes[0], prev_logits[0]
    follow = lax.dynamic_index_in_dim(branch_points[0], index // 2, keepdims=True)
    scal = jnp.concatenate(
        [
            index ^ jnp.arange(group, dtype=jnp.int32),
            follow.astype(jnp.int32),
            (index % 2)[None].astype(jnp.int32),
        ]
    )

    shards = gather_group(qkv_weight, 1)
    weights = (gate_weight, up_weight, down_weight)
    mine = replica.astype(jnp.int32)[None]
    early = []
    if spread:
        early = [pack_weights(mine, weights, 0, per, count, ())]
    (
        prompt_rows,
        grad_block,
        slots,
        route_lanes,
        prev_lanes,
        previous,
        mixers,
        mixers_t,
        resid_t,
        vectors,
    ) = prepare(
        route_rows,
        prev,
        cot,
        router_weight,
        resid_weight,
        const_weight,
        const_vector,
        tok,
        early,
    )
    prompts = gather_group(prompt_rows, 2)
    for offset in range(0, group, 2):
        prompts[offset + 1] = xor_permute(prompts[offset] if offset else tok, 1)
    gain_one = attn_gain.astype(F32)[None]
    gain_two = ffn_gain.astype(F32)[None]

    offsets = [o for o in range(0, group, 2)] + [o for o in range(1, group, 2)]

    def group_blocks(block):
        held = gather_group(block, 2)
        own = [held[o] for o in range(0, group, 2)]
        return own + [xor_permute(piece, 1) for piece in own]

    def all_blocks(block):
        result, forth, back = [[block]], block, block
        for step in range(1, count // 2 + 1):
            forth = ring_permute(forth, 1)
            result.append([forth])
            if step < count - step:
                back = ring_permute(back, -1)
                result[-1].append(back)
        return result

    grad_far = all_blocks(grad_block) if spread else [[grad_block]]
    hops = len(grad_far) - 1

    def hop_of(blocks, at):
        return blocks[at] if 0 < at <= hops else []

    q, kp, vp, kc, vc, w_qkv, normed, later_block, later_shard, *early = whole_call(
        partial(projection_kernel, group),
        "projections",
        scal,
        [gain_one, tok]
        + [prompts[o] for o in range(1, group)]
        + [shards[o] for o in range(group)]
        + [grad_block, out_weight, *early],
        [
            shape_of((TOK_DEV, D), BF16),
            shape_of((prompt, D), BF16),
            shape_of((prompt, D), BF16),
            shape_of((2 * P_DEV, D), BF16),
            shape_of((2 * P_DEV, D), BF16),
            shape_of((D, 3 * D), BF16),
            shape_of((TOK_DEV, D), BF16),
            shape_of((BLOCK, D), BF16),
            shape_of((D // group, D), BF16),
            *[shape_of(v.shape, BF16) for v in early],
        ],
        2 * TOK_DEV * D * D + 4 * (prompt + 2 * P_DEV) * D * D,
    )
    out_shards = gather_group(later_shard, 1)
    grad_near = group_blocks(later_block)
    packed = [gather_group(v, 1) for v in early]
    o32, lse = attention(scal, q, kp, vp, kc, vc, group, hop_of(grad_far, 1) if W_FRONT else [])
    w_out, res, base, block, info, mixed_low = whole_call(
        partial(routing_kernel, group),
        "routing",
        scal,
        [tok, o32]
        + [out_shards[o] for o in range(group)]
        + [gain_two, mixers, vectors, previous, route_lanes],
        [
            shape_of((D, D), BF16),
            shape_of((TOK_DEV, D), F32),
            shape_of((TOK_DEV, D), F32),
            shape_of((BLOCK, D), BF16),
            shape_of((TOK_DEV, LANES), F32),
            shape_of((TOK_DEV, D), BF16),
        ],
        2 * TOK_DEV * D * D,
        waits=[*(hop_of(grad_far, 2) if W_FRONT else []), *(grad_near[1:-1] if W_NEAR else [])],
    )

    near = group_blocks(block)
    rings, returned, locals_out = [], {}, []

    def give_back(member):
        for offset in range(group):
            value = locals_out[member][offset]
            returned[offset, member] = xor_permute(value, offset) if offset else value
        return [returned[offset, member] for offset in range(1, group)]

    if not spread:
        local = near_rows(scal, near, grad_near, group, per, share, ())
        locals_out = [
            local_expert(*local, *weights, member, offsets, group, per, ())
            for member in range(per)
        ]
    else:
        forth = back = block
        stacks, done, kept = (), 0, []
        for hop in range(1, hops + 1):
            forth = ring_permute(forth, 1)
            back = ring_permute(back, -1) if hop < count - hop else None
            take, waits = [(block, grad_block)], hop_of(grad_far, 3)
            if hop == 2:
                take, waits = kept, hop_of(grad_far, 4)
            elif hop > 2:
                take, waits = kept if hop == hops else (), locals_out[-1][:1] if locals_out else ()
            kept = [] if hop == 1 or take is kept else kept
            if take:
                stacks = column_rows(
                    [h for h, g in take], [g for h, g in take], done, count, stacks, waits
                )
                done += len(take)
            if hop == 2:
                for member in range(1, per):
                    later = pack_weights(mine, weights, member, per, count, [near[1], *([h for h, g in take] if W_PACK else [])])
                    packed.append(gather_group(later, 1))
            if hop == 3:
                waits = [packed[-1][0], *packed[0].values(), stacks[0]]
                local = near_rows(scal, near, grad_near, group, per, share, waits[:-1])
                locals_out.append(
                    local_expert(*local, *weights, 0, offsets, group, per, ())
                )
            kept = kept + list(zip([v for v in (forth, back) if v is not None], grad_far[hop]))
        stacks = column_rows(
            [h for h, g in kept], [g for h, g in kept], done, count, stacks, ()
        )
        parts = [{} for _ in range(per)]
        last = [v for p in packed for v in p.values()]
        for low in range(group - 2, -1, -2):
            chosen = [(m, o) for m in range(per) for o in (low + 1, low)]
            experts = jnp.stack([(index ^ o) * per + m for m, o in chosen]).astype(jnp.int32)
            outs = weight_slices(experts, stacks, [packed[m][o] for m, o in chosen], last)
            for m in range(per):
                parts[m][low] = add_low(outs[2 * m + 1], xor_permute(outs[2 * m], 1))
            last = [outs[0]]
            if low:
                last += [parts[0][low]]
                last += give_back(0) if W_SLICE else []
        for member, part in enumerate(parts):
            bit = 2
            while bit < group:
                for offset in sorted(part, reverse=True):
                    if offset & bit:
                        value = part.pop(offset)
                        if rings:
                            value, rings[-1][0] = lax.optimization_barrier((value, rings[-1][0]))
                        value = xor_permute(value, bit)
                        if rings:
                            waits = [last[0], rings[0][0]] if W_LOCAL else []
                            outs = local_expert(
                                *local, *weights, member, offsets, group, per, waits
                            )
                            if W_LOCAL:
                                value, *outs = lax.optimization_barrier((value, *outs))
                            locals_out.append(outs)
                            give_back(member)
                        part[offset ^ bit] = add_low(part[offset ^ bit], value)
                bit *= 2
            rings.append([part[0]])
    for member in range(per):
        if (0, member) not in returned:
            give_back(member)
    placed = ()
    units = gate_weight.shape[1]
    spot = jnp.where(replica % 2 == 0, replica // 2, count - 1 - replica // 2)

    def advance(step):
        nonlocal placed
        for member, ring in enumerate(rings):
            toward = 1 - 2 * (member % 2)
            if step < count:
                ring.append(ring_permute(ring[-1], toward))
            source = (spot - toward * (step - 1)) % count
            source = jnp.where(source < count // 2, 2 * source, 2 * (count - 1 - source) + 1)
            at = source.astype(jnp.int32)[None] + member * count
            placed = place_slice(at, ring[step - 1], placed, units)
            if step < count and W_BACK:
                ring[step], *placed = lax.optimization_barrier((ring[step], *placed))

    def advance_to(*steps):
        for step in steps:
            if spread:
                advance(step)

    def arrived(*steps):
        return [ring[step] for ring, step in zip(rings, steps) if step >= 0]

    advance_to(1, 2, 3)
    layer_out, res_grad, mix_grad, mixed_grad, prev_grad, small = whole_call(
        partial(combine_kernel, group, per, share),
        "combine",
        scal,
        [returned[o, m] for o in range(group) for m in range(per)]
        + [
            base,
            cot,
            block,
            info,
            slots,
            route_lanes,
            res,
            gain_two,
            vectors,
            mixers_t,
            resid_t,
            prev_lanes,
            w_out,
        ],
        [
            shape_of((TOK_DEV, D), F32),
            shape_of((TOK_DEV, D), F32),
            shape_of((TOK_DEV, D), BF16),
            shape_of((TOK_DEV, D), BF16),
            shape_of((TOK_DEV, LANES), F32),
            shape_of((SMALL_ROWS, D), F32),
        ],
        6 * TOK_DEV * group * per * CAP * D + 2 * TOK_DEV * D * D,
        waits=arrived(1, 0) if W_RING else (),
    )

    back = attention_back(
        scal, q, kp, vp, kc, vc, mixed_grad, o32, lse, group, arrived(2, 1) if W_RING else []
    )
    dq, pieces, later_own, later_other = back[0], list(back[1 : 1 + group]), back[-2], back[-1]
    if W_KEYS and spread:
        tied = lax.optimization_barrier((later_other, *pieces[1:], rings[0][3], rings[1][2]))
        later_other, rings[0][3], rings[1][2] = tied[0], tied[-2], tied[-1]
        pieces = [pieces[0], *tied[1:-2]]
    advance_to(4, 5)
    later_in = xor_permute(later_other, 1)
    held = {o: [pieces[o]] for o in range(group)}
    bit = 1
    while bit < group:
        for offset in sorted(held):
            if offset & bit:
                terms = held.pop(offset)
                value = terms[0]
                if len(terms) > 1:
                    value = sum(t.astype(F32) for t in terms).astype(BF16)
                held[offset ^ bit].append(xor_permute(value, bit))
        bit *= 2
    terms = held[0]
    qkv_low, input_grad, small_two = whole_call(
        partial(finish_kernel, len(terms)),
        "finish",
        scal,
        [dq, later_own, later_in] + terms + [w_qkv, tok, gain_one, res_grad],
        [
            shape_of((TOK_DEV, 3 * D), BF16),
            shape_of((TOK_DEV, D), F32),
            shape_of((8, D), F32),
        ],
        6 * TOK_DEV * D * D,
        waits=(arrived(4, 3) if W_KEYS else arrived(3, 2)) if W_RING else (),
    )
    full = jnp.concatenate([mm_tn(normed, qkv_low), mm_tn(mixed_low, mix_grad)], axis=1)
    rows = D // group
    held = {
        o: lax.dynamic_slice_in_dim(full, (index ^ o) * rows, rows, axis=0) for o in range(group)
    }
    bit, at = 1, 5
    while bit < group:
        for offset in sorted(held):
            if offset & bit:
                value = xor_permute(held.pop(offset).astype(BF16), bit)
                if W_DENSE and spread and offset == bit:
                    value, rings[0][at], rings[1][at - 1] = lax.optimization_barrier(
                        (value, rings[0][at], rings[1][at - 1])
                    )
                    at += 1
                    advance_to(at)
                held[offset ^ bit] = held[offset ^ bit] + value.astype(F32)
        bit *= 2
    if SC_DENSE:
        dense = lax.psum(held[0].astype(BF16), "rep").astype(F32)
    else:
        dense = sum_replicas(held[0])
    small = jnp.concatenate([small, small_two], axis=0)
    if W_DENSE and spread:
        advance_to(*range(len(rings[0]), count))
        small, rings[0][6], rings[1][6] = lax.optimization_barrier(
            (small, rings[0][6], rings[1][6])
        )
    small = lax.psum(small, ("rep", "grp")) if SC_SMALL else sum_everywhere(small)

    if spread:
        for step in range(len(rings[0]), count + 1):
            advance(step)
        gate_sum, up_sum, down_sum = placed
    else:
        x, s = local[0][0], local[1][0]
        hidden, grad_a, grad_b = expert_terms(
            mm(x, gate_weight), mm(x, up_weight), mm_nt(s, down_weight)
        )
        sums = (mm_tn(x, grad_a), mm_tn(x, grad_b), mm_tn(hidden, s))
        gate_sum, up_sum, down_sum = [
            lax.psum(part.astype(BF16), "rep").astype(F32) for part in sums
        ]

    gains = jnp.stack([small[SMALL_ROWS], small[18]], axis=0)
    router_grad = jnp.transpose(small[:IDS])
    const_grad = jnp.transpose(small[IDS : IDS + 4].reshape(2, 2, D), (0, 2, 1))
    resid_grad = jnp.transpose(small[24 : 24 + IDS, :IDS])
    return (
        layer_out[None],
        input_grad[None],
        prev_grad[:, :IDS][None],
        gains,
        dense[:, : 3 * D],
        dense[:, 3 * D :],
        router_grad,
        resid_grad,
        const_grad,
        small[16:18],
        gate_sum,
        up_sum,
        down_sum,
    )


def solution(mesh):
    in_specs = (
        P("rep", "grp", None),
        P("rep", "grp", None),
        P("rep", "grp", None),
        P("rep", None),
        P("rep", "grp", None),
        P(),
        P("grp", None),
        P("grp", None),
        P(),
        P(),
        P(),
        P(),
        P(),
        P(None, "grp"),
        P(None, "grp"),
        P("grp", None),
    )
    out_specs = (
        P("rep", "grp", None),
        P("rep", "grp", None),
        P("rep", "grp", None),
        P(),
        P("grp", None),
        P("grp", None),
        P(),
        P(),
        P(),
        P(),
        P(None, "grp"),
        P(None, "grp"),
        P("grp", None),
    )
    return jax.shard_map(body, mesh=mesh, in_specs=in_specs, out_specs=out_specs, check_vma=False)
```

```python
from functools import partial
import math

import jax
import jax.numpy as jnp
import numpy as np
from jax import lax
from jax.experimental import pallas as pl
from jax.experimental.pallas import tpu as pltpu
from jax.sharding import PartitionSpec as P

D = 768
HEADS = 12
HEAD_DIM = 64
EXPERTS = 8
TOP = 2
P_DEV = 256
TOK_DEV = 512
CAP = 128
IDS = EXPERTS + 4
EXT = 16
BLOCK = TOK_DEV + EXT
LANES = 128
PAIRS = D // LANES

NORM_EPS = 1e-06
MASKED = -1e30
HIGHEST = lax.Precision.HIGHEST
F32 = jnp.float32
BF16 = jnp.bfloat16
VMEM_LIMIT = 56 * 2**20
SMALL_ROWS = 40
COST = {"column_rows": 4.0}
W_KEYS = 1
SC_DENSE = 1
W_DENSE = 1
SC_SMALL = 0
W_PACK = 0
W_NEAR = 1
W_FRONT = 1
W_RING = 0
W_LOCAL = 1
W_SLICE = 1
W_BACK = 1


def mm(left, right):
    return jnp.dot(left, right, preferred_element_type=F32)


def mm_nt(left, right):
    return lax.dot_general(left, right, (((1,), (1,)), ((), ())), preferred_element_type=F32)


def mm_tn(left, right):
    return lax.dot_general(left, right, (((0,), (0,)), ((), ())), preferred_element_type=F32)


def split(values):
    high = values.astype(BF16)
    return high, (values - high.astype(F32)).astype(BF16)


def shape_of(dims, dtype):
    return jax.ShapeDtypeStruct(dims, dtype)


def estimate(name, flops, bytes_accessed):
    scale = COST.get(name, 1.0)
    return pl.CostEstimate(
        flops=int(scale * flops), bytes_accessed=int(scale * bytes_accessed), transcendentals=0
    )


def params():
    return pltpu.CompilerParams(vmem_limit_bytes=VMEM_LIMIT)


def without(kernel, first, count):
    if not count:
        return kernel

    def run(*refs):
        return kernel(*refs[:first], *refs[first + count :])

    return run


HELD = pl.BlockSpec(memory_space=pl.ANY)


def whole_call(kernel, name, scalars, arrays, outs, flops, scratch=(), waits=()):
    vmem = pl.BlockSpec(memory_space=pltpu.VMEM)
    moved = sum(a.size * a.dtype.itemsize for a in arrays)
    moved += sum(math.prod(o.shape) * np.dtype(o.dtype).itemsize for o in outs)
    return pl.pallas_call(
        without(kernel, 1 + len(arrays), len(waits)),
        out_shape=tuple(outs),
        in_specs=[pl.BlockSpec(memory_space=pltpu.SMEM)]
        + [vmem] * len(arrays)
        + [HELD] * len(waits),
        out_specs=tuple([vmem] * len(outs)),
        scratch_shapes=list(scratch),
        compiler_params=params(),
        cost_estimate=estimate(name, flops, moved),
        name=name,
    )(scalars, *arrays, *waits)


def xor_permute(value, offset):
    pairs = [(source, source ^ offset) for source in range(lax.axis_size("grp"))]
    return lax.ppermute(value, "grp", pairs)


def ring_permute(value, step):
    count = lax.axis_size("rep")
    order = list(range(0, count, 2)) + list(range(count - 1, 0, -2))
    pairs = [(order[at], order[(at + step) % count]) for at in range(count)]
    return lax.ppermute(value, "rep", pairs)


def gather_group(value, lowest):
    pieces = {0: value}
    bit = lax.axis_size("grp") // 2
    while bit >= lowest:
        for offset in list(pieces):
            pieces[offset | bit] = xor_permute(pieces[offset], bit)
        bit //= 2
    return pieces


def lanes_of(values):
    rows, width = values.shape
    return jnp.concatenate([values, jnp.zeros((rows, LANES - width), values.dtype)], axis=1)


def prepare_kernel(routes, prev, cot, router, resid, const_w, const_v, prompt, *rest):
    prompt_out, block, slots_out, routes_out, prev_out, previous_out, mixers_out, turned_out, resid_out, vectors_out = rest
    prompt_out[...] = prompt[:P_DEV, :]
    lane = lax.broadcasted_iota(jnp.int32, (1, LANES), 1)
    ids = routes[...]
    named = (ids[:, 0:1] == lane) | (ids[:, 1:2] == lane)
    row = lax.broadcasted_iota(jnp.int32, (TOK_DEV, 1), 0)
    col = lax.broadcasted_iota(jnp.int32, (1, TOK_DEV), 1)
    before = jnp.where(col < row, 1.0, 0.0).astype(BF16)
    slots = jnp.where(named, mm(before, jnp.where(named, 1.0, 0.0).astype(BF16)), -1.0)
    slots_out[...] = slots
    block[:TOK_DEV, :] = cot[...]
    block[TOK_DEV:, :TOK_DEV] = jnp.transpose(slots)[:EXT, :].astype(BF16)
    block[TOK_DEV:, TOK_DEV:] = jnp.full((EXT, D - TOK_DEV), -1, BF16)
    routes_out[...] = jnp.where(lane == 0, ids[:, 0:1], jnp.where(lane == 1, ids[:, 1:2], 0))
    wide = lanes_of(prev[...])
    prev_out[...] = wide
    square = jnp.concatenate(
        [lanes_of(resid[...].astype(F32)), jnp.zeros((LANES - IDS, LANES), F32)], axis=0
    )
    turned_resid = jnp.transpose(square).astype(BF16)
    resid_out[...] = turned_resid
    high, rest_of = split(wide)
    low = (wide - high.astype(F32) - rest_of.astype(F32)).astype(BF16)
    resid_low = square.astype(BF16)
    previous_out[...] = mm(high, resid_low) + mm(rest_of, resid_low) + mm(low, resid_low)
    mixers = jnp.concatenate(
        [
            router[...].astype(F32),
            const_w[0].astype(F32),
            const_w[1].astype(F32),
            jnp.zeros((D, LANES - IDS - 4), F32),
        ],
        axis=1,
    )
    mixers_out[...] = mixers.astype(BF16)
    turned_out[...] = jnp.transpose(mixers).astype(BF16)
    vectors_out[...] = jnp.concatenate([const_v[...].astype(F32), jnp.zeros((6, D), F32)], axis=0)


def prepare(routes, prev, cot, router, resid, const_w, const_v, tok, waits):
    vmem = pl.BlockSpec(memory_space=pltpu.VMEM)
    arrays = (routes, prev, cot, router, resid, const_w, const_v, tok)
    outs = (
        shape_of((P_DEV, D), BF16),
        shape_of((BLOCK, D), BF16),
        shape_of((TOK_DEV, LANES), F32),
        shape_of((TOK_DEV, LANES), jnp.int32),
        shape_of((TOK_DEV, LANES), F32),
        shape_of((TOK_DEV, LANES), F32),
        shape_of((D, LANES), BF16),
        shape_of((LANES, D), BF16),
        shape_of((LANES, LANES), BF16),
        shape_of((8, D), F32),
    )
    return pl.pallas_call(
        without(prepare_kernel, len(arrays), len(waits)),
        out_shape=outs,
        in_specs=[vmem] * len(arrays) + [HELD] * len(waits),
        out_specs=tuple([vmem] * len(outs)),
        compiler_params=params(),
        cost_estimate=estimate("prepare", 2 * TOK_DEV * TOK_DEV * LANES, 8 * TOK_DEV * D),
        name="prepare",
    )(*arrays, *waits)


def projection_kernel(group, scal, gain, tok, *rest):
    prompts, shards = rest[: group - 1], rest[group - 1 : 2 * group - 1]
    passed = (len(rest) - 2 * group + 1 - 7) // 2
    q_out, kp_out, vp_out, kc_out, vc_out, w_out, n_out = rest[2 * group - 1 + passed : 2 * group + 6 + passed]
    for at in range(passed):
        rest[2 * group + 6 + passed + at][...] = rest[2 * group - 1 + at][...]
    rows = D // group
    for offset in range(group):
        start = pl.multiple_of(scal[offset] * rows, rows)
        w_out[pl.ds(start, rows), :] = shards[offset][...]

    def normed(values):
        wide = values.astype(F32)
        scale = lax.rsqrt(jnp.mean(wide * wide, axis=-1, keepdims=True) + NORM_EPS)
        return (wide * scale * gain[...]).astype(BF16)

    own = normed(tok[...])
    n_out[...] = own
    q_out[...] = mm(own, w_out[:, :D]).astype(BF16)
    kv = mm(own, w_out[:, D:]).astype(BF16)
    start = pl.multiple_of(scal[0] * P_DEV, P_DEV)
    kp_out[pl.ds(start, P_DEV), :] = kv[:P_DEV, :D]
    vp_out[pl.ds(start, P_DEV), :] = kv[:P_DEV, D:]
    kc_out[:P_DEV, :] = kv[P_DEV:, :D]
    vc_out[:P_DEV, :] = kv[P_DEV:, D:]
    kv = mm(normed(prompts[0][P_DEV:, :]), w_out[:, D:]).astype(BF16)
    kc_out[P_DEV:, :] = kv[:, :D]
    vc_out[P_DEV:, :] = kv[:, D:]
    for offset in range(1, group):
        kv = mm(normed(prompts[offset - 1][:P_DEV, :]), w_out[:, D:]).astype(BF16)
        start = pl.multiple_of(scal[offset] * P_DEV, P_DEV)
        kp_out[pl.ds(start, P_DEV), :] = kv[:, :D]
        vp_out[pl.ds(start, P_DEV), :] = kv[:, D:]


def place_of(local, side):
    half = P_DEV // 2
    return (side + 2 * (local // half)) * half + local % half


def attention_kernel(group, scal, q_ref, kp_ref, vp_ref, kc_ref, vc_ref, o_ref, lse_ref):
    prompt = kp_ref.shape[0]
    index, follow, side = scal[0], scal[group], scal[group + 1]
    lane = lax.broadcasted_iota(jnp.int32, (1, LANES), 1)
    row = lax.broadcasted_iota(jnp.int32, (P_DEV, 1), 0)
    key_at = lax.broadcasted_iota(jnp.int32, (1, prompt), 1)
    cont_at = lax.broadcasted_iota(jnp.int32, (1, 2 * P_DEV), 1)
    cont_place = place_of(cont_at % P_DEV, jnp.where(cont_at < P_DEV, side, 1 - side))
    row_place = place_of(row, side)
    for part in range(2):
        rows = pl.ds(part * P_DEV, P_DEV)
        scaled = q_ref[rows, :] * BF16(1.0 / math.sqrt(HEAD_DIM))
        limit = index * P_DEV + row + 1 if part == 0 else jnp.broadcast_to(follow, (P_DEV, 1))
        mixed, logs = [], []
        for head in range(2):
            masked = jnp.where(lane // HEAD_DIM == head, scaled, BF16(0))
            scores = jnp.where(key_at < limit, mm_nt(masked, kp_ref[...]), MASKED)
            top = jnp.max(scores, axis=1, keepdims=True)
            if part == 1:
                later = jnp.where(cont_place <= row_place, mm_nt(masked, kc_ref[...]), MASKED)
                top = jnp.maximum(top, jnp.max(later, axis=1, keepdims=True))
            weights = jnp.exp(scores - top)
            total = jnp.sum(weights, axis=1, keepdims=True)
            out = mm(weights.astype(BF16), vp_ref[...])
            if part == 1:
                weights = jnp.exp(later - top)
                total = total + jnp.sum(weights, axis=1, keepdims=True)
                out = out + mm(weights.astype(BF16), vc_ref[...])
            mixed.append(out / total)
            logs.append(top + jnp.log(total))
        o_ref[rows, :] = jnp.where(lane < HEAD_DIM, mixed[0], mixed[1])
        lse_ref[rows, :] = jnp.where(lane < HEAD_DIM, logs[0], logs[1])


def attention(scal, q, kp, vp, kc, vc, group, waits):
    prompt = kp.shape[0]
    column = lambda rows: pl.BlockSpec((rows, LANES), lambda p: (0, p))
    flops = 4 * 2 * HEADS * P_DEV * (2 * prompt + 2 * P_DEV) * LANES
    return pl.pallas_call(
        without(partial(attention_kernel, group), 6, len(waits)),
        out_shape=(shape_of((TOK_DEV, D), F32), shape_of((TOK_DEV, D), F32)),
        grid=(PAIRS,),
        in_specs=[pl.BlockSpec(memory_space=pltpu.SMEM)]
        + [column(n) for n in (TOK_DEV, prompt, prompt, 2 * P_DEV, 2 * P_DEV)]
        + [HELD] * len(waits),
        out_specs=(column(TOK_DEV), column(TOK_DEV)),
        compiler_params=params(),
        cost_estimate=estimate("attention_forward", flops, 10 * TOK_DEV * D * 2),
        name="attention_forward",
    )(scal, q, kp, vp, kc, vc, *waits)


def attention_back_kernel(group, scal, q_ref, kp_ref, vp_ref, kc_ref, vc_ref, do_ref, o_ref, lse_ref, *rest):
    prompt = kp_ref.shape[0]
    dq_ref = rest[0]
    pieces = rest[1 : 1 + group]
    own_ref, other_ref, dkp_acc, dvp_acc, dkc_acc, dvc_acc = rest[1 + group :]
    index, follow, side = scal[0], scal[group], scal[group + 1]
    lane = lax.broadcasted_iota(jnp.int32, (1, LANES), 1)
    sub = lax.broadcasted_iota(jnp.int32, (LANES, 1), 0)
    col = lax.broadcasted_iota(jnp.int32, (1, P_DEV), 1)
    key_at = lax.broadcasted_iota(jnp.int32, (prompt, 1), 0)
    cont_at = lax.broadcasted_iota(jnp.int32, (2 * P_DEV, 1), 0)
    cont_place = place_of(cont_at % P_DEV, jnp.where(cont_at < P_DEV, side, 1 - side))
    col_place = place_of(col, side)
    logs = jnp.transpose(lse_ref[...])
    products = jnp.transpose(do_ref[...].astype(F32) * o_ref[...])
    keys_t = jnp.transpose(kp_ref[...])
    later_t = jnp.transpose(kc_ref[...])
    for part in range(2):
        rows = pl.ds(part * P_DEV, P_DEV)
        span = slice(part * P_DEV, (part + 1) * P_DEV)
        scaled = q_ref[rows, :] * BF16(1.0 / math.sqrt(HEAD_DIM))
        grads = do_ref[rows, :]
        limit = index * P_DEV + col + 1 if part == 0 else jnp.broadcast_to(follow, (1, P_DEV))
        turned = []
        for head in range(2):
            mine = lane // HEAD_DIM == head
            query = jnp.where(mine, scaled, BF16(0))
            grad = jnp.where(mine, grads, BF16(0))
            log_row = logs[head * HEAD_DIM : head * HEAD_DIM + 1, span]
            delta = jnp.sum(
                products[head * HEAD_DIM : (head + 1) * HEAD_DIM, span], axis=0, keepdims=True
            )

            def back(keys, values, allowed):
                probs = jnp.exp(jnp.where(allowed, mm_nt(keys, query) - log_row, MASKED))
                score_grad = (probs * (mm_nt(values, grad) - delta)).astype(BF16)
                return score_grad, mm(score_grad, query), mm(probs.astype(BF16), grad)

            score_grad, dk, dv = back(kp_ref[...], vp_ref[...], key_at < limit)
            dq_t = mm(keys_t, score_grad)
            if part == 0 and head == 0:
                dkp_acc[...] = dk
                dvp_acc[...] = dv
            else:
                dkp_acc[...] += dk
                dvp_acc[...] += dv
            if part == 1:
                score_grad, dk, dv = back(kc_ref[...], vc_ref[...], cont_place <= col_place)
                dq_t = dq_t + mm(later_t, score_grad)
                if head == 0:
                    dkc_acc[...] = dk
                    dvc_acc[...] = dv
                else:
                    dkc_acc[...] += dk
                    dvc_acc[...] += dv
            turned.append(dq_t)
        both = jnp.where(sub < HEAD_DIM, turned[0], turned[1]) * (1.0 / math.sqrt(HEAD_DIM))
        dq_ref[rows, :] = jnp.transpose(both).astype(BF16)
    for offset in range(group):
        start = pl.multiple_of(scal[offset] * P_DEV, P_DEV)
        pieces[offset][0] = dkp_acc[pl.ds(start, P_DEV), :].astype(BF16)
        pieces[offset][1] = dvp_acc[pl.ds(start, P_DEV), :].astype(BF16)
    own_ref[0] = dkc_acc[:P_DEV, :]
    own_ref[1] = dvc_acc[:P_DEV, :]
    other_ref[0] = dkc_acc[P_DEV:, :].astype(BF16)
    other_ref[1] = dvc_acc[P_DEV:, :].astype(BF16)


def attention_back(scal, q, kp, vp, kc, vc, do, o32, lse, group, waits):
    prompt = kp.shape[0]
    column = lambda rows: pl.BlockSpec((rows, LANES), lambda p: (0, p))
    double = pl.BlockSpec((2, P_DEV, LANES), lambda p: (0, 0, p))
    flops = 10 * 2 * HEADS * P_DEV * (2 * prompt + 2 * P_DEV) * LANES
    return pl.pallas_call(
        without(partial(attention_back_kernel, group), 9, len(waits)),
        out_shape=(
            shape_of((TOK_DEV, D), BF16),
            *[shape_of((2, P_DEV, D), BF16)] * group,
            shape_of((2, P_DEV, D), F32),
            shape_of((2, P_DEV, D), BF16),
        ),
        grid=(PAIRS,),
        in_specs=[pl.BlockSpec(memory_space=pltpu.SMEM)]
        + [
            column(n)
            for n in (TOK_DEV, prompt, prompt, 2 * P_DEV, 2 * P_DEV, TOK_DEV, TOK_DEV, TOK_DEV)
        ]
        + [HELD] * len(waits),
        out_specs=(column(TOK_DEV), *[double] * group, double, double),
        scratch_shapes=[
            pltpu.VMEM((prompt, LANES), F32),
            pltpu.VMEM((prompt, LANES), F32),
            pltpu.VMEM((2 * P_DEV, LANES), F32),
            pltpu.VMEM((2 * P_DEV, LANES), F32),
        ],
        compiler_params=params(),
        cost_estimate=estimate("attention_backward", flops, 20 * TOK_DEV * D * 2),
        name="attention_backward",
    )(scal, q, kp, vp, kc, vc, do, o32, lse, *waits)


def columns(values):
    lane = lax.broadcasted_iota(jnp.int32, (1, LANES), 1)
    packed = None
    for at, value in values.items():
        term = jnp.where(lane == at, value, 0.0)
        packed = term if packed is None else packed + term
    return packed


def routing_kernel(group, scal, tok, o32, *rest):
    shards = rest[:group]
    gain, mixers, vectors, previous, routes = rest[group : group + 5]
    w_out, res_out, base_out, blk_out, info_out, low_out = rest[group + 5 :]
    rows = D // group
    for offset in range(group):
        start = pl.multiple_of(scal[offset] * rows, rows)
        w_out[pl.ds(start, rows), :] = shards[offset][...]
    low = o32[...].astype(BF16)
    low_out[...] = low
    res = tok[...].astype(F32) + mm(low, w_out[...])
    res_out[...] = res
    scale = lax.rsqrt(jnp.mean(res * res, axis=-1, keepdims=True) + NORM_EPS)
    hidden = res * scale * gain[...]
    hidden_low = hidden.astype(BF16)
    blk_out[:TOK_DEV, :] = hidden_low
    lane = lax.broadcasted_iota(jnp.int32, (1, LANES), 1)
    dots = mm(hidden_low, mixers[...])
    logits = jnp.where(lane < IDS, dots + previous[...], MASKED)
    weights = jnp.exp(logits - jnp.max(logits, axis=1, keepdims=True))
    chances = weights / jnp.sum(weights, axis=1, keepdims=True)
    first, second = routes[:, 0:1], routes[:, 1:2]
    chosen0 = jnp.sum(jnp.where(lane == first, chances, 0.0), axis=1, keepdims=True)
    chosen1 = jnp.sum(jnp.where(lane == second, chances, 0.0), axis=1, keepdims=True)
    both = chosen0 + chosen1
    gate0, gate1 = chosen0 / both, chosen1 / both

    def gate_of(ident):
        return jnp.where(first == ident, gate0, 0.0) + jnp.where(second == ident, gate1, 0.0)

    info = {12: gate0, 13: gate1, 21: both}
    hidden_part = gate_of(EXPERTS + 1)
    base = res
    for member in range(2):
        left = dots[:, IDS + 2 * member : IDS + 2 * member + 1]
        right = dots[:, IDS + 2 * member + 1 : IDS + 2 * member + 2]
        top = jnp.maximum(left, right)
        left, right = jnp.exp(left - top), jnp.exp(right - top)
        alpha0, alpha1 = left / (left + right), right / (left + right)
        gate = gate_of(EXPERTS + 2 + member)
        hidden_part = hidden_part + gate * alpha0
        base = base + (gate * alpha1) * vectors[member : member + 1, :]
        info[15 + member] = gate * alpha1
        info[17 + 2 * member] = alpha0
        info[18 + 2 * member] = alpha1
        info[22 + member] = gate
    info[14] = hidden_part
    base_out[...] = base + hidden_part * hidden
    info_out[...] = jnp.where(lane < IDS, chances, columns(info))
    gates = jnp.where(lane == first, gate0, 0.0) + jnp.where(lane == second, gate1, 0.0)
    turned = jnp.transpose(gates)[:EXPERTS, :]
    high = turned.astype(BF16).astype(F32)
    ext = jnp.concatenate([high, turned - high], axis=0).astype(BF16)
    blk_out[TOK_DEV:, :TOK_DEV] = ext
    blk_out[TOK_DEV:, TOK_DEV:] = jnp.zeros((EXT, D - TOK_DEV), BF16)


def fill_rows(hidden, grads, experts, slots, gates, chooser, scales):
    slot = lax.broadcasted_iota(jnp.int32, (CAP, 1), 0).astype(F32)
    slots[...] = grads[TOK_DEV:, :TOK_DEV].astype(F32)
    pair = hidden[TOK_DEV:, :TOK_DEV].astype(F32)
    gates[...] = pair[:EXPERTS, :] + pair[EXPERTS:, :]
    for at, expert in enumerate(experts):
        picked = slots[pl.ds(expert, 1), :] == slot
        span = pl.ds(at * CAP, CAP)
        chooser[span, :] = jnp.where(picked, 1.0, 0.0).astype(BF16)
        scales[span, :] = jnp.sum(
            jnp.where(picked, gates[pl.ds(expert, 1), :], 0.0), axis=1, keepdims=True
        )
    x = mm(chooser[...], hidden[:TOK_DEV, :]).astype(BF16)
    s = (mm(chooser[...], grads[:TOK_DEV, :]) * scales[...]).astype(BF16)
    return x, s


def row_scratch(experts):
    return (
        pltpu.VMEM((EXT, TOK_DEV), F32),
        pltpu.VMEM((EXPERTS, TOK_DEV), F32),
        pltpu.VMEM((experts * CAP, TOK_DEV), BF16),
        pltpu.VMEM((experts * CAP, 1), F32),
    )


def near_rows_kernel(group, per, share, scal, *rest):
    hidden, grads = rest[:group], rest[group : 2 * group]
    x_out, s_out = rest[2 * group : 2 * group + 2]
    experts = [(scal[0] * per + member) // share for member in range(per)]
    for at in range(group):
        x, s = fill_rows(hidden[at], grads[at], experts, *rest[2 * group + 2 :])
        for member in range(per):
            part = slice(member * CAP, (member + 1) * CAP)
            x_out[member, at * CAP : (at + 1) * CAP, :] = x[part]
            s_out[member, at * CAP : (at + 1) * CAP, :] = s[part]


def near_rows(scal, hidden, grads, group, per, share, waits):
    dims = (per, group * CAP, D)
    return whole_call(
        partial(near_rows_kernel, group, per, share),
        "near_rows",
        scal,
        [*hidden, *grads],
        [shape_of(dims, BF16), shape_of(dims, BF16)],
        4 * group * per * CAP * TOK_DEV * D,
        row_scratch(per),
        waits,
    )


def column_rows_kernel(many, *refs):
    x_out, s_out = refs[-6:-4]
    for at in range(many):

        @pl.when(pl.program_id(0) == at)
        def _():
            x, s = fill_rows(refs[at], refs[many + at], range(EXPERTS), *refs[-4:])
            x_out[...] = x.reshape(1, EXPERTS, CAP, D)
            s_out[...] = s.reshape(1, EXPERTS, CAP, D)


def column_rows(hidden, grads, first, count, stacks, waits):
    many = len(hidden)
    dims = (count, EXPERTS, CAP, D)
    block = pl.BlockSpec((1, *dims[1:]), lambda i: (first + i, 0, 0, 0))
    token = pl.BlockSpec((BLOCK, D), lambda i: (0, 0))
    return pl.pallas_call(
        partial(column_rows_kernel, many),
        out_shape=(shape_of(dims, BF16), shape_of(dims, BF16)),
        grid=(many,),
        in_specs=[token] * (2 * many) + [HELD] * (len(stacks) + len(waits)),
        out_specs=(block, block),
        scratch_shapes=list(row_scratch(EXPERTS)),
        input_output_aliases={2 * many + n: n for n in range(len(stacks))},
        compiler_params=params(),
        cost_estimate=estimate("column_rows",
            4 * many * EXPERTS * CAP * TOK_DEV * D, 4 * many * (BLOCK + EXPERTS * CAP) * D
        ),
        name="column_rows",
    )(*hidden, *grads, *stacks, *waits)


def sigmoid(values):
    return 0.5 * jnp.tanh(0.5 * values) + 0.5


def add_low(left, right):
    return (left.astype(F32) + right.astype(F32)).astype(BF16)


def expert_terms(act_a, act_b, hidden_grad):
    sig = sigmoid(act_a)
    silu = act_a * sig
    hidden = (silu * act_b).astype(BF16)
    grad_a = (hidden_grad * act_b * (sig + silu * (1.0 - sig))).astype(BF16)
    grad_b = (hidden_grad * silu).astype(BF16)
    return hidden, grad_a, grad_b


def expert_kernel(group, offsets, x_ref, s_ref, wg, wu, wd, *rest):
    outs, out_acc, in_acc = rest[:group], rest[group], rest[group + 1]
    step = pl.program_id(0)
    rows = x_ref.shape[1]
    chunk = min(rows, 512)
    for start in range(0, rows, chunk):
        span = pl.ds(start, chunk)
        x = x_ref[0, span, :]
        hidden, grad_a, grad_b = expert_terms(
            mm(x, wg[...]), mm(x, wu[...]), mm_nt(s_ref[0, span, :], wd[...])
        )
        out = mm(hidden, wd[...])
        back = mm_nt(grad_a, wg[...]) + mm_nt(grad_b, wu[...])

        @pl.when(step == 0)
        def _():
            out_acc[span, :] = out
            in_acc[span, :] = back

        @pl.when(step > 0)
        def _():
            out_acc[span, :] += out
            in_acc[span, :] += back

    @pl.when(step == pl.num_programs(0) - 1)
    def _():
        for at in range(group):
            outs[offsets[at]][0] = out_acc[at * CAP : (at + 1) * CAP, :].astype(BF16)
            outs[offsets[at]][1] = in_acc[at * CAP : (at + 1) * CAP, :].astype(BF16)


def local_expert(x, s, gate_w, up_w, down_w, member, offsets, group, per, waits):
    width = gate_w.shape[1] // per
    tile = min(512, width)
    steps = width // tile
    rows = group * CAP
    side = pl.BlockSpec((1, rows, D), lambda t: (member, 0, 0))
    wide = pl.BlockSpec((D, tile), lambda t: (0, member * steps + t))
    tall = pl.BlockSpec((tile, D), lambda t: (member * steps + t, 0))
    piece = pl.BlockSpec((2, CAP, D), lambda t: (0, 0, 0))
    return pl.pallas_call(
        without(partial(expert_kernel, group, offsets), 5, len(waits)),
        out_shape=tuple([shape_of((2, CAP, D), BF16)] * group),
        grid=(steps,),
        in_specs=[side, side, wide, wide, tall] + [HELD] * len(waits),
        out_specs=tuple([piece] * group),
        scratch_shapes=[pltpu.VMEM((rows, D), F32), pltpu.VMEM((rows, D), F32)],
        compiler_params=params(),
        cost_estimate=estimate("local_expert", 12 * rows * D * width, 6 * D * width + 8 * rows * D),
        name="local_expert",
    )(x, s, gate_w, up_w, down_w, *waits)


def pack_kernel(at_ref, wg, wu, wd, out):
    out[0, 0] = jnp.transpose(wg[...])
    out[0, 1] = jnp.transpose(wu[...])
    out[0, 2] = wd[...]


def pack_weights(at, weights, member, per, count, waits):
    tile = weights[0].shape[1] // per // count
    wide = pl.BlockSpec((D, tile), lambda m, ref: (0, ref[0] + member * count))
    tall = pl.BlockSpec((tile, D), lambda m, ref: (ref[0] + member * count, 0))
    return pl.pallas_call(
        without(pack_kernel, 4, len(waits)),
        out_shape=shape_of((1, 3, tile, D), BF16),
        grid_spec=pltpu.PrefetchScalarGridSpec(
            num_scalar_prefetch=1,
            grid=(1,),
            in_specs=[wide, wide, tall] + [HELD] * len(waits),
            out_specs=pl.BlockSpec((1, 3, tile, D), lambda m, ref: (0, 0, 0, 0)),
        ),
        compiler_params=params(),
        cost_estimate=estimate("pack_weights", 0, 12 * tile * D),
        name="pack_weights",
    )(at, *weights, *waits)


def slice_kernel(many, experts, x_ref, s_ref, *rest):
    weights, outs = rest[:many], rest[many:]
    for at in range(many):

        @pl.when(pl.program_id(0) == at)
        def _():
            rows = x_ref.shape[0] * x_ref.shape[2]
            x, s = x_ref[...].reshape(rows, D), s_ref[...].reshape(rows, D)
            gate_w, up_w, down_w = (weights[at][0, n] for n in range(3))
            act_a, act_b = mm_nt(gate_w, x), mm_nt(up_w, x)
            hidden, grad_a, grad_b = expert_terms(act_a, act_b, mm_nt(down_w, s))
            outs[at][0] = mm(grad_a, x).astype(BF16)
            outs[at][1] = mm(grad_b, x).astype(BF16)
            outs[at][2] = mm(hidden, s).astype(BF16)


def weight_slices(experts, stacks, packed, waits):
    count, tile, many = stacks[0].shape[0], packed[0].shape[2], len(packed)
    side = pl.BlockSpec((count, 1, CAP, D), lambda t, ref: (0, ref[t], 0, 0))
    held = pl.BlockSpec((1, 3, tile, D), lambda t, ref: (0, 0, 0, 0))
    out = pl.BlockSpec((3, tile, D), lambda t, ref: (0, 0, 0))
    rows = count * CAP
    return pl.pallas_call(
        without(partial(slice_kernel, many), 3 + many, len(waits)),
        out_shape=tuple([shape_of((3, tile, D), BF16)] * many),
        grid_spec=pltpu.PrefetchScalarGridSpec(
            num_scalar_prefetch=1,
            grid=(many,),
            in_specs=[side, side] + [held] * many + [HELD] * len(waits),
            out_specs=tuple([out] * many),
        ),
        compiler_params=params(),
        cost_estimate=estimate("weight_slices", 12 * many * rows * D * tile, many * (4 * rows + 12 * tile) * D),
        name="weight_slices",
    )(experts, *stacks, *packed, *waits)


def place_kernel(held, at_ref, piece, *rest):
    gate_out, up_out, down_out = rest[held:]
    gate_out[...] = jnp.transpose(piece[0].astype(F32))
    up_out[...] = jnp.transpose(piece[1].astype(F32))
    down_out[...] = piece[2].astype(F32)


def place_slice(at, piece, held, units):
    tile = piece.shape[1]
    wide = pl.BlockSpec((D, tile), lambda t, ref: (0, ref[0]))
    tall = pl.BlockSpec((tile, D), lambda t, ref: (ref[0], 0))
    return pl.pallas_call(
        partial(place_kernel, len(held)),
        out_shape=(shape_of((D, units), F32), shape_of((D, units), F32), shape_of((units, D), F32)),
        grid_spec=pltpu.PrefetchScalarGridSpec(
            num_scalar_prefetch=1,
            grid=(1,),
            in_specs=[pl.BlockSpec((3, tile, D), lambda t, ref: (0, 0, 0))]
            + [HELD] * len(held),
            out_specs=(wide, wide, tall),
        ),
        input_output_aliases={2 + n: n for n in range(len(held))},
        compiler_params=params(),
        cost_estimate=estimate("place_slice", 0, 18 * D * tile),
        name="place_slice",
    )(at, piece, *held)


def combine_kernel(group, per, share, scal, *refs):
    pieces = refs[: group * per]
    (base, cot, blk, info_ref, slots, routes, res_ref, gain, vectors, mixers_t, resid_t, prev, w_out) = refs[
        group * per : group * per + 13
    ]
    layer_out, grad_out, mix_out, mixed_out, prev_out, small_out = refs[
        group * per + 13 : group * per + 19
    ]
    out_rows, back_rows, pick0, pick1 = refs[group * per + 19 :]
    info = info_ref[...]
    first, second = routes[:, 0:1], routes[:, 1:2]
    lane = lax.broadcasted_iota(jnp.int32, (1, LANES), 1)
    slot_lane = lane.astype(F32)
    taken = slots[...]
    for offset in range(group):
        for member in range(per):
            expert = (scal[offset] * per + member) // share
            column = jnp.sum(jnp.where(lane == expert, taken, 0.0), axis=1, keepdims=True)
            at = offset * per + member
            span = slice(at * CAP, (at + 1) * CAP)
            out_rows[span, :] = pieces[at][0]
            back_rows[span, :] = pieces[at][1]
            column0 = jnp.where(first == expert, column, -1.0)
            column1 = jnp.where(second == expert, column, -1.0)
            pick0[:, span] = jnp.where(column0 == slot_lane, 1.0, 0.0).astype(BF16)
            pick1[:, span] = jnp.where(column1 == slot_lane, 1.0, 0.0).astype(BF16)
    out0, out1 = mm(pick0[...], out_rows[...]), mm(pick1[...], out_rows[...])
    back = mm(pick0[...] + pick1[...], back_rows[...])
    get = lambda at: info[:, at : at + 1]
    gate0, gate1, hidden_part, both = get(12), get(13), get(14), get(21)
    layer_out[...] = base[...] + gate0 * out0 + gate1 * out1
    grad = cot[...].astype(F32)
    res = res_ref[...]
    scale = lax.rsqrt(jnp.mean(res * res, axis=-1, keepdims=True) + NORM_EPS)
    unit = res * scale
    total = lambda values: jnp.sum(values, axis=1, keepdims=True)
    dot_hidden = total(grad * (unit * gain[...]))
    dot_vector = [total(grad * vectors[k : k + 1, :]) for k in range(2)]

    def gate_grad(route, out):
        value = total(grad * out) + jnp.where(route == EXPERTS + 1, dot_hidden, 0.0)
        for k in range(2):
            const = get(17 + 2 * k) * dot_hidden + get(18 + 2 * k) * dot_vector[k]
            value = value + jnp.where(route == EXPERTS + 2 + k, const, 0.0)
        return value

    dgate0, dgate1 = gate_grad(first, out0), gate_grad(second, out1)
    mean = gate0 * dgate0 + gate1 * dgate1
    dchance = (
        jnp.where(lane == first, dgate0 - mean, 0.0) + jnp.where(lane == second, dgate1 - mean, 0.0)
    ) / both
    chances = jnp.where(lane < IDS, info, 0.0)
    logits_grad = chances * (dchance - total(chances * dchance))
    extra = {16: get(15), 17: get(16)}
    for k in range(2):
        alpha0, alpha1, gate = get(17 + 2 * k), get(18 + 2 * k), get(22 + k)
        d0, d1 = gate * dot_hidden, gate * dot_vector[k]
        inner = alpha0 * d0 + alpha1 * d1
        extra[IDS + 2 * k] = alpha0 * (d0 - inner)
        extra[IDS + 2 * k + 1] = alpha1 * (d1 - inner)
    packed = logits_grad + columns(extra)
    high, low = split(packed)
    prev_out[...] = mm(high, resid_t[...]) + mm(low, resid_t[...])
    hidden_total = (
        back + hidden_part * grad + mm(high, mixers_t[...]) + mm(low, mixers_t[...])
    )
    turned = jnp.transpose(packed)[:32, :]
    t_high, t_low = split(turned)
    hidden_low = blk[:TOK_DEV, :]
    by_hidden = mm(t_high, hidden_low) + mm(t_low, hidden_low)
    by_grad = mm(t_high, cot[...]) + mm(t_low, cot[...])
    prev_high, prev_low = split(prev[...])
    by_prev = mm(t_high, prev_high) + mm(t_high, prev_low) + mm(t_low, prev_high)
    gain_grad = jnp.sum(hidden_total * unit, axis=0, keepdims=True)
    sub = lax.broadcasted_iota(jnp.int32, (8, 1), 0)
    small_out[:16, :] = by_hidden[:16, :]
    small_out[16:24, :] = jnp.where(sub == 2, gain_grad, by_grad[16:24, :])
    small_out[24:40, :] = jnp.zeros((16, D), F32)
    small_out[24:40, :LANES] = by_prev[:16, :]
    u = gain[...] * hidden_total
    inner = jnp.mean(res * u, axis=1, keepdims=True)
    residual_grad = grad + scale * u - res * (scale * scale * scale * inner)
    grad_out[...] = residual_grad
    mix = residual_grad.astype(BF16)
    mix_out[...] = mix
    mixed_out[...] = mm_nt(mix, w_out[...]).astype(BF16)


def finish_kernel(prompt_terms, scal, dq, own, received, *rest):
    terms = rest[:prompt_terms]
    weights, tok, gain, res_grad = rest[prompt_terms : prompt_terms + 4]
    low_out, grad_out, small_out = rest[prompt_terms + 4 :]
    low_out[:, :D] = dq[...]
    for half in range(2):
        columns_at = slice((half + 1) * D, (half + 2) * D)
        prompt = terms[0][half].astype(F32)
        for term in terms[1:]:
            prompt = prompt + term[half].astype(F32)
        low_out[:P_DEV, columns_at] = prompt.astype(BF16)
        low_out[P_DEV:, columns_at] = (own[half] + received[half].astype(F32)).astype(BF16)
    normed_grad = mm_nt(low_out[...], weights[...])
    x = tok[...].astype(F32)
    scale = lax.rsqrt(jnp.mean(x * x, axis=-1, keepdims=True) + NORM_EPS)
    u = gain[...] * normed_grad
    inner = jnp.mean(x * u, axis=1, keepdims=True)
    grad_out[...] = res_grad[...] + scale * u - x * (scale * scale * scale * inner)
    row = jnp.sum(normed_grad * (x * scale), axis=0, keepdims=True)
    sub = lax.broadcasted_iota(jnp.int32, (8, 1), 0)
    small_out[...] = jnp.where(sub == 0, row, 0.0)


def sum_everywhere(value):
    for axis in ("rep", "grp"):
        count = lax.axis_size(axis)
        bit = 1
        while bit < count:
            pairs = [(source, source ^ bit) for source in range(count)]
            value = value + lax.ppermute(value, axis, pairs)
            bit *= 2
    return value


def sum_replicas(value):
    count = lax.axis_size("rep")
    index = lax.axis_index("rep")
    bits = [1 << n for n in range(count.bit_length() - 1)]
    for bit in bits:
        half = value.shape[1] // 2
        left, right = value[:, :half], value[:, half:]
        upper = (index & bit) != 0
        keep = jnp.where(upper, right, left)
        give = jnp.where(upper, left, right).astype(BF16)
        pairs = [(source, source ^ bit) for source in range(count)]
        value = keep + lax.ppermute(give, "rep", pairs).astype(F32)
    value = value.astype(BF16)
    for bit in reversed(bits):
        pairs = [(source, source ^ bit) for source in range(count)]
        other = lax.ppermute(value, "rep", pairs)
        upper = (index & bit) != 0
        value = jnp.concatenate(
            [jnp.where(upper, other, value), jnp.where(upper, value, other)], axis=1
        )
    return value.astype(F32)


def body(
    tokens,
    prev_logits,
    routes,
    branch_points,
    cotangent,
    attn_gain,
    qkv_weight,
    out_weight,
    ffn_gain,
    router_weight,
    resid_weight,
    const_weight,
    const_vector,
    gate_weight,
    up_weight,
    down_weight,
):
    group, count = lax.axis_size("grp"), lax.axis_size("rep")
    index, replica = lax.axis_index("grp"), lax.axis_index("rep")
    per, share = max(1, EXPERTS // group), max(1, group // EXPERTS)
    prompt = P_DEV * group
    spread = group * count <= 32
    tok, cot, route_rows, prev = tokens[0], cotangent[0], routes[0], prev_logits[0]
    follow = lax.dynamic_index_in_dim(branch_points[0], index // 2, keepdims=True)
    scal = jnp.concatenate(
        [
            index ^ jnp.arange(group, dtype=jnp.int32),
            follow.astype(jnp.int32),
            (index % 2)[None].astype(jnp.int32),
        ]
    )

    shards = gather_group(qkv_weight, 1)
    weights = (gate_weight, up_weight, down_weight)
    mine = replica.astype(jnp.int32)[None]
    early = []
    if spread:
        early = [pack_weights(mine, weights, 0, per, count, ())]
    (
        prompt_rows,
        grad_block,
        slots,
        route_lanes,
        prev_lanes,
        previous,
        mixers,
        mixers_t,
        resid_t,
        vectors,
    ) = prepare(
        route_rows,
        prev,
        cot,
        router_weight,
        resid_weight,
        const_weight,
        const_vector,
        tok,
        early,
    )
    prompts = gather_group(prompt_rows, 2)
    for offset in range(0, group, 2):
        prompts[offset + 1] = xor_permute(prompts[offset] if offset else tok, 1)
    gain_one = attn_gain.astype(F32)[None]
    gain_two = ffn_gain.astype(F32)[None]

    offsets = [o for o in range(0, group, 2)] + [o for o in range(1, group, 2)]

    def group_blocks(block):
        held = gather_group(block, 2)
        own = [held[o] for o in range(0, group, 2)]
        return own + [xor_permute(piece, 1) for piece in own]

    def all_blocks(block):
        result, forth, back = [[block]], block, block
        for step in range(1, count // 2 + 1):
            forth = ring_permute(forth, 1)
            result.append([forth])
            if step < count - step:
                back = ring_permute(back, -1)
                result[-1].append(back)
        return result

    grad_far = all_blocks(grad_block) if spread else [[grad_block]]
    hops = len(grad_far) - 1

    def hop_of(blocks, at):
        return blocks[at] if 0 < at <= hops else []

    q, kp, vp, kc, vc, w_qkv, normed, later_block, later_shard, *early = whole_call(
        partial(projection_kernel, group),
        "projections",
        scal,
        [gain_one, tok]
        + [prompts[o] for o in range(1, group)]
        + [shards[o] for o in range(group)]
        + [grad_block, out_weight, *early],
        [
            shape_of((TOK_DEV, D), BF16),
            shape_of((prompt, D), BF16),
            shape_of((prompt, D), BF16),
            shape_of((2 * P_DEV, D), BF16),
            shape_of((2 * P_DEV, D), BF16),
            shape_of((D, 3 * D), BF16),
            shape_of((TOK_DEV, D), BF16),
            shape_of((BLOCK, D), BF16),
            shape_of((D // group, D), BF16),
            *[shape_of(v.shape, BF16) for v in early],
        ],
        2 * TOK_DEV * D * D + 4 * (prompt + 2 * P_DEV) * D * D,
    )
    out_shards = gather_group(later_shard, 1)
    grad_near = group_blocks(later_block)
    packed = [gather_group(v, 1) for v in early]
    o32, lse = attention(scal, q, kp, vp, kc, vc, group, hop_of(grad_far, 1) if W_FRONT else [])
    w_out, res, base, block, info, mixed_low = whole_call(
        partial(routing_kernel, group),
        "routing",
        scal,
        [tok, o32]
        + [out_shards[o] for o in range(group)]
        + [gain_two, mixers, vectors, previous, route_lanes],
        [
            shape_of((D, D), BF16),
            shape_of((TOK_DEV, D), F32),
            shape_of((TOK_DEV, D), F32),
            shape_of((BLOCK, D), BF16),
            shape_of((TOK_DEV, LANES), F32),
            shape_of((TOK_DEV, D), BF16),
        ],
        2 * TOK_DEV * D * D,
        waits=[*(hop_of(grad_far, 2) if W_FRONT else []), *(grad_near[1:-1] if W_NEAR else [])],
    )

    near = group_blocks(block)
    rings, returned, locals_out = [], {}, []

    def give_back(member):
        for offset in range(group):
            value = locals_out[member][offset]
            returned[offset, member] = xor_permute(value, offset) if offset else value
        return [returned[offset, member] for offset in range(1, group)]

    if not spread:
        local = near_rows(scal, near, grad_near, group, per, share, ())
        locals_out = [
            local_expert(*local, *weights, member, offsets, group, per, ())
            for member in range(per)
        ]
    else:
        forth = back = block
        stacks, done, kept = (), 0, []
        for hop in range(1, hops + 1):
            forth = ring_permute(forth, 1)
            back = ring_permute(back, -1) if hop < count - hop else None
            take, waits = [(block, grad_block)], hop_of(grad_far, 3)
            if hop == 2:
                take, waits = kept, hop_of(grad_far, 4)
            elif hop > 2:
                take, waits = kept if hop == hops else (), locals_out[-1][:1] if locals_out else ()
            kept = [] if hop == 1 or take is kept else kept
            if take:
                stacks = column_rows(
                    [h for h, g in take], [g for h, g in take], done, count, stacks, waits
                )
                done += len(take)
            if hop == 2:
                for member in range(1, per):
                    later = pack_weights(mine, weights, member, per, count, [near[1], *([h for h, g in take] if W_PACK else [])])
                    packed.append(gather_group(later, 1))
            if hop == 3:
                waits = [packed[-1][0], *packed[0].values(), stacks[0]]
                local = near_rows(scal, near, grad_near, group, per, share, waits[:-1])
                locals_out.append(
                    local_expert(*local, *weights, 0, offsets, group, per, ())
                )
            kept = kept + list(zip([v for v in (forth, back) if v is not None], grad_far[hop]))
        stacks = column_rows(
            [h for h, g in kept], [g for h, g in kept], done, count, stacks, ()
        )
        parts = [{} for _ in range(per)]
        last = [v for p in packed for v in p.values()]
        for low in range(group - 2, -1, -2):
            chosen = [(m, o) for m in range(per) for o in (low + 1, low)]
            experts = jnp.stack([(index ^ o) * per + m for m, o in chosen]).astype(jnp.int32)
            outs = weight_slices(experts, stacks, [packed[m][o] for m, o in chosen], last)
            for m in range(per):
                parts[m][low] = add_low(outs[2 * m + 1], xor_permute(outs[2 * m], 1))
            last = [outs[0]]
            if low:
                last += [parts[0][low]]
                last += give_back(0) if W_SLICE else []
        for member, part in enumerate(parts):
            bit = 2
            while bit < group:
                for offset in sorted(part, reverse=True):
                    if offset & bit:
                        value = part.pop(offset)
                        if rings:
                            value, rings[-1][0] = lax.optimization_barrier((value, rings[-1][0]))
                        value = xor_permute(value, bit)
                        if rings:
                            waits = [last[0], rings[0][0]] if W_LOCAL else []
                            outs = local_expert(
                                *local, *weights, member, offsets, group, per, waits
                            )
                            if W_LOCAL:
                                value, *outs = lax.optimization_barrier((value, *outs))
                            locals_out.append(outs)
                            give_back(member)
                        part[offset ^ bit] = add_low(part[offset ^ bit], value)
                bit *= 2
            rings.append([part[0]])
    for member in range(per):
        if (0, member) not in returned:
            give_back(member)
    placed = ()
    units = gate_weight.shape[1]
    spot = jnp.where(replica % 2 == 0, replica // 2, count - 1 - replica // 2)

    def advance(step):
        nonlocal placed
        for member, ring in enumerate(rings):
            toward = 1 - 2 * (member % 2)
            if step < count:
                ring.append(ring_permute(ring[-1], toward))
            source = (spot - toward * (step - 1)) % count
            source = jnp.where(source < count // 2, 2 * source, 2 * (count - 1 - source) + 1)
            at = source.astype(jnp.int32)[None] + member * count
            placed = place_slice(at, ring[step - 1], placed, units)
            if step < count and W_BACK:
                ring[step], *placed = lax.optimization_barrier((ring[step], *placed))

    def advance_to(*steps):
        for step in steps:
            if spread:
                advance(step)

    def arrived(*steps):
        return [ring[step] for ring, step in zip(rings, steps) if step >= 0]

    advance_to(1, 2, 3)
    layer_out, res_grad, mix_grad, mixed_grad, prev_grad, small = whole_call(
        partial(combine_kernel, group, per, share),
        "combine",
        scal,
        [returned[o, m] for o in range(group) for m in range(per)]
        + [
            base,
            cot,
            block,
            info,
            slots,
            route_lanes,
            res,
            gain_two,
            vectors,
            mixers_t,
            resid_t,
            prev_lanes,
            w_out,
        ],
        [
            shape_of((TOK_DEV, D), F32),
            shape_of((TOK_DEV, D), F32),
            shape_of((TOK_DEV, D), BF16),
            shape_of((TOK_DEV, D), BF16),
            shape_of((TOK_DEV, LANES), F32),
            shape_of((SMALL_ROWS, D), F32),
        ],
        6 * TOK_DEV * group * per * CAP * D + 2 * TOK_DEV * D * D,
        scratch=[
            pltpu.VMEM((group * per * CAP, D), BF16),
            pltpu.VMEM((group * per * CAP, D), BF16),
            pltpu.VMEM((TOK_DEV, group * per * CAP), BF16),
            pltpu.VMEM((TOK_DEV, group * per * CAP), BF16),
        ],
        waits=arrived(1, 0) if W_RING else (),
    )

    back = attention_back(
        scal, q, kp, vp, kc, vc, mixed_grad, o32, lse, group, arrived(2, 1) if W_RING else []
    )
    dq, pieces, later_own, later_other = back[0], list(back[1 : 1 + group]), back[-2], back[-1]
    if W_KEYS and spread:
        tied = lax.optimization_barrier((later_other, *pieces[1:], rings[0][3], rings[1][2]))
        later_other, rings[0][3], rings[1][2] = tied[0], tied[-2], tied[-1]
        pieces = [pieces[0], *tied[1:-2]]
    advance_to(4, 5)
    later_in = xor_permute(later_other, 1)
    held = {o: [pieces[o]] for o in range(group)}
    bit = 1
    while bit < group:
        for offset in sorted(held):
            if offset & bit:
                terms = held.pop(offset)
                value = terms[0]
                if len(terms) > 1:
                    value = sum(t.astype(F32) for t in terms).astype(BF16)
                held[offset ^ bit].append(xor_permute(value, bit))
        bit *= 2
    terms = held[0]
    qkv_low, input_grad, small_two = whole_call(
        partial(finish_kernel, len(terms)),
        "finish",
        scal,
        [dq, later_own, later_in] + terms + [w_qkv, tok, gain_one, res_grad],
        [
            shape_of((TOK_DEV, 3 * D), BF16),
            shape_of((TOK_DEV, D), F32),
            shape_of((8, D), F32),
        ],
        6 * TOK_DEV * D * D,
        waits=(arrived(4, 3) if W_KEYS else arrived(3, 2)) if W_RING else (),
    )
    full = jnp.concatenate([mm_tn(normed, qkv_low), mm_tn(mixed_low, mix_grad)], axis=1)
    rows = D // group
    held = {
        o: lax.dynamic_slice_in_dim(full, (index ^ o) * rows, rows, axis=0) for o in range(group)
    }
    bit, at = 1, 5
    while bit < group:
        for offset in sorted(held):
            if offset & bit:
                value = xor_permute(held.pop(offset).astype(BF16), bit)
                if W_DENSE and spread and offset == bit:
                    value, rings[0][at], rings[1][at - 1] = lax.optimization_barrier(
                        (value, rings[0][at], rings[1][at - 1])
                    )
                    at += 1
                    advance_to(at)
                held[offset ^ bit] = held[offset ^ bit] + value.astype(F32)
        bit *= 2
    if SC_DENSE:
        dense = lax.psum(held[0].astype(BF16), "rep").astype(F32)
    else:
        dense = sum_replicas(held[0])
    small = jnp.concatenate([small, small_two], axis=0)
    if W_DENSE and spread:
        advance_to(*range(len(rings[0]), count))
        small, rings[0][6], rings[1][6] = lax.optimization_barrier(
            (small, rings[0][6], rings[1][6])
        )
    small = lax.psum(small, ("rep", "grp")) if SC_SMALL else sum_everywhere(small)

    if spread:
        for step in range(len(rings[0]), count + 1):
            advance(step)
        gate_sum, up_sum, down_sum = placed
    else:
        x, s = local[0][0], local[1][0]
        hidden, grad_a, grad_b = expert_terms(
            mm(x, gate_weight), mm(x, up_weight), mm_nt(s, down_weight)
        )
        sums = (mm_tn(x, grad_a), mm_tn(x, grad_b), mm_tn(hidden, s))
        gate_sum, up_sum, down_sum = [
            lax.psum(part.astype(BF16), "rep").astype(F32) for part in sums
        ]

    gains = jnp.stack([small[SMALL_ROWS], small[18]], axis=0)
    router_grad = jnp.transpose(small[:IDS])
    const_grad = jnp.transpose(small[IDS : IDS + 4].reshape(2, 2, D), (0, 2, 1))
    resid_grad = jnp.transpose(small[24 : 24 + IDS, :IDS])
    return (
        layer_out[None],
        input_grad[None],
        prev_grad[:, :IDS][None],
        gains,
        dense[:, : 3 * D],
        dense[:, 3 * D :],
        router_grad,
        resid_grad,
        const_grad,
        small[16:18],
        gate_sum,
        up_sum,
        down_sum,
    )


def solution(mesh):
    in_specs = (
        P("rep", "grp", None),
        P("rep", "grp", None),
        P("rep", "grp", None),
        P("rep", None),
        P("rep", "grp", None),
        P(),
        P("grp", None),
        P("grp", None),
        P(),
        P(),
        P(),
        P(),
        P(),
        P(None, "grp"),
        P(None, "grp"),
        P("grp", None),
    )
    out_specs = (
        P("rep", "grp", None),
        P("rep", "grp", None),
        P("rep", "grp", None),
        P(),
        P("grp", None),
        P("grp", None),
        P(),
        P(),
        P(),
        P(),
        P(None, "grp"),
        P(None, "grp"),
        P("grp", None),
    )
    return jax.shard_map(body, mesh=mesh, in_specs=in_specs, out_specs=out_specs, check_vma=False)
```
